128 devices in a mesh: tile: 16 (over y, z), layer: 8 (over x, core).
Axes of the slice: x: 4, y: 4, z: 4, core: 2. Of those that a mesh axis runs over, the one named last changes fastest.
Arguments:
- newton_rhs: float32 [3, 24, 256, 2048], P(None, 'layer', 'tile'), may hold values from -6 to 6
- weights: float32 [3, 24, 256, 2048], P(None, 'layer', 'tile'), may hold values from 0.2 to 1
- block_diag: float32 [3, 3, 24, 256, 2048], P(None, None, 'layer', 'tile'), as said below
- block_inv: float32 [3, 3, 24, 256, 2048], P(None, None, 'layer', 'tile'), as said below
- trans_x: float32 [24, 256, 2048], P('layer', 'tile'), may hold values from 0.2 to 1
- trans_y: float32 [24, 256, 2048], P('layer', 'tile'), may hold values from 0.2 to 1
- trans_z: float32 [24, 256, 2048], P('layer', 'tile'), may hold values from 0.2 to 1
- storage: float32 [24, 256, 2048], P('layer', 'tile'), may hold values from 0.05 to 0.5
- perf_cell: int32 [32768], P(('tile', 'layer')), may hold values from 0 to 98303
- perf_front: int32 [32768], P(('tile', 'layer')), may hold values from 0 to 8191
- productivity: float32 [32768], P(('tile', 'layer')), may hold values from 0.5 to 2
- front_inverse: float32 [8192, 8192], P(('tile', 'layer')), may hold values from -0.0625 to 0.0625
Outputs:
- update: float32 [3, 24, 256, 2048], P(None, 'layer', 'tile')
- lin_res: float32 [3, 24, 256, 2048], P(None, 'layer', 'tile')
- ratio: float32 [], replicated
The draws below stay inside these ranges and needn't reach their ends.
Inputs may be any that keep to these rules, and one draw needn't show every extreme that they name: perf_cell indexes the [3, 16, 2048] block of the device that holds the perforation; cells may hold several perforations. `perf_front`: front unknowns may receive several perforations from many devices. Diagonal entries of block_diag lie between 6 and 9. Diagonal entries of block_inv lie between 0.1 and 0.2.
All inputs are finite; a program needn't handle non-finite values.
Results may differ from the reference program's by a relative error of at most 0.000098.
Values sent between devices are 32-bit elements; how exact they have to be, the bound alone decides.
A program may use at most 128 MiB of HBM per device.

```python
import math
import jax
import jax.numpy as jnp
from jax import lax

LZ = 3
CX = 16
NY = 2048
NF = 8192
PERF_DEV = 256
NZ = 24
NX = 256
NPERF = 32768
N_LAYER = 8


def draw_block_diag(key, part):
    first, second = jax.random.split(jax.random.fold_in(key, 11))
    shape = (3, 3, NZ, NX, NY)
    eye = jnp.eye(3, dtype=jnp.float32)[:, :, None, None, None]
    off = 0.5 * jax.random.normal(first, shape, jnp.float32)
    diag = 6.0 + 3.0 * jax.random.uniform(second, shape, jnp.float32)
    return eye * diag + (1.0 - eye) * off


def draw_block_inv(key, part):
    first, second = jax.random.split(jax.random.fold_in(key, 23))
    shape = (3, 3, NZ, NX, NY)
    eye = jnp.eye(3, dtype=jnp.float32)[:, :, None, None, None]
    off = 0.02 * jax.random.normal(first, shape, jnp.float32)
    diag = 0.1 + 0.1 * jax.random.uniform(second, shape, jnp.float32)
    return eye * diag + (1.0 - eye) * off


def touch_ends(values, key, smallest, top_value):
    longest = values.shape.index(max(values.shape))
    spots = []
    for shift in (0, 1):
        where = [jax.random.randint(jax.random.fold_in(key, axis), (), 0, length) for axis, length in enumerate(values.shape)]
        where[longest] = (where[longest] + shift) % values.shape[longest]
        spots.append(tuple(where))
    return values.at[spots[0]].set(smallest).at[spots[1]].set(top_value)


def block_scale(own_key, extent, shards, least, top_value):
    def one(position, blocks):
        steps = jax.random.uniform(jax.random.fold_in(jax.random.fold_in(own_key, 6), position), (blocks,), jnp.float32, least / len(shards), top_value / len(shards))
        return jnp.repeat(jnp.exp(steps), extent[position] // blocks).reshape((-1,) + (1,) * (len(extent) - position - 1))

    level = one(*shards[0])
    for cut in shards[1:]:
        level = level * one(*cut)
    return level


def noise(stream_key, extent, scale, most, pieces=(), held_as=jnp.bfloat16):
    drawn = scale * jax.random.normal(stream_key, extent, jnp.float32)
    if pieces:
        drawn = drawn * block_scale(stream_key, extent, pieces, -0.22, 0.18)
    return jnp.clip(drawn, -most, most).astype(held_as)


def setup_inputs(seed: int = 0) -> dict:
    splits = jax.random.split(jax.random.key(seed), 13)
    newton_rhs = noise(splits[0], (3, NZ, NX, NY), 1.0, 6.0, ((1, 8), (2, 16)), jnp.float32)
    weights = jnp.clip(0.2 + 0.8 * jax.random.uniform(splits[1], (3, NZ, NX, NY), jnp.float32) ** block_scale(splits[1], (3, NZ, NX, NY), ((1, 8), (2, 16)), -0.2, 0.2), 0.2, 1.0)
    block_diag = draw_block_diag(jax.random.fold_in(splits[12], 71), 0)
    block_inv = draw_block_inv(jax.random.fold_in(splits[12], 71), 0)
    trans_x = jnp.clip(jnp.exp(math.log(1.0) - 1.609438 * jax.random.uniform(splits[4], (NZ, NX, NY), jnp.float32) ** block_scale(splits[4], (NZ, NX, NY), ((0, 8), (1, 16)), -0.2, 0.2)), 0.2, 1.0)
    trans_y = jnp.clip(jnp.exp(math.log(1.0) - 1.609438 * jax.random.uniform(splits[5], (NZ, NX, NY), jnp.float32) ** block_scale(splits[5], (NZ, NX, NY), ((0, 8), (1, 16)), -0.2, 0.2)), 0.2, 1.0)
    trans_z = jnp.clip(jnp.exp(math.log(1.0) - 1.609438 * jax.random.uniform(splits[6], (NZ, NX, NY), jnp.float32) ** block_scale(splits[6], (NZ, NX, NY), ((0, 8), (1, 16)), -0.2, 0.2)), 0.2, 1.0)
    storage = jnp.clip(jnp.exp(math.log(0.5) - 2.3025851 * jax.random.uniform(splits[7], (NZ, NX, NY), jnp.float32) ** block_scale(splits[7], (NZ, NX, NY), ((0, 8), (1, 16)), -0.2, 0.2)), 0.05, 0.5)
    perf_cell = touch_ends(jax.random.randint(splits[8], (NPERF,), 0, LZ * CX * NY), jax.random.fold_in(splits[8], 1), 0, (LZ * CX * NY) - 1).astype(jnp.int32)
    perf_front = touch_ends(jax.random.randint(splits[9], (NPERF,), 0, NF), jax.random.fold_in(splits[9], 1), 0, NF - 1).astype(jnp.int32)
    productivity = jnp.clip(jnp.exp(math.log(2.0) - 1.3862944 * jax.random.uniform(splits[10], (NPERF,), jnp.float32) ** block_scale(splits[10], (NPERF,), ((0, 128),), -0.2, 0.2)), 0.5, 2.0)
    front_inverse = noise(splits[11], (NF, NF), NF ** -0.5, 0.0625, ((0, 128),), jnp.float32)
    return {"newton_rhs": newton_rhs, "weights": weights, "block_diag": block_diag, "block_inv": block_inv, "trans_x": trans_x, "trans_y": trans_y, "trans_z": trans_z, "storage": storage, "perf_cell": perf_cell, "perf_front": perf_front, "productivity": productivity, "front_inverse": front_inverse}


def couple(field, trans_x, trans_y, trans_z):
    lead = field.ndim - 3
    pads = [(0, 0)] * lead + [(1, 1), (1, 1), (1, 1)]
    padded = jnp.pad(field, pads)
    tpad = [(1, 1), (1, 1), (1, 1)]
    txp = jnp.pad(trans_x, tpad)
    typ = jnp.pad(trans_y, tpad)
    tzp = jnp.pad(trans_z, tpad)
    total = trans_x * padded[..., 1:-1, 2:, 1:-1] + txp[1:-1, :-2, 1:-1] * padded[..., 1:-1, :-2, 1:-1]
    total = total + trans_y * padded[..., 1:-1, 1:-1, 2:] + typ[1:-1, 1:-1, :-2] * padded[..., 1:-1, 1:-1, :-2]
    total = total + trans_z * padded[..., 2:, 1:-1, 1:-1] + tzp[:-2, 1:-1, 1:-1] * padded[..., :-2, 1:-1, 1:-1]
    return total

def block_apply(matrix, vector):
    return matrix[:, 0] * vector[0][None] + matrix[:, 1] * vector[1][None] + matrix[:, 2] * vector[2][None]

def jacobian(field, block_diag, trans_x, trans_y, trans_z):
    return block_apply(block_diag, field) - couple(field, trans_x, trans_y, trans_z)

def line_solve(rhs, upper_raw, store):
    depth = rhs.shape[0]
    live = (lax.iota(jnp.int32, depth) < depth - 1).astype(jnp.float32)[:, None, None]
    upper = upper_raw * live
    lower = jnp.concatenate([jnp.zeros_like(upper[:1]), upper[:-1]], 0)
    diag = lower + upper + store

    def forward(carry, item):
        gprev, dprev = carry
        low, up, dia, rh = item
        pivot = dia - low * gprev
        gnow = up / pivot
        dnow = (rh + low * dprev) / pivot
        return ((gnow, dnow), (gnow, dnow))
    zero = jnp.zeros_like(rhs[0])
    _, (gall, dall) = lax.scan(forward, (zero, zero), (lower, upper, diag, rhs))

    def backward(carry, item):
        gnow, dnow = item
        value = dnow + gnow * carry
        return (value, value)
    _, sol = lax.scan(backward, zero, (gall, dall), reverse=True)
    return sol

def reference(newton_rhs, weights, block_diag, block_inv, trans_x, trans_y, trans_z, storage, perf_cell, perf_front, productivity, front_inverse):
    pres_rhs = lax.optimization_barrier(jnp.sum(weights * newton_rhs, axis=0))
    slot = lax.iota(jnp.int32, NPERF)
    device = slot // PERF_DEV
    tile_idx = device // N_LAYER
    layer_idx = device % N_LAYER
    local_z = perf_cell // (CX * NY)
    local_x = perf_cell // NY % CX
    local_y = perf_cell % NY
    glob = ((layer_idx * LZ + local_z) * NX + tile_idx * CX + local_x) * NY + local_y
    glob = glob.astype(jnp.int32)
    flat = pres_rhs.reshape(-1)
    front_rhs = jnp.zeros((NF,), jnp.float32).at[perf_front].add(productivity * flat[glob])
    front_sol = jnp.dot(front_inverse, front_rhs, precision=lax.Precision.HIGHEST)
    adjusted = flat.at[glob].add(-productivity * front_sol[perf_front]).reshape(pres_rhs.shape)
    pressure = line_solve(adjusted, trans_z, storage)
    zeros_two = jnp.zeros((2,) + pressure.shape, jnp.float32)
    pe0 = jnp.concatenate([pressure[None], zeros_two], 0)
    remain = newton_rhs - jacobian(pe0, block_diag, trans_x, trans_y, trans_z)
    search = pe0 + block_apply(block_inv, remain)
    image = jacobian(search, block_diag, trans_x, trans_y, trans_z)
    along = jnp.sum(image * newton_rhs)
    power = jnp.sum(image * image)
    start_sq = jnp.sum(newton_rhs * newton_rhs)
    omega = along / power
    update = omega * search
    lin_res = newton_rhs - omega * image
    ratio = jnp.sqrt(jnp.sum(lin_res * lin_res) / start_sq)
    return (update, lin_res, ratio)
```

```python
import functools

import jax
import jax.numpy as jnp
from jax import lax
from jax.experimental import pallas as pl
from jax.experimental.pallas import tpu as pltpu
from jax.sharding import PartitionSpec as P

MESH = pl.DeviceIdType.MESH
F32 = jnp.float32
BF16 = jnp.bfloat16
I32 = jnp.int32


def bits(n):
    assert n & (n - 1) == 0
    return n.bit_length() - 1


def quot(a, n):
    return lax.shift_right_logical(a, jnp.full_like(a, bits(n)))


def rest(a, n):
    return a & (n - 1)


def split3(x):
    hi = x.astype(BF16)
    left = x - hi.astype(F32)
    mid = left.astype(BF16)
    low = (left - mid.astype(F32)).astype(BF16)
    return jnp.concatenate([hi, mid, low], axis=1)


def pick_dot(onehot, pieces):
    out = lax.dot_general(onehot, pieces, (((1,), (0,)), ((), ())), preferred_element_type=F32)
    n = out.shape[1] // 3
    return out[:, :n] + out[:, n : 2 * n] + out[:, 2 * n :]


def tiles(block):
    rows, cols = block.shape
    return [
        block[i : i + 8, j : j + 128] for i in range(0, rows, 8) for j in range(0, cols, 128)
    ]


def untile(mat, rows, cols):
    per = cols // 128
    out = []
    for i in range(rows // 8):
        out.append(
            jnp.concatenate(
                [mat[(i * per + j) * 8 : (i * per + j + 1) * 8, :] for j in range(per)], axis=1
            )
        )
    return jnp.concatenate(out, axis=0)


def fold(block):
    parts = tiles(block)
    while len(parts) > 1:
        parts = [a + b for a, b in zip(parts[::2], parts[1::2])]
    return parts[0]


def total(x):
    return jnp.sum(jnp.sum(x, axis=1, keepdims=True), axis=0, keepdims=True)


def onehot(mask):
    return jnp.where(mask, 1.0, 0.0).astype(BF16)


def kernel(
    T, L, LZ, CX, NY, NF,
    rhs_h, wts_h, bd_h, bi_h, tx_h, ty_h, tz_h, st_h, cell_h, front_h, prod_h, finv_h,
    search_o, image_o, stat_o,
    rhs, wts, bd, bi, tx, ty, tz, st, cell, front, prod, finv,
    perf_own, perf_buf, pres, fpart, f1, f2, f3, g1, g2,
    rown, rto, rtg, rgs, csol, ccell, q3,
    prest, tzt, stt, inv, mul, gam, pcol, corr,
    tzp, txs, txp, press, hsend, phalo, adj,
    search, image, xsend, xhalo, zsend, zhalo, s1, s2,
    ld, f1s, f1r, f2s, f2r, f3s, f3r, g1s, g1r, g2s, g2r, pfs, pfr, bts, btr, bto,
    tzs, tzr, txps, txpr, rts, rtr, rto_sem, hls, hlr, xhs, xhr, zhs, zhr,
    s1s, s1r, s2s, s2r, outs,
):
    NYL, NFR = NY // L, NF // 128
    NBL, RS, RPD = NYL // 128, NFR // T, NF // (T * L)
    HALF = 128 // RPD
    RL = CX * NYL // 128
    RO = LZ * CX * NY // 128
    NB = NY // 128
    t, l = lax.axis_index("tile"), lax.axis_index("layer")

    loads = {}
    order = [
        ("cell", cell_h, cell), ("front", front_h, front), ("prod", prod_h, prod),
        ("rhs", rhs_h, rhs), ("wts", wts_h, wts), ("finv", finv_h, finv), ("tx", tx_h, tx),
        ("tz", tz_h, tz), ("st", st_h, st), ("ty", ty_h, ty), ("bi", bi_h, bi), ("bd", bd_h, bd),
    ]
    for i, (name, src, dst) in enumerate(order):
        loads[name] = pltpu.make_async_copy(src, dst, ld.at[i])
        loads[name].start()

    tn, tb = lax.rem(t + 1, T), lax.rem(t + T - 1, T)
    ln, lb = lax.rem(l + 1, L), lax.rem(l + L - 1, L)
    barrier = pltpu.get_barrier_semaphore()
    peers = [(t, lax.rem(l + i, L)) for i in range(1, L)]
    peers += [(lax.rem(t + i, T), l) for i in range(1, T)]
    peers += [(a, lax.rem(l + i, L)) for a in (tn, tb) for i in range(1, L)]
    for peer in peers:
        pl.semaphore_signal(barrier, inc=1, device_id=peer, device_id_type=MESH)

    started = []

    def send(src, dst, ssem, rsem, to):
        copy = pltpu.make_async_remote_copy(
            src_ref=src, dst_ref=dst, send_sem=ssem, recv_sem=rsem,
            device_id=to, device_id_type=MESH,
        )
        copy.start()
        started.append(copy)

    def arrived(dst, ssem, rsem):
        pltpu.make_async_remote_copy(
            src_ref=dst, dst_ref=dst, send_sem=ssem, recv_sem=rsem,
            device_id=(t, l), device_id_type=MESH,
        ).wait_recv()

    def to_tiles(src, dst, ss, rs):
        for i in range(1, T):
            peer = lax.rem(t + i, T)
            send(src(peer), dst.at[t], ss.at[i - 1], rs.at[i - 1], (peer, l))

    def from_tiles(dst, ss, rs):
        for i in range(1, T):
            arrived(dst.at[lax.rem(t + T - i, T)], ss.at[i - 1], rs.at[i - 1])

    def to_layers(src, dst, ss, rs):
        for i in range(1, L):
            peer = lax.rem(l + i, L)
            send(src(peer), dst, ss.at[i - 1], rs.at[i - 1], (t, peer))

    def from_layers(dst, ss, rs):
        for i in range(1, L):
            arrived(dst(lax.rem(l + L - i, L)), ss.at[i - 1], rs.at[i - 1])

    def add_up(buf, n):
        parts = [buf[i] for i in range(n)]
        while len(parts) > 1:
            parts = [a + b for a, b in zip(parts[::2], parts[1::2])]
        return parts[0]

    def cols_block(ref, i):
        return ref.at[:, :, pl.ds(pl.multiple_of(i * NYL, NYL), NYL)]

    def lane_iota(rows, cols):
        return lax.broadcasted_iota(I32, (rows, cols), 1)

    def row_iota(rows, cols):
        return lax.broadcasted_iota(I32, (rows, cols), 0)

    def own_row(c):
        z, x, y = quot(c, CX * NY), rest(quot(c, NY), CX), rest(c, NY)
        return ((z * (CX // 8) + quot(x, 8)) * NB + quot(y, 128)) * 8 + rest(x, 8)

    def group_row(c, e):
        z, x, y = quot(c, CX * NY), rest(quot(c, NY), CX), rest(c, NY)
        row = (((e * LZ + z) * (CX // 8) + quot(x, 8)) * NBL + quot(rest(y, NYL), 128)) * 8
        return jnp.where(quot(y, NYL) == l, row + rest(x, 8), -1)

    def rhs_row(f):
        r = quot(f, 128)
        return quot(r, RS) * 8 + rest(r, RS)

    def sol_row(f):
        d = quot(f, RPD)
        return rest(d, L) * 8 + quot(quot(d, L), HALF)

    def sol_lane(f):
        return rest(quot(quot(f, RPD), L), HALF) * RPD + rest(f, RPD)

    for name in ("cell", "front", "prod"):
        loads[name].wait()
    perf_own[...] = jnp.zeros((8, 128), F32)
    perf_own[0:2, :] = cell[...].astype(F32)
    perf_own[2:4, :] = front[...].astype(F32)
    perf_own[4:6, :] = prod[...]
    own = perf_own[...]
    perf_buf[l] = own
    own_t = jnp.transpose(jnp.concatenate([own, jnp.zeros((120, 128), F32)], axis=0))
    for h in range(2):
        c = own_t[:, h : h + 1].astype(I32)
        rown[h * 128 : (h + 1) * 128, :] = onehot(lane_iota(128, RO) == own_row(c))

    loads["rhs"].wait()
    loads["wts"].wait()
    for z in range(LZ):
        pres[z] = wts[0, z] * rhs[0, z] + wts[1, z] * rhs[1, z] + wts[2, z] * rhs[2, z]
    pieces = split3(jnp.concatenate([p for z in range(LZ) for p in tiles(pres[z])], axis=0))
    at_perf = pick_dot(rown[...], pieces)
    lanes = lane_iota(128, 128)
    spread, where_to = [], []
    for h in range(2):
        c = own_t[:, h : h + 1].astype(I32)
        f = own_t[:, 2 + h : 3 + h].astype(I32)
        value = jnp.sum(
            jnp.where(lanes == rest(c, 128), at_perf[h * 128 : (h + 1) * 128, :], 0.0),
            axis=1, keepdims=True,
        ) * own_t[:, 4 + h : 5 + h]
        spread.append(split3(jnp.where(lanes == rest(f, 128), value, 0.0)))
        where_to.append(onehot(row_iota(T * 8, 128) == rhs_row(own[2 + h : 3 + h, :].astype(I32))))
    part = pick_dot(jnp.concatenate(where_to, axis=1), jnp.concatenate(spread, axis=0))
    for i in range(T):
        fpart[i] = part[i * 8 : (i + 1) * 8, :]
    f1[t] = fpart[t]

    pl.semaphore_wait(barrier, len(peers))
    to_tiles(lambda p: fpart.at[p], f1, f1s, f1r)
    to_layers(lambda p: perf_own, perf_buf.at[l], pfs, pfr)
    mine = pl.ds(l * LZ, LZ)

    def spread_columns(i, src, dst):
        to_layers(lambda p: cols_block(src, p), dst.at[mine], bts.at[i], btr.at[i])
        pltpu.make_async_copy(cols_block(src, l), dst.at[mine], bto.at[i]).start()

    def columns_here(i, src, dst):
        from_layers(lambda p: dst.at[pl.ds(p * LZ, LZ)], bts.at[i], btr.at[i])
        pltpu.make_async_copy(cols_block(src, l), dst.at[mine], bto.at[i]).wait()

    spread_columns(0, st_h, stt)

    for h in range(2):
        c = own[h : h + 1, :].astype(I32)
        rto[:, h * 128 : (h + 1) * 128] = onehot(row_iota(RO, 128) == own_row(c))
    from_layers(lambda p: perf_buf.at[p], pfs, pfr)
    group_t = jnp.transpose(
        jnp.concatenate([perf_buf[i] for i in range(L)] + [jnp.zeros((128 - 8 * L, 128), F32)], axis=0)
    )
    for e in range(L):
        for h in range(2):
            b = (e * 2 + h) * 128
            c = group_t[:, e * 8 + h : e * 8 + h + 1].astype(I32)
            f = group_t[:, e * 8 + 2 + h : e * 8 + 3 + h].astype(I32)
            rgs[b : b + 128, :] = onehot(lane_iota(128, 8 * L) == sol_row(f))
            csol[b : b + 128, :] = jnp.where(
                lanes == sol_lane(f), group_t[:, e * 8 + 4 + h : e * 8 + 5 + h], 0.0
            )
            ccell[b : b + 128, :] = jnp.where(lanes == rest(c, 128), 1.0, 0.0)

    from_tiles(f1, f1s, f1r)
    f2[l] = add_up(f1, T)
    to_layers(lambda p: f2.at[l], f2.at[l], f2s, f2r)
    spread_columns(1, tz_h, tzt)
    spread_columns(2, pres, prest)
    send(tz_h.at[LZ - 1], tzp, tzs.at[0], tzr.at[0], (t, ln))
    loads["tx"].wait()
    for z in range(LZ):
        txs[z : z + 1, :] = tx[z, CX - 1 : CX, :]
    from_layers(lambda p: f2.at[p], f2s, f2r)
    f3[t] = add_up(f2, L)
    to_tiles(lambda p: f3.at[t], f3, f3s, f3r)
    send(txs, txp, txps.at[0], txpr.at[0], (tn, l))
    for e in range(L):
        for h in range(2):
            c = perf_buf[e, h : h + 1, :].astype(I32)
            rtg[:, (e * 2 + h) * 128 : (e * 2 + h + 1) * 128] = onehot(
                row_iota(L * LZ * RL, 128) == group_row(c, e)
            )
    loads["finv"].wait()
    from_tiles(f3, f3s, f3r)

    acc = jnp.zeros((RPD, 128), F32)
    for r in range(NFR):
        acc = acc + finv[:, r * 128 : (r + 1) * 128] * f3[r // RS, r % RS : r % RS + 1, :]
    rows = lax.dot_general(
        jnp.ones((8, 128), F32), acc, (((1,), (1,)), ((), ())),
        precision=lax.Precision.HIGHEST, preferred_element_type=F32,
    )
    rows = jnp.concatenate([rows] * HALF, axis=1)
    keep = (row_iota(8, 128) == t // HALF) & (quot(lane_iota(8, 128), RPD) == lax.rem(t, HALF))
    g1[t] = jnp.where(keep, rows, 0.0)
    to_tiles(lambda p: g1.at[t], g1, g1s, g1r)

    columns_here(0, st_h, stt)
    columns_here(1, tz_h, tzt)
    gprev = jnp.zeros((CX, NYL), F32)
    low = jnp.zeros((CX, NYL), F32)
    for k in range(L * LZ):
        up = tzt[k] if k < L * LZ - 1 else jnp.zeros((CX, NYL), F32)
        recip = 1.0 / (low + up + stt[k] - low * gprev)
        gprev = up * recip
        inv[k] = recip
        mul[k] = low * recip
        gam[k] = gprev
        low = up

    from_tiles(g1, g1s, g1r)
    g2[l] = add_up(g1, T)
    to_layers(lambda p: g2.at[l], g2.at[l], g2s, g2r)
    columns_here(2, pres, prest)
    from_layers(lambda p: g2.at[p], g2s, g2r)

    sol = split3(jnp.concatenate([g2[i] for i in range(L)], axis=0))
    picked = pick_dot(rgs[...], sol)
    for b in range(0, L * 256, 128):
        q = jnp.sum(picked[b : b + 128, :] * csol[b : b + 128, :], axis=1, keepdims=True)
        q3[b : b + 128, :] = split3(ccell[b : b + 128, :] * q)
    corr[...] = pick_dot(rtg[...], q3[...])
    d = jnp.zeros((CX, NYL), F32)
    for k in range(L * LZ):
        r = prest[k] - untile(corr[k * RL : (k + 1) * RL, :], CX, NYL)
        d = r * inv[k] + mul[k] * d
        pcol[k] = d
    for k in range(L * LZ - 2, -1, -1):
        d = pcol[k] + gam[k] * d
        pcol[k] = d
    for k in range(L * LZ):
        e, z = k // LZ, k % LZ
        hsend[0, e, z : z + 1, :] = pcol[k, CX - 1 : CX, :]
        hsend[1, e, z : z + 1, :] = pcol[k, 0:1, :]
    to_layers(lambda p: pcol.at[pl.ds(p * LZ, LZ)], cols_block(press, l), rts, rtr)
    pltpu.make_async_copy(pcol.at[mine], cols_block(press, l), rto_sem.at[0]).start()
    here = pl.ds(pl.multiple_of(l * NYL, NYL), NYL)
    for i in range(L):
        e = lax.rem(l + i, L)
        send(hsend.at[0, e], phalo.at[0, :, here], hls.at[0, i], hlr.at[0, i], (tn, e))
        send(hsend.at[1, e], phalo.at[1, :, here], hls.at[1, i], hlr.at[1, i], (tb, e))

    own_corr = pick_dot(rto[...], q3[pl.ds(pl.multiple_of(l * 256, 256), 256), :])
    for z in range(LZ):
        n = CX * NY // 128
        adj[z] = pres[z] - untile(own_corr[z * n : (z + 1) * n, :], CX, NY)
    for name in ("tz", "st", "ty", "bi", "bd"):
        loads[name].wait()
    arrived(tzp, tzs.at[0], tzr.at[0])
    arrived(txp, txps.at[0], txpr.at[0])
    from_layers(lambda p: cols_block(press, p), rts, rtr)
    pltpu.make_async_copy(pcol.at[mine], cols_block(press, l), rto_sem.at[0]).wait()
    for i in range(L):
        e = lax.rem(l + L - i, L)
        there = pl.ds(pl.multiple_of(e * NYL, NYL), NYL)
        arrived(phalo.at[0, :, there], hls.at[0, i], hlr.at[0, i])
        arrived(phalo.at[1, :, there], hls.at[1, i], hlr.at[1, i])

    sub, lane = row_iota(CX, NY), lane_iota(CX, NY)
    has_tb, has_tn = jnp.where(t > 0, 1.0, 0.0), jnp.where(t < T - 1, 1.0, 0.0)
    has_lb, has_ln = jnp.where(l > 0, 1.0, 0.0), jnp.where(l < L - 1, 1.0, 0.0)

    def from_xb(w, row):
        return jnp.where(sub == 0, row, pltpu.roll(w, 1, 0))

    def from_xn(v, row):
        return jnp.where(sub == CX - 1, row, pltpu.roll(v, CX - 1, 0))

    def from_yb(w):
        return jnp.where(lane == 0, 0.0, pltpu.roll(w, 1, 1))

    def from_yn(v):
        return jnp.where(lane == NY - 1, 0.0, pltpu.roll(v, NY - 1, 1))

    for z in [LZ - 1, 0] + list(range(1, LZ - 1)):
        p = press[z]
        before = tz[z - 1] if z else tzp[...] * has_lb
        after = tz[z] if z < LZ - 1 else tz[z] * has_ln
        near = (before + after + st[z]) * p - adj[z]
        near = near + tx[z] * from_xn(p, phalo[1, z : z + 1, :] * has_tn)
        near = near + from_xb(tx[z] * p, txp[z : z + 1, :] * phalo[0, z : z + 1, :] * has_tb)
        near = near + ty[z] * from_yn(p) + from_yb(ty[z] * p)
        r0 = rhs[0, z] - bd[0, 0, z] * p + near
        r1 = rhs[1, z] - bd[1, 0, z] * p
        r2 = rhs[2, z] - bd[2, 0, z] * p
        for c in range(3):
            v = bi[c, 0, z] * r0 + bi[c, 1, z] * r1 + bi[c, 2, z] * r2
            if c == 0:
                v = p + v
            search[c, z] = v
            i = c * LZ + z
            xsend[0, i : i + 1, :] = tx[z, CX - 1 : CX, :] * v[CX - 1 : CX, :]
            xsend[1, i : i + 1, :] = v[0:1, :]
            if z == LZ - 1:
                zsend[c] = tz[z] * v
        if z == LZ - 1:
            send(zsend, zhalo.at[0], zhs.at[0], zhr.at[0], (t, ln))
        if z == 0:
            send(search.at[:, 0], zhalo.at[1], zhs.at[1], zhr.at[1], (t, lb))
    send(xsend.at[0], xhalo.at[0], xhs.at[0], xhr.at[0], (tn, l))
    send(xsend.at[1], xhalo.at[1], xhs.at[1], xhr.at[1], (tb, l))
    out_search = pltpu.make_async_copy(search, search_o, outs.at[0])
    out_search.start()

    for i in range(2):
        arrived(xhalo.at[i], xhs.at[i], xhr.at[i])
    for i in range(2):
        arrived(zhalo.at[i], zhs.at[i], zhr.at[i])

    along = jnp.zeros((8, 128), F32)
    power = jnp.zeros((8, 128), F32)
    start = jnp.zeros((8, 128), F32)
    for z in range(LZ):
        for c in range(3):
            v = search[c, z]
            i = c * LZ + z
            near = tx[z] * from_xn(v, xhalo[1, i : i + 1, :] * has_tn)
            near = near + from_xb(tx[z] * v, xhalo[0, i : i + 1, :] * has_tb)
            near = near + ty[z] * from_yn(v) + from_yb(ty[z] * v)
            near = near + tz[z] * (search[c, z + 1] if z < LZ - 1 else zhalo[1, c] * has_ln)
            near = near + (tz[z - 1] * search[c, z - 1] if z else zhalo[0, c] * has_lb)
            im = (
                bd[c, 0, z] * search[0, z] + bd[c, 1, z] * search[1, z] + bd[c, 2, z] * search[2, z]
            ) - near
            image[c, z] = im
            b = rhs[c, z]
            along = along + fold(im * b)
            power = power + fold(im * im)
            start = start + fold(b * b)
    out_image = pltpu.make_async_copy(image, image_o, outs.at[1])
    out_image.start()
    along, power, start = total(along), total(power), total(start)
    guess = jnp.where(power > 0.0, along / jnp.where(power > 0.0, power, 1.0), 0.0)
    err = jnp.zeros((8, 128), F32)
    tilt = jnp.zeros((8, 128), F32)
    for z in range(LZ):
        for c in range(3):
            im = image[c, z]
            r = rhs[c, z] - guess * im
            err = err + fold(r * r)
            tilt = tilt + fold(r * im)
    row = jnp.zeros((8, 128), F32)
    lane8 = lane_iota(8, 128)
    for i, x in enumerate((guess, power, start, total(err), total(tilt), along)):
        row = jnp.where(lane8 == i, x, row)
    s1[l] = jnp.where(row_iota(8, 128) == l, row, 0.0)
    to_layers(lambda p: s1.at[l], s1.at[l], s1s, s1r)
    from_layers(lambda p: s1.at[p], s1s, s1r)
    s2[t] = add_up(s1, L)
    to_tiles(lambda p: s2.at[t], s2, s2s, s2r)
    from_tiles(s2, s2s, s2r)
    allrows = jnp.concatenate([s2[i] for i in range(T)], axis=0)
    sums = jnp.sum(allrows, axis=0, keepdims=True)
    omega = sums[:, 5:6] / sums[:, 1:2]
    shift = omega - allrows[:, 0:1]
    left = allrows[:, 3:4] - 2.0 * shift * allrows[:, 4:5] + shift * shift * allrows[:, 1:2]
    left = jnp.maximum(jnp.sum(left, axis=0, keepdims=True), 0.0)
    ratio = jnp.sqrt(left / sums[:, 2:3])
    stat_o[...] = jnp.where(lane8 == 0, omega, ratio)
    out_search.wait()
    out_image.wait()
    for copy in started:
        copy.wait_send()


def shards(rhs, wts, bd, bi, tx, ty, tz, st, cell, front, prod, finv):
    T, L = lax.axis_size("tile"), lax.axis_size("layer")
    _, LZ, CX, NY = rhs.shape
    RPD, NF = finv.shape
    NYL = NY // L
    RO, RG = LZ * CX * NY // 128, L * LZ * CX * NYL // 128
    K = L * 256
    field = (LZ, CX, NY)
    colf = (L * LZ, CX, NYL)
    V = lambda *s: pltpu.VMEM(s, F32)
    H = lambda *s: pltpu.VMEM(s, BF16)
    D = lambda *s: pltpu.SemaphoreType.DMA(s)
    scratch = [
        V(3, *field), V(3, *field), V(3, 3, *field), V(3, 3, *field),
        V(*field), V(*field), V(*field), V(*field),
        pltpu.VMEM((2, 128), I32), pltpu.VMEM((2, 128), I32), V(2, 128), V(RPD, NF),
        V(8, 128), V(L, 8, 128), V(*field), V(T, 8, 128), V(T, 8, 128), V(L, 8, 128), V(T, 8, 128),
        V(T, 8, 128), V(L, 8, 128),
        H(256, RO), H(RO, 256), H(RG, K), H(K, 8 * L), V(K, 128), V(K, 128), H(K, 384),
        V(*colf), V(*colf), V(*colf), V(*colf), V(*colf), V(*colf), V(*colf), V(RG, 128),
        V(CX, NY), V(8, NY), V(8, NY), V(*field), V(2, L, 8, NYL), V(2, 8, NY), V(*field),
        V(3, *field), V(3, *field), V(2, 16, NY), V(2, 16, NY), V(3, CX, NY), V(2, 3, CX, NY),
        V(L, 8, 128), V(T, 8, 128),
        D(12),
        D(T - 1), D(T - 1), D(L - 1), D(L - 1), D(T - 1), D(T - 1),
        D(T - 1), D(T - 1), D(L - 1), D(L - 1), D(L - 1), D(L - 1),
        D(3, L - 1), D(3, L - 1), D(3),
        D(1), D(1), D(1), D(1), D(L - 1), D(L - 1), D(1), D(2, L), D(2, L),
        D(2), D(2), D(2), D(2),
        D(L - 1), D(L - 1), D(T - 1), D(T - 1), D(2),
    ]
    anywhere = pl.BlockSpec(memory_space=pl.ANY)
    search, image, stat = pl.pallas_call(
        functools.partial(kernel, T, L, LZ, CX, NY, NF),
        out_shape=(
            jax.ShapeDtypeStruct(rhs.shape, F32),
            jax.ShapeDtypeStruct(rhs.shape, F32),
            jax.ShapeDtypeStruct((8, 128), F32),
        ),
        in_specs=[anywhere] * 12,
        out_specs=(anywhere, anywhere, pl.BlockSpec(memory_space=pltpu.VMEM)),
        scratch_shapes=scratch,
        compiler_params=pltpu.CompilerParams(
            collective_id=0, has_side_effects=True, vmem_limit_bytes=60 * 1024 * 1024
        ),
    )(
        rhs, wts, bd, bi, tx, ty, tz, st,
        cell.reshape(2, 128), front.reshape(2, 128), prod.reshape(2, 128), finv,
    )
    omega = stat[0, 0]
    return omega * search, rhs - omega * image, stat[0, 1]


def solution(mesh):
    return jax.shard_map(
        shards,
        mesh=mesh,
        in_specs=(
            P(None, "layer", "tile", None),
            P(None, "layer", "tile", None),
            P(None, None, "layer", "tile", None),
            P(None, None, "layer", "tile", None),
            P("layer", "tile", None),
            P("layer", "tile", None),
            P("layer", "tile", None),
            P("layer", "tile", None),
            P(("tile", "layer")),
            P(("tile", "layer")),
            P(("tile", "layer")),
            P(("tile", "layer"), None),
        ),
        out_specs=(P(None, "layer", "tile", None), P(None, "layer", "tile", None), P()),
        check_vma=False,
    )
```

```python
import functools

import jax
import jax.numpy as jnp
from jax import lax
from jax.experimental import pallas as pl
from jax.experimental.pallas import tpu as pltpu
from jax.sharding import PartitionSpec as P

MESH = pl.DeviceIdType.MESH
F32 = jnp.float32
BF16 = jnp.bfloat16
I32 = jnp.int32


def bits(n):
    assert n & (n - 1) == 0
    return n.bit_length() - 1


def quot(a, n):
    return lax.shift_right_logical(a, jnp.full_like(a, bits(n)))


def rest(a, n):
    return a & (n - 1)


def split2(x):
    hi = x.astype(BF16)
    return jnp.concatenate([hi, (x - hi.astype(F32)).astype(BF16)], axis=1)


def pick_dot(onehot, pieces):
    out = lax.dot_general(onehot, pieces, (((1,), (0,)), ((), ())), preferred_element_type=F32)
    n = out.shape[1] // 2
    return out[:, :n] + out[:, n:]


def tiles(block):
    rows, cols = block.shape
    return [
        block[i : i + 8, j : j + 128] for i in range(0, rows, 8) for j in range(0, cols, 128)
    ]


def untile(mat, rows, cols):
    per = cols // 128
    out = []
    for i in range(rows // 8):
        out.append(
            jnp.concatenate(
                [mat[(i * per + j) * 8 : (i * per + j + 1) * 8, :] for j in range(per)], axis=1
            )
        )
    return jnp.concatenate(out, axis=0)


def fold(block):
    parts = tiles(block)
    while len(parts) > 1:
        parts = [a + b for a, b in zip(parts[::2], parts[1::2])]
    return parts[0]


def total(x):
    return jnp.sum(jnp.sum(x, axis=1, keepdims=True), axis=0, keepdims=True)


def onehot(mask):
    return jnp.where(mask, 1.0, 0.0).astype(BF16)


def kernel(
    T, L, LZ, CX, NY, NF,
    rhs_h, wts_h, bd_h, bi_h, tx_h, ty_h, tz_h, st_h, cell_h, front_h, prod_h, finv_h,
    search, image, omega_o, ratio_o,
    rhs, wts, bd, bi, tx, ty, tz, st, cell, front, prod, finv,
    perf_own, perf_buf, pres, fpart, f1, f2, f3, g1, g2,
    rown, rto, rtg, rgs, csol, ccell, q3,
    prest, tzt, stt, inv, mul, gam, pcol, corr,
    tzp, txs, txp, press, hsend, phalo, adj,
    slope, diag, xsend, xhalo, zsend, zhalo, s1, s2,
    ld, f1s, f1r, f2s, f2r, f3s, f3r, g1s, g1r, g2s, g2r, pfs, pfr, bts, btr, bto,
    tzs, tzr, txps, txpr, rts, rtr, rto_sem, hls, hlr, xhs, xhr, zhs, zhr,
    s1s, s1r, s2s, s2r,
):
    NYL, NFR = NY // L, NF // 128
    NBL, RS, RPD = NYL // 128, NFR // T, NF // (T * L)
    HALF = 128 // RPD
    RL = CX * NYL // 128
    RO = LZ * CX * NY // 128
    NB = NY // 128
    t, l = lax.axis_index("tile"), lax.axis_index("layer")

    loads = {}
    order = [
        ("cell", cell_h, cell), ("front", front_h, front), ("prod", prod_h, prod),
        ("rhs", rhs_h, rhs), ("wts", wts_h, wts), ("finv", finv_h, finv), ("tx", tx_h, tx),
        ("tz", tz_h, tz), ("st", st_h, st), ("ty", ty_h, ty), ("bi", bi_h, bi), ("bd", bd_h, bd),
    ]
    for i, (name, src, dst) in enumerate(order):
        loads[name] = pltpu.make_async_copy(src, dst, ld.at[i])
        if i < 5:
            loads[name].start()

    tn, tb = lax.rem(t + 1, T), lax.rem(t + T - 1, T)
    ln, lb = lax.rem(l + 1, L), lax.rem(l + L - 1, L)
    barrier = pltpu.get_barrier_semaphore()
    peers = [(t, lax.rem(l + i, L)) for i in range(1, L)]
    peers += [(lax.rem(t + i, T), l) for i in range(1, T)]
    peers += [(a, lax.rem(l + i, L)) for a in (tn, tb) for i in range(1, L)]
    for peer in peers:
        pl.semaphore_signal(barrier, inc=1, device_id=peer, device_id_type=MESH)

    started = []

    def send(*args):
        started.append(push(*args))

    def push(src, dst, ssem, rsem, to):
        copy = pltpu.make_async_remote_copy(
            src_ref=src, dst_ref=dst, send_sem=ssem, recv_sem=rsem,
            device_id=to, device_id_type=MESH,
        )
        copy.start()
        return copy

    def arrived(dst, ssem, rsem):
        pltpu.make_async_remote_copy(
            src_ref=dst, dst_ref=dst, send_sem=ssem, recv_sem=rsem,
            device_id=(t, l), device_id_type=MESH,
        ).wait_recv()

    def to_tiles(src, dst, ss, rs):
        for i in range(1, T):
            peer = lax.rem(t + i, T)
            send(src(peer), dst.at[t], ss.at[i - 1], rs.at[i - 1], (peer, l))

    def from_tiles(dst, ss, rs):
        for i in range(1, T):
            arrived(dst.at[lax.rem(t + T - i, T)], ss.at[i - 1], rs.at[i - 1])

    def to_layers(src, dst, ss, rs):
        for i in range(1, L):
            peer = lax.rem(l + i, L)
            send(src(peer), dst, ss.at[i - 1], rs.at[i - 1], (t, peer))

    def from_layers(dst, ss, rs):
        for i in range(1, L):
            arrived(dst(lax.rem(l + L - i, L)), ss.at[i - 1], rs.at[i - 1])

    def add_up(buf, n):
        parts = [buf[i] for i in range(n)]
        while len(parts) > 1:
            parts = [a + b for a, b in zip(parts[::2], parts[1::2])]
        return parts[0]

    def cols_block(ref, i):
        return ref.at[:, :, pl.ds(pl.multiple_of(i * NYL, NYL), NYL)]

    def lane_iota(rows, cols):
        return lax.broadcasted_iota(I32, (rows, cols), 1)

    def row_iota(rows, cols):
        return lax.broadcasted_iota(I32, (rows, cols), 0)

    def own_row(c):
        z, x, y = quot(c, CX * NY), rest(quot(c, NY), CX), rest(c, NY)
        return ((z * (CX // 8) + quot(x, 8)) * NB + quot(y, 128)) * 8 + rest(x, 8)

    def group_row(c, e):
        z, x, y = quot(c, CX * NY), rest(quot(c, NY), CX), rest(c, NY)
        row = (((e * LZ + z) * (CX // 8) + quot(x, 8)) * NBL + quot(rest(y, NYL), 128)) * 8
        return jnp.where(quot(y, NYL) == l, row + rest(x, 8), -1)

    def rhs_row(f):
        r = quot(f, 128)
        return r

    def sol_row(f):
        d = quot(f, RPD)
        return rest(d, L) * 8 + quot(quot(d, L), HALF)

    def sol_lane(f):
        return rest(quot(quot(f, RPD), L), HALF) * RPD + rest(f, RPD)

    for name in ("cell", "front", "prod"):
        loads[name].wait()
    perf_own[...] = jnp.zeros((8, 128), F32)
    perf_own[0:2, :] = cell[...].astype(F32)
    perf_own[2:4, :] = front[...].astype(F32)
    perf_own[4:6, :] = prod[...]
    own = perf_own[...]
    perf_buf[l] = own
    own_t = jnp.transpose(jnp.concatenate([own, jnp.zeros((120, 128), F32)], axis=0))
    for h in range(2):
        c = own_t[:, h : h + 1].astype(I32)
        rown[h * 128 : (h + 1) * 128, :] = onehot(lane_iota(128, RO) == own_row(c))

    loads["rhs"].wait()
    loads["wts"].wait()
    for name, _, _ in order[5:]:
        loads[name].start()
    for z in range(LZ):
        pres[z] = wts[0, z] * rhs[0, z] + wts[1, z] * rhs[1, z] + wts[2, z] * rhs[2, z]
    pieces = split2(jnp.concatenate([p for z in range(LZ) for p in tiles(pres[z])], axis=0))
    at_perf = pick_dot(rown[...], pieces)
    lanes = lane_iota(128, 128)
    spread, where_to = [], []
    for h in range(2):
        c = own_t[:, h : h + 1].astype(I32)
        f = own_t[:, 2 + h : 3 + h].astype(I32)
        value = jnp.sum(
            jnp.where(lanes == rest(c, 128), at_perf[h * 128 : (h + 1) * 128, :], 0.0),
            axis=1, keepdims=True,
        ) * own_t[:, 4 + h : 5 + h]
        spread.append(split2(jnp.where(lanes == rest(f, 128), value, 0.0)))
        where_to.append(onehot(row_iota(NFR, 128) == rhs_row(own[2 + h : 3 + h, :].astype(I32))))
    part = pick_dot(jnp.concatenate(where_to, axis=1), jnp.concatenate(spread, axis=0))
    for i in range(T):
        fpart[i] = part[i * RS : (i + 1) * RS, :]
    f1[t] = fpart[t]

    pl.semaphore_wait(barrier, len(peers))
    to_tiles(lambda p: fpart.at[p], f1, f1s, f1r)
    to_layers(lambda p: perf_own, perf_buf.at[l], pfs, pfr)
    mine = pl.ds(l * LZ, LZ)

    def spread_columns(i, src, dst):
        to_layers(lambda p: cols_block(src, p), dst.at[mine], bts.at[i], btr.at[i])
        pltpu.make_async_copy(cols_block(src, l), dst.at[mine], bto.at[i]).start()

    def columns_here(i, src, dst):
        from_layers(lambda p: dst.at[pl.ds(p * LZ, LZ)], bts.at[i], btr.at[i])
        pltpu.make_async_copy(cols_block(src, l), dst.at[mine], bto.at[i]).wait()

    spread_columns(0, st_h, stt)

    for h in range(2):
        c = own[h : h + 1, :].astype(I32)
        rto[:, h * 128 : (h + 1) * 128] = onehot(row_iota(RO, 128) == own_row(c))
    from_layers(lambda p: perf_buf.at[p], pfs, pfr)
    group_t = jnp.transpose(
        jnp.concatenate([perf_buf[i] for i in range(L)] + [jnp.zeros((128 - 8 * L, 128), F32)], axis=0)
    )
    for e in range(L):
        for h in range(2):
            b = (e * 2 + h) * 128
            c = group_t[:, e * 8 + h : e * 8 + h + 1].astype(I32)
            f = group_t[:, e * 8 + 2 + h : e * 8 + 3 + h].astype(I32)
            rgs[b : b + 128, :] = onehot(lane_iota(128, 8 * L) == sol_row(f))
            csol[b : b + 128, :] = jnp.where(
                lanes == sol_lane(f), group_t[:, e * 8 + 4 + h : e * 8 + 5 + h], 0.0
            )
            ccell[b : b + 128, :] = jnp.where(lanes == rest(c, 128), 1.0, 0.0)

    from_tiles(f1, f1s, f1r)
    f2[l] = add_up(f1, T)
    to_layers(lambda p: f2.at[l], f2.at[l], f2s, f2r)
    spread_columns(1, tz_h, tzt)
    spread_columns(2, pres, prest)
    send(tz_h.at[LZ - 1], tzp, tzs.at[0], tzr.at[0], (t, ln))
    loads["tx"].wait()
    for z in range(LZ):
        txs[z : z + 1, :] = tx[z, CX - 1 : CX, :]
    from_layers(lambda p: f2.at[p], f2s, f2r)
    f3[t] = add_up(f2, L)
    to_tiles(lambda p: f3.at[t], f3, f3s, f3r)
    send(txs, txp, txps.at[0], txpr.at[0], (tn, l))
    for e in range(L):
        for h in range(2):
            c = perf_buf[e, h : h + 1, :].astype(I32)
            rtg[:, (e * 2 + h) * 128 : (e * 2 + h + 1) * 128] = onehot(
                row_iota(L * LZ * RL, 128) == group_row(c, e)
            )
    loads["finv"].wait()
    from_tiles(f3, f3s, f3r)

    acc = jnp.zeros((RPD, 128), F32)
    for r in range(NFR):
        acc = acc + finv[:, r * 128 : (r + 1) * 128] * f3[r // RS, r % RS : r % RS + 1, :]
    rows = lax.dot_general(
        jnp.ones((8, 128), F32), acc, (((1,), (1,)), ((), ())),
        precision=lax.Precision.HIGHEST, preferred_element_type=F32,
    )
    rows = jnp.concatenate([rows] * HALF, axis=1)
    g1[t] = jnp.where(quot(lane_iota(1, 128), RPD) == lax.rem(t, HALF), rows[0:1, :], 0.0)
    to_tiles(lambda p: g1.at[t], g1, g1s, g1r)

    columns_here(0, st_h, stt)
    columns_here(1, tz_h, tzt)
    gprev = jnp.zeros((CX, NYL), F32)
    low = jnp.zeros((CX, NYL), F32)
    for k in range(L * LZ):
        up = tzt[k] if k < L * LZ - 1 else jnp.zeros((CX, NYL), F32)
        recip = 1.0 / (low + up + stt[k] - low * gprev)
        gprev = up * recip
        inv[k] = recip
        mul[k] = low * recip
        gam[k] = gprev
        low = up

    from_tiles(g1, g1s, g1r)
    pairs = [sum(g1[i + j] for j in range(1, HALF)) + g1[i] for i in range(0, T, HALF)]
    pairs += [jnp.zeros((1, 128), F32)] * (8 - len(pairs))
    g2[l] = jnp.concatenate(pairs, axis=0)
    to_layers(lambda p: g2.at[l], g2.at[l], g2s, g2r)
    columns_here(2, pres, prest)
    from_layers(lambda p: g2.at[p], g2s, g2r)

    sol = split2(jnp.concatenate([g2[i] for i in range(L)], axis=0))
    picked = pick_dot(rgs[...], sol)
    for b in range(0, L * 256, 128):
        q = jnp.sum(picked[b : b + 128, :] * csol[b : b + 128, :], axis=1, keepdims=True)
        q3[b : b + 128, :] = split2(ccell[b : b + 128, :] * q)
    corr[...] = pick_dot(rtg[...], q3[...])
    d = jnp.zeros((CX, NYL), F32)
    for k in range(L * LZ):
        r = prest[k] - untile(corr[k * RL : (k + 1) * RL, :], CX, NYL)
        d = r * inv[k] + mul[k] * d
        pcol[k] = d
    for k in range(L * LZ - 2, -1, -1):
        d = pcol[k] + gam[k] * d
        pcol[k] = d
    for k in range(L * LZ):
        e, z = k // LZ, k % LZ
        hsend[0, e, z : z + 1, :] = pcol[k, CX - 1 : CX, :]
        hsend[1, e, z : z + 1, :] = pcol[k, 0:1, :]
    to_layers(lambda p: pcol.at[pl.ds(p * LZ, LZ)], cols_block(press, l), rts, rtr)
    pltpu.make_async_copy(pcol.at[mine], cols_block(press, l), rto_sem.at[0]).start()
    here = pl.ds(pl.multiple_of(l * NYL, NYL), NYL)
    for i in range(L):
        e = lax.rem(l + i, L)
        send(hsend.at[0, e], phalo.at[0, :, here], hls.at[0, i], hlr.at[0, i], (tn, e))
        send(hsend.at[1, e], phalo.at[1, :, here], hls.at[1, i], hlr.at[1, i], (tb, e))

    own_corr = pick_dot(rto[...], q3[pl.ds(pl.multiple_of(l * 256, 256), 256), :])
    for z in range(LZ):
        n = CX * NY // 128
        adj[z] = pres[z] - untile(own_corr[z * n : (z + 1) * n, :], CX, NY)
    for name in ("tz", "st", "ty", "bi", "bd"):
        loads[name].wait()
    arrived(tzp, tzs.at[0], tzr.at[0])
    arrived(txp, txps.at[0], txpr.at[0])
    has_tb, has_tn = jnp.where(t > 0, 1.0, 0.0), jnp.where(t < T - 1, 1.0, 0.0)
    has_lb, has_ln = jnp.where(l > 0, 1.0, 0.0), jnp.where(l < L - 1, 1.0, 0.0)
    start = jnp.zeros((8, 128), F32)
    for z in range(LZ):
        before = tz[z - 1] if z else tzp[...] * has_lb
        diag[z] = before + (tz[z] if z < LZ - 1 else tz[z] * has_ln) + st[z]
        for c in range(3):
            b = [bi[c, d, z] for d in range(3)]
            search[c, z] = b[0] * rhs[0, z] + b[1] * rhs[1, z] + b[2] * rhs[2, z]
            slope[c, z] = (1.0 if c == 0 else 0.0) - (
                b[0] * bd[0, 0, z] + b[1] * bd[1, 0, z] + b[2] * bd[2, 0, z]
            )
            start = start + fold(rhs[c, z] * rhs[c, z])
    from_layers(lambda p: cols_block(press, p), rts, rtr)
    pltpu.make_async_copy(pcol.at[mine], cols_block(press, l), rto_sem.at[0]).wait()
    for i in range(L):
        e = lax.rem(l + L - i, L)
        there = pl.ds(pl.multiple_of(e * NYL, NYL), NYL)
        arrived(phalo.at[0, :, there], hls.at[0, i], hlr.at[0, i])
        arrived(phalo.at[1, :, there], hls.at[1, i], hlr.at[1, i])

    sub, lane = row_iota(CX, NY), lane_iota(CX, NY)

    def from_xb(w, row):
        return jnp.where(sub == 0, row, pltpu.roll(w, 1, 0))

    def from_xn(v, row):
        return jnp.where(sub == CX - 1, row, pltpu.roll(v, CX - 1, 0))

    def from_yb(w):
        return jnp.where(lane == 0, 0.0, pltpu.roll(w, 1, 1))

    def from_yn(v):
        return jnp.where(lane == NY - 1, 0.0, pltpu.roll(v, NY - 1, 1))

    for z in [LZ - 1, 0] + list(range(1, LZ - 1)):
        p = press[z]
        near = diag[z] * p - adj[z]
        near = near + tx[z] * from_xn(p, phalo[1, z : z + 1, :] * has_tn)
        near = near + from_xb(tx[z] * p, txp[z : z + 1, :] * phalo[0, z : z + 1, :] * has_tb)
        near = near + ty[z] * from_yn(p) + from_yb(ty[z] * p)
        for c in range(3):
            v = search[c, z] + slope[c, z] * p + bi[c, 0, z] * near
            search[c, z] = v
            i = c * LZ + z
            xsend[0, i : i + 1, :] = tx[z, CX - 1 : CX, :] * v[CX - 1 : CX, :]
            xsend[1, i : i + 1, :] = v[0:1, :]
            if z == LZ - 1:
                zsend[c] = tz[z] * v
        if z == LZ - 1:
            send(zsend, zhalo.at[0], zhs.at[0], zhr.at[0], (t, ln))
        if z == 0:
            send(search.at[:, 0], zhalo.at[1], zhs.at[1], zhr.at[1], (t, lb))
    send(xsend.at[0], xhalo.at[0], xhs.at[0], xhr.at[0], (tn, l))
    send(xsend.at[1], xhalo.at[1], xhs.at[1], xhr.at[1], (tb, l))
    along = jnp.zeros((8, 128), F32)
    power = jnp.zeros((8, 128), F32)
    none = jnp.zeros((1, NY), F32)
    for z in range(LZ):
        for c in range(3):
            v = search[c, z]
            near = tx[z] * from_xn(v, none) + from_xb(tx[z] * v, none)
            near = near + ty[z] * from_yn(v) + from_yb(ty[z] * v)
            if z < LZ - 1:
                near = near + tz[z] * search[c, z + 1]
            if z:
                near = near + tz[z - 1] * search[c, z - 1]
            im = (
                bd[c, 0, z] * search[0, z] + bd[c, 1, z] * search[1, z] + bd[c, 2, z] * search[2, z]
            ) - near
            image[c, z] = im
            along = along + fold(im * rhs[c, z])
            power = power + fold(im * im)
    along, power = total(along), total(power)
    guess = jnp.where(power > 0.0, along / jnp.where(power > 0.0, power, 1.0), 0.0)

    for i in range(2):
        arrived(xhalo.at[i], xhs.at[i], xhr.at[i])
    for z in range(LZ):
        for c in range(3):
            i = c * LZ + z
            image[c, z, 0:1, :] = image[c, z, 0:1, :] - xhalo[0, i : i + 1, :] * has_tb
            image[c, z, CX - 1 : CX, :] = (
                image[c, z, CX - 1 : CX, :] - tx[z, CX - 1 : CX, :] * (xhalo[1, i : i + 1, :] * has_tn)
            )
    along = jnp.zeros((8, 128), F32)
    power = jnp.zeros((8, 128), F32)
    err = jnp.zeros((8, 128), F32)
    for z in list(range(1, LZ - 1)) + [0] + ([LZ - 1] if LZ > 1 else []):
        if z == 0:
            for i in range(2):
                arrived(zhalo.at[i], zhs.at[i], zhr.at[i])
        for c in range(3):
            im = image[c, z]
            if z == 0:
                im = im - zhalo[0, c] * has_lb
            if z == LZ - 1:
                im = im - tz[z] * (zhalo[1, c] * has_ln)
            if z in (0, LZ - 1):
                image[c, z] = im
            b = rhs[c, z]
            r = b - guess * im
            along = along + fold(im * b)
            power = power + fold(im * im)
            err = err + fold(r * r)
    along, power, start = total(along), total(power), total(start)
    tilt = along - guess * power
    row = jnp.zeros((8, 128), F32)
    lane8 = lane_iota(8, 128)
    for i, x in enumerate((guess, power, start, total(err), tilt, along)):
        row = jnp.where(lane8 == i, x, row)
    s1[l] = jnp.where(row_iota(8, 128) == l, row, 0.0)
    to_layers(lambda p: s1.at[l], s1.at[l], s1s, s1r)
    from_layers(lambda p: s1.at[p], s1s, s1r)
    s2[t] = add_up(s1, L)
    ahead = list(started)
    started.clear()
    to_tiles(lambda p: s2.at[t], s2, s2s, s2r)
    for copy in ahead:
        copy.wait_send()
    from_tiles(s2, s2s, s2r)
    allrows = jnp.concatenate([s2[i] for i in range(T)], axis=0)
    sums = jnp.sum(allrows, axis=0, keepdims=True)
    omega = sums[:, 5:6] / sums[:, 1:2]
    shift = omega - allrows[:, 0:1]
    left = allrows[:, 3:4] - 2.0 * shift * allrows[:, 4:5] + shift * shift * allrows[:, 1:2]
    left = jnp.maximum(jnp.sum(left, axis=0, keepdims=True), 0.0)
    ratio = jnp.sqrt(left / sums[:, 2:3])
    omega_o[...] = omega
    ratio_o[...] = ratio
    for copy in started:
        copy.wait_send()


def shards(rhs, wts, bd, bi, tx, ty, tz, st, cell, front, prod, finv):
    T, L = lax.axis_size("tile"), lax.axis_size("layer")
    _, LZ, CX, NY = rhs.shape
    RPD, NF = finv.shape
    NYL = NY // L
    RO, RG = LZ * CX * NY // 128, L * LZ * CX * NYL // 128
    K = L * 256
    RS = NF // 128 // T
    field = (LZ, CX, NY)
    colf = (L * LZ, CX, NYL)
    V = lambda *s: pltpu.VMEM(s, F32)
    H = lambda *s: pltpu.VMEM(s, BF16)
    D = lambda *s: pltpu.SemaphoreType.DMA(s)
    scratch = [
        V(3, *field), V(3, *field), V(3, 3, *field), V(3, 3, *field),
        V(*field), V(*field), V(*field), V(*field),
        pltpu.VMEM((2, 128), I32), pltpu.VMEM((2, 128), I32), V(2, 128), V(RPD, NF),
        V(8, 128), V(L, 8, 128), V(*field), V(T, RS, 128), V(T, RS, 128), V(L, RS, 128), V(T, RS, 128),
        V(T, 1, 128), V(L, 8, 128),
        H(256, RO), H(RO, 256), H(RG, K), H(K, 8 * L), V(K, 128), V(K, 128), H(K, 256),
        V(*colf), V(*colf), V(*colf), V(*colf), V(*colf), V(*colf), V(*colf), V(RG, 128),
        V(CX, NY), V(8, NY), V(8, NY), V(*field), V(2, L, 8, NYL), V(2, 8, NY), V(*field),
        V(3, *field), V(*field), V(2, 16, NY), V(2, 16, NY), V(3, CX, NY), V(2, 3, CX, NY),
        V(L, 8, 128), V(T, 8, 128),
        D(12),
        D(T - 1), D(T - 1), D(L - 1), D(L - 1), D(T - 1), D(T - 1),
        D(T - 1), D(T - 1), D(L - 1), D(L - 1), D(L - 1), D(L - 1),
        D(3, L - 1), D(3, L - 1), D(3),
        D(1), D(1), D(1), D(1), D(L - 1), D(L - 1), D(1), D(2, L), D(2, L),
        D(2), D(2), D(2), D(2),
        D(L - 1), D(L - 1), D(T - 1), D(T - 1),
    ]
    anywhere = pl.BlockSpec(memory_space=pl.ANY)
    search, image, omega, ratio = pl.pallas_call(
        functools.partial(kernel, T, L, LZ, CX, NY, NF),
        out_shape=(
            pltpu.VMEM(rhs.shape, F32),
            pltpu.VMEM(rhs.shape, F32),
            jax.ShapeDtypeStruct((1, 1), F32),
            jax.ShapeDtypeStruct((1, 1), F32),
        ),
        in_specs=[anywhere] * 12,
        out_specs=(pl.BlockSpec(memory_space=pltpu.VMEM),) * 2 + (pl.BlockSpec(memory_space=pltpu.VMEM),) * 2,
        scratch_shapes=scratch,
        compiler_params=pltpu.CompilerParams(
            collective_id=0, has_side_effects=True, vmem_limit_bytes=int(56 * 1024 * 1024)
        ),
    )(
        rhs, wts, bd, bi, tx, ty, tz, st,
        cell.reshape(2, 128), front.reshape(2, 128), prod.reshape(2, 128), finv,
    )
    omega = omega[0, 0]
    return omega * search, rhs - omega * image, ratio[0, 0]


def solution(mesh):
    return jax.shard_map(
        shards,
        mesh=mesh,
        in_specs=(
            P(None, "layer", "tile", None),
            P(None, "layer", "tile", None),
            P(None, None, "layer", "tile", None),
            P(None, None, "layer", "tile", None),
            P("layer", "tile", None),
            P("layer", "tile", None),
            P("layer", "tile", None),
            P("layer", "tile", None),
            P(("tile", "layer")),
            P(("tile", "layer")),
            P(("tile", "layer")),
            P(("tile", "layer"), None),
        ),
        out_specs=(P(None, "layer", "tile", None), P(None, "layer", "tile", None), P()),
        check_vma=False,
    )
```

```python
import functools

import jax
import jax.numpy as jnp
from jax import lax
from jax.experimental import pallas as pl
from jax.experimental.pallas import tpu as pltpu
from jax.sharding import PartitionSpec as P

MESH = pl.DeviceIdType.MESH
F32 = jnp.float32
BF16 = jnp.bfloat16
I32 = jnp.int32


def bits(n):
    assert n & (n - 1) == 0
    return n.bit_length() - 1


def quot(a, n):
    return lax.shift_right_logical(a, jnp.full_like(a, bits(n)))


def rest(a, n):
    return a & (n - 1)


def split2(x):
    hi = x.astype(BF16)
    return jnp.concatenate([hi, (x - hi.astype(F32)).astype(BF16)], axis=1)


def pick_dot(onehot, pieces):
    out = lax.dot_general(onehot, pieces, (((1,), (0,)), ((), ())), preferred_element_type=F32)
    n = out.shape[1] // 2
    return out[:, :n] + out[:, n:]


def tiles(block):
    rows, cols = block.shape
    return [
        block[i : i + 8, j : j + 128] for i in range(0, rows, 8) for j in range(0, cols, 128)
    ]


def untile(mat, rows, cols):
    per = cols // 128
    out = []
    for i in range(rows // 8):
        out.append(
            jnp.concatenate(
                [mat[(i * per + j) * 8 : (i * per + j + 1) * 8, :] for j in range(per)], axis=1
            )
        )
    return jnp.concatenate(out, axis=0)


def fold(block):
    parts = tiles(block)
    while len(parts) > 1:
        parts = [a + b for a, b in zip(parts[::2], parts[1::2])]
    return parts[0]


def total(x):
    return jnp.sum(jnp.sum(x, axis=1, keepdims=True), axis=0, keepdims=True)


def onehot(mask):
    return jnp.where(mask, 1.0, 0.0).astype(BF16)


def kernel(
    T, L, LZ, CX, NY, NF,
    rhs_h, wts_h, bd_h, bi_h, tx_h, ty_h, tz_h, st_h, cell_h, front_h, prod_h, finv_h,
    search, image, omega_o, ratio_o,
    rhs, wts, bd, bi, tx, ty, tz, st, cell, front, prod, finv,
    perf_own, perf_buf, pres, fpart, f1, f2, f3, g1, g2,
    rown, rto, rtg, rgs, csol, ccell, q3, qs,
    alpha, beta, pivot, ratio_up, mred, rred, mcol, rcol, inv, mul, gam, ucol, corr,
    tzp, txs, txp, asend, ahalo, wsend, whalo, ends, hsend, phalo, adj, inner,
    slope, diag, xsend, xhalo, zsend, zhalo, s1, s2,
    ld, f1s, f1r, f2s, f2r, f3s, f3r, g1s, g1r, g2s, g2r, pfs, pfr, bts, btr, bto,
    tzs, tzr, txps, txpr, ahs, ahr, whs, whr, rts, rtr, rto_sem, hls, hlr, xhs, xhr, zhs, zhr,
    s1s, s1r, s2s, s2r,
):
    NYL, NFR = NY // L, NF // 128
    NBL, RS, RPD = NYL // 128, NFR // L, NF // (T * L)
    N = LZ - 1
    HALF = 128 // RPD
    RL = CX * NYL // 128
    RO = LZ * CX * NY // 128
    NB = NY // 128
    t, l = lax.axis_index("tile"), lax.axis_index("layer")

    loads = {}
    order = [
        ("cell", cell_h, cell), ("front", front_h, front), ("prod", prod_h, prod),
        ("rhs", rhs_h, rhs), ("wts", wts_h, wts), ("tz", tz_h, tz), ("st", st_h, st),
        ("finv", finv_h, finv), ("tx", tx_h, tx), ("ty", ty_h, ty), ("bi", bi_h, bi), ("bd", bd_h, bd),
    ]
    for i, (name, src, dst) in enumerate(order):
        loads[name] = pltpu.make_async_copy(src, dst, ld.at[i])
        if i < 5:
            loads[name].start()

    tn, tb = lax.rem(t + 1, T), lax.rem(t + T - 1, T)
    ln, lb = lax.rem(l + 1, L), lax.rem(l + L - 1, L)
    barrier = pltpu.get_barrier_semaphore()
    peers = [(t, lax.rem(l + i, L)) for i in range(1, L)]
    peers += [(lax.rem(t + i, T), l) for i in range(1, T)]
    peers += [(a, lax.rem(l + i, L)) for a in (tn, tb) for i in range(1, L)]
    for peer in peers:
        pl.semaphore_signal(barrier, inc=1, device_id=peer, device_id_type=MESH)

    started = []

    def send(*args):
        started.append(push(*args))

    def push(src, dst, ssem, rsem, to):
        copy = pltpu.make_async_remote_copy(
            src_ref=src, dst_ref=dst, send_sem=ssem, recv_sem=rsem,
            device_id=to, device_id_type=MESH,
        )
        copy.start()
        return copy

    def arrived(dst, ssem, rsem):
        pltpu.make_async_remote_copy(
            src_ref=dst, dst_ref=dst, send_sem=ssem, recv_sem=rsem,
            device_id=(t, l), device_id_type=MESH,
        ).wait_recv()

    def to_tiles(src, dst, ss, rs):
        for i in range(1, T):
            peer = lax.rem(t + i, T)
            send(src(peer), dst.at[t], ss.at[i - 1], rs.at[i - 1], (peer, l))

    def from_tiles(dst, ss, rs):
        for i in range(1, T):
            arrived(dst.at[lax.rem(t + T - i, T)], ss.at[i - 1], rs.at[i - 1])

    def to_layers(src, dst, ss, rs):
        for i in range(1, L):
            peer = lax.rem(l + i, L)
            send(src(peer), dst, ss.at[i - 1], rs.at[i - 1], (t, peer))

    def from_layers(dst, ss, rs):
        for i in range(1, L):
            arrived(dst(lax.rem(l + L - i, L)), ss.at[i - 1], rs.at[i - 1])

    def add_up(buf, n):
        parts = [buf[i] for i in range(n)]
        while len(parts) > 1:
            parts = [a + b for a, b in zip(parts[::2], parts[1::2])]
        return parts[0]

    def cols_block(ref, i):
        return ref.at[:, :, pl.ds(pl.multiple_of(i * NYL, NYL), NYL)]

    def lane_iota(rows, cols):
        return lax.broadcasted_iota(I32, (rows, cols), 1)

    def row_iota(rows, cols):
        return lax.broadcasted_iota(I32, (rows, cols), 0)

    def own_row(c):
        z, x, y = quot(c, CX * NY), rest(quot(c, NY), CX), rest(c, NY)
        return ((z * (CX // 8) + quot(x, 8)) * NB + quot(y, 128)) * 8 + rest(x, 8)

    def column_row(c):
        x, y = rest(quot(c, NY), CX), rest(c, NY)
        row = (quot(x, 8) * NBL + quot(rest(y, NYL), 128)) * 8 + rest(x, 8)
        return jnp.where(quot(y, NYL) == l, row, -(L + 1) * RL)

    def sol_row(f):
        d = quot(f, RPD)
        return rest(d, L) * 8 + quot(quot(d, L), HALF)

    def sol_lane(f):
        return rest(quot(quot(f, RPD), L), HALF) * RPD + rest(f, RPD)

    for name in ("cell", "front", "prod"):
        loads[name].wait()
    perf_own[...] = jnp.zeros((8, 128), F32)
    perf_own[0:2, :] = cell[...].astype(F32)
    perf_own[2:4, :] = front[...].astype(F32)
    perf_own[4:6, :] = prod[...]
    own = perf_own[...]
    own_t = jnp.transpose(jnp.concatenate([own, jnp.zeros((120, 128), F32)], axis=0))
    for h in range(2):
        c = own_t[:, h : h + 1].astype(I32)
        rown[h * 128 : (h + 1) * 128, :] = onehot(lane_iota(128, RO) == own_row(c))

    loads["rhs"].wait()
    loads["wts"].wait()
    for name, _, _ in order[5:]:
        loads[name].start()
    for z in range(LZ):
        pres[z] = wts[0, z] * rhs[0, z] + wts[1, z] * rhs[1, z] + wts[2, z] * rhs[2, z]
    pieces = split2(jnp.concatenate([p for z in range(LZ) for p in tiles(pres[z])], axis=0))
    at_perf = pick_dot(rown[...], pieces)
    lanes = lane_iota(128, 128)
    spread, where_to = [], []
    for h in range(2):
        c = own_t[:, h : h + 1].astype(I32)
        f = own_t[:, 2 + h : 3 + h].astype(I32)
        value = jnp.sum(
            jnp.where(lanes == rest(c, 128), at_perf[h * 128 : (h + 1) * 128, :], 0.0),
            axis=1, keepdims=True,
        ) * own_t[:, 4 + h : 5 + h]
        spread.append(split2(jnp.where(lanes == rest(f, 128), value, 0.0)))
        where_to.append(onehot(row_iota(NFR, 128) == quot(own[2 + h : 3 + h, :].astype(I32), 128)))
    part = pick_dot(jnp.concatenate(where_to, axis=1), jnp.concatenate(spread, axis=0))
    for i in range(L):
        fpart[i] = part[i * RS : (i + 1) * RS, :]
    f1[l] = fpart[l]

    pl.semaphore_wait(barrier, len(peers))
    to_layers(lambda p: fpart.at[p], f1.at[l], f1s, f1r)

    def spread_columns(i, src, dst):
        to_layers(lambda p: cols_block(src, p), dst.at[l], bts.at[i], btr.at[i])
        pltpu.make_async_copy(cols_block(src, l), dst.at[l], bto.at[i]).start()

    def columns_here(i, src, dst):
        from_layers(lambda p: dst.at[p], bts.at[i], btr.at[i])
        pltpu.make_async_copy(cols_block(src, l), dst.at[l], bto.at[i]).wait()

    has_tb, has_tn = jnp.where(t > 0, 1.0, 0.0), jnp.where(t < T - 1, 1.0, 0.0)
    has_lb, has_ln = jnp.where(l > 0, 1.0, 0.0), jnp.where(l < L - 1, 1.0, 0.0)

    def solve_inner(right):
        d = []
        for i in range(N):
            r = right[i]
            if i and d[-1] is not None:
                link = tz[i] * d[-1]
                r = link if r is None else r + link
            d.append(None if r is None else r * pivot[i])
        for i in range(N - 2, -1, -1):
            back = ratio_up[i] * d[i + 1]
            d[i] = back if d[i] is None else d[i] + back
        return d

    loads["tz"].wait()
    loads["st"].wait()
    bottom = tz[LZ - 1] * has_ln
    for i in range(N):
        below = tz[i + 1] if i < N - 1 else bottom
        dia = tz[i] + below + st[i + 1]
        if i:
            dia = dia - tz[i] * ratio_up[i - 1]
        pivot[i] = 1.0 / dia
        if i < N - 1:
            ratio_up[i] = below * pivot[i]
    a = solve_inner([tz[0]] + [None] * (N - 1))
    b = solve_inner([None] * (N - 1) + [bottom])
    for i in range(N):
        alpha[i] = a[i]
        beta[i] = b[i]
    mred[0] = tz[0] + st[0] - tz[0] * a[0]
    mred[1] = tz[0] * b[0]
    mred[2] = bottom * (1.0 - b[N - 1])

    weight = []
    for first, rows in ((1.0, alpha), (0.0, beta)):
        parts = tiles(jnp.full((CX, NY), first, F32)) + [p for i in range(N) for p in tiles(rows[i])]
        at_perf = pick_dot(rown[...], split2(jnp.concatenate(parts, axis=0)))
        for h in range(2):
            c = own_t[:, h : h + 1].astype(I32)
            weight.append(
                jnp.sum(
                    jnp.where(lanes == rest(c, 128), at_perf[h * 128 : (h + 1) * 128, :], 0.0),
                    axis=1, keepdims=True,
                ) * own_t[:, 4 + h : 5 + h]
            )
    wide = jnp.zeros((128, 128), F32)
    for i in range(4):
        wide = jnp.where(lanes == i, weight[i], wide)
    perf_own[4:8, :] = jnp.transpose(wide)[0:4, :]
    perf_buf[l] = perf_own[...]
    to_layers(lambda p: perf_own, perf_buf.at[l], pfs, pfr)
    spread_columns(0, mred, mcol)

    from_layers(lambda p: f1.at[p], f1s, f1r)
    f2[t] = add_up(f1, L)
    to_tiles(lambda p: f2.at[t], f2, f2s, f2r)
    w = solve_inner([pres[i + 1] for i in range(N)])
    rred[0] = pres[0] + tz[0] * w[0]
    rred[1] = bottom * w[N - 1]
    for h in range(2):
        c = own[h : h + 1, :].astype(I32)
        rto[:, h * 128 : (h + 1) * 128] = onehot(row_iota(RO, 128) == own_row(c))
    from_layers(lambda p: perf_buf.at[p], pfs, pfr)
    group_t = jnp.transpose(
        jnp.concatenate([perf_buf[i] for i in range(L)] + [jnp.zeros((128 - 8 * L, 128), F32)], axis=0)
    )
    for e in range(L):
        for h in range(2):
            b = (e * 2 + h) * 128
            c = group_t[:, e * 8 + h : e * 8 + h + 1].astype(I32)
            f = group_t[:, e * 8 + 2 + h : e * 8 + 3 + h].astype(I32)
            rgs[b : b + 128, :] = onehot(lane_iota(128, 8 * L) == sol_row(f))
            csol[b : b + 128, :] = jnp.where(lanes == sol_lane(f), 1.0, 0.0)
            for i in range(2):
                ccell[i, b : b + 128, :] = jnp.where(
                    lanes == rest(c, 128), group_t[:, e * 8 + 4 + 2 * i + h : e * 8 + 5 + 2 * i + h], 0.0
                )
    from_tiles(f2, f2s, f2r)
    f3[l] = add_up(f2, T)
    to_layers(lambda p: f3.at[l], f3.at[l], f3s, f3r)
    spread_columns(1, rred, rcol)
    send(tz_h.at[LZ - 1], tzp, tzs.at[0], tzr.at[0], (t, ln))
    loads["tx"].wait()
    for z in range(LZ):
        txs[z : z + 1, :] = tx[z, CX - 1 : CX, :]
    for i in range(N):
        for d, x in enumerate((CX - 1, 0)):
            asend[d, i : i + 1, :] = alpha[i, x : x + 1, :]
            asend[d, N + i : N + i + 1, :] = beta[i, x : x + 1, :]
    send(txs, txp, txps.at[0], txpr.at[0], (tn, l))
    send(asend.at[0], ahalo.at[0], ahs.at[0], ahr.at[0], (tn, l))
    send(asend.at[1], ahalo.at[1], ahs.at[1], ahr.at[1], (tb, l))
    for e in range(L):
        for h in range(2):
            row = column_row(perf_buf[e, h : h + 1, :].astype(I32)) + e * RL
            for i in range(2):
                k = (i * L * 2 + e * 2 + h) * 128
                rtg[:, k : k + 128] = onehot(row_iota(L * RL, 128) == row + i * RL)
    loads["finv"].wait()
    from_layers(lambda p: f3.at[p], f3s, f3r)

    acc = jnp.zeros((RPD, 128), F32)
    for r in range(NFR):
        acc = acc + finv[:, r * 128 : (r + 1) * 128] * f3[r // RS, r % RS : r % RS + 1, :]
    rows = lax.dot_general(
        jnp.ones((8, 128), F32), acc, (((1,), (1,)), ((), ())),
        precision=lax.Precision.HIGHEST, preferred_element_type=F32,
    )
    rows = jnp.concatenate([rows] * HALF, axis=1)
    g1[t] = jnp.where(quot(lane_iota(1, 128), RPD) == lax.rem(t, HALF), rows[0:1, :], 0.0)
    to_tiles(lambda p: g1.at[t], g1, g1s, g1r)

    columns_here(0, mred, mcol)
    for k in range(L):
        dia = mcol[k, 0] + mcol[k - 1, 2] - mcol[k - 1, 1] * gam[k - 1] if k else mcol[k, 0]
        inv[k] = 1.0 / dia
        gam[k] = mcol[k, 1] * inv[k]
        if k:
            mul[k] = mcol[k - 1, 1] * inv[k]

    from_tiles(g1, g1s, g1r)
    pairs = [sum(g1[i + j] for j in range(1, HALF)) + g1[i] for i in range(0, T, HALF)]
    pairs += [jnp.zeros((1, 128), F32)] * (8 - len(pairs))
    g2[l] = jnp.concatenate(pairs, axis=0)
    to_layers(lambda p: g2.at[l], g2.at[l], g2s, g2r)
    columns_here(1, rred, rcol)
    from_layers(lambda p: g2.at[p], g2s, g2r)

    sol = split2(jnp.concatenate([g2[i] for i in range(L)], axis=0))
    picked = pick_dot(rgs[...], sol)
    for b in range(0, L * 256, 128):
        q = jnp.sum(picked[b : b + 128, :] * csol[b : b + 128, :], axis=1, keepdims=True)
        qs[b : b + 128, 0:1] = q
        for i in range(2):
            q3[i * L * 256 + b : i * L * 256 + b + 128, :] = split2(ccell[i, b : b + 128, :] * q)
    corr[...] = pick_dot(rtg[...], q3[...])
    for k in range(L):
        r = rcol[k, 0] - untile(corr[k * RL : (k + 1) * RL, :], CX, NYL)
        d = (r + rcol[k - 1, 1]) * inv[k] + mul[k] * d if k else r * inv[k]
        ucol[k] = d
    ucol[L] = jnp.zeros((CX, NYL), F32)
    for k in range(L - 2, -1, -1):
        d = ucol[k] + gam[k] * d
        ucol[k] = d
    for e in range(L):
        for i in range(2):
            hsend[0, e, i : i + 1, :] = ucol[e + i, CX - 1 : CX, :]
            hsend[1, e, i : i + 1, :] = ucol[e + i, 0:1, :]
    to_layers(lambda p: ucol.at[pl.ds(p, 2)], cols_block(ends, l), rts, rtr)
    pltpu.make_async_copy(ucol.at[pl.ds(l, 2)], cols_block(ends, l), rto_sem.at[0]).start()
    here = pl.ds(pl.multiple_of(l * NYL, NYL), NYL)
    for i in range(L):
        e = lax.rem(l + i, L)
        send(hsend.at[0, e], phalo.at[0, :, here], hls.at[0, i], hlr.at[0, i], (tn, e))
        send(hsend.at[1, e], phalo.at[1, :, here], hls.at[1, i], hlr.at[1, i], (tb, e))

    mine = []
    for h in range(2):
        q = qs[pl.ds(pl.multiple_of(l * 256 + h * 128, 128), 128), 0:1] * own_t[:, 4 + h : 5 + h]
        c = own_t[:, h : h + 1].astype(I32)
        mine.append(split2(jnp.where(lanes == rest(c, 128), q, 0.0)))
    own_corr = pick_dot(rto[...], jnp.concatenate(mine, axis=0))
    for z in range(LZ):
        n = CX * NY // 128
        adj[z] = pres[z] - untile(own_corr[z * n : (z + 1) * n, :], CX, NY)
    w = solve_inner([adj[i + 1] for i in range(N)])
    for i in range(N):
        inner[i] = w[i]
        wsend[0, i : i + 1, :] = w[i][CX - 1 : CX, :]
        wsend[1, i : i + 1, :] = w[i][0:1, :]
    send(wsend.at[0], whalo.at[0], whs.at[0], whr.at[0], (tn, l))
    send(wsend.at[1], whalo.at[1], whs.at[1], whr.at[1], (tb, l))
    for name in ("ty", "bi", "bd"):
        loads[name].wait()
    arrived(tzp, tzs.at[0], tzr.at[0])
    arrived(txp, txps.at[0], txpr.at[0])
    for i in range(2):
        arrived(ahalo.at[i], ahs.at[i], ahr.at[i])
    start = jnp.zeros((8, 128), F32)
    for z in range(LZ):
        before = tz[z - 1] if z else tzp[...] * has_lb
        diag[z] = before + (tz[z] if z < LZ - 1 else tz[z] * has_ln) + st[z]
        for c in range(3):
            b = [bi[c, d, z] for d in range(3)]
            search[c, z] = b[0] * rhs[0, z] + b[1] * rhs[1, z] + b[2] * rhs[2, z]
            slope[c, z] = (1.0 if c == 0 else 0.0) - (
                b[0] * bd[0, 0, z] + b[1] * bd[1, 0, z] + b[2] * bd[2, 0, z]
            )
            start = start + fold(rhs[c, z] * rhs[c, z])
    for i in range(2):
        arrived(whalo.at[i], whs.at[i], whr.at[i])
    from_layers(lambda p: cols_block(ends, p), rts, rtr)
    pltpu.make_async_copy(ucol.at[pl.ds(l, 2)], cols_block(ends, l), rto_sem.at[0]).wait()
    for i in range(L):
        e = lax.rem(l + L - i, L)
        there = pl.ds(pl.multiple_of(e * NYL, NYL), NYL)
        arrived(phalo.at[0, :, there], hls.at[0, i], hlr.at[0, i])
        arrived(phalo.at[1, :, there], hls.at[1, i], hlr.at[1, i])

    sub, lane = row_iota(CX, NY), lane_iota(CX, NY)

    def from_xb(w, row):
        return jnp.where(sub == 0, row, pltpu.roll(w, 1, 0))

    def from_xn(v, row):
        return jnp.where(sub == CX - 1, row, pltpu.roll(v, CX - 1, 0))

    def from_yb(w):
        return jnp.where(lane == 0, 0.0, pltpu.roll(w, 1, 1))

    def from_yn(v):
        return jnp.where(lane == NY - 1, 0.0, pltpu.roll(v, NY - 1, 1))

    for z in [LZ - 1, 0] + list(range(1, LZ - 1)):
        p = inner[z - 1] + alpha[z - 1] * ends[0] + beta[z - 1] * ends[1] if z else ends[0]
        edge = [phalo[d, 0:1, :] for d in range(2)]
        if z:
            edge = [
                whalo[d, z - 1 : z, :]
                + ahalo[d, z - 1 : z, :] * phalo[d, 0:1, :]
                + ahalo[d, N + z - 1 : N + z, :] * phalo[d, 1:2, :]
                for d in range(2)
            ]
        near = diag[z] * p - adj[z]
        near = near + tx[z] * from_xn(p, edge[1] * has_tn)
        near = near + from_xb(tx[z] * p, txp[z : z + 1, :] * edge[0] * has_tb)
        near = near + ty[z] * from_yn(p) + from_yb(ty[z] * p)
        for c in range(3):
            v = search[c, z] + slope[c, z] * p + bi[c, 0, z] * near
            search[c, z] = v
            i = c * LZ + z
            xsend[0, i : i + 1, :] = tx[z, CX - 1 : CX, :] * v[CX - 1 : CX, :]
            xsend[1, i : i + 1, :] = v[0:1, :]
            if z == LZ - 1:
                zsend[c] = tz[z] * v
        if z == LZ - 1:
            send(zsend, zhalo.at[0], zhs.at[0], zhr.at[0], (t, ln))
        if z == 0:
            send(search.at[:, 0], zhalo.at[1], zhs.at[1], zhr.at[1], (t, lb))
    send(xsend.at[0], xhalo.at[0], xhs.at[0], xhr.at[0], (tn, l))
    send(xsend.at[1], xhalo.at[1], xhs.at[1], xhr.at[1], (tb, l))
    along = jnp.zeros((8, 128), F32)
    power = jnp.zeros((8, 128), F32)
    none = jnp.zeros((1, NY), F32)
    for z in range(LZ):
        for c in range(3):
            v = search[c, z]
            near = tx[z] * from_xn(v, none) + from_xb(tx[z] * v, none)
            near = near + ty[z] * from_yn(v) + from_yb(ty[z] * v)
            if z < LZ - 1:
                near = near + tz[z] * search[c, z + 1]
            if z:
                near = near + tz[z - 1] * search[c, z - 1]
            im = (
                bd[c, 0, z] * search[0, z] + bd[c, 1, z] * search[1, z] + bd[c, 2, z] * search[2, z]
            ) - near
            image[c, z] = im
            along = along + fold(im * rhs[c, z])
            power = power + fold(im * im)
    along, power = total(along), total(power)
    guess = jnp.where(power > 0.0, along / jnp.where(power > 0.0, power, 1.0), 0.0)

    for i in range(2):
        arrived(xhalo.at[i], xhs.at[i], xhr.at[i])
    for z in range(LZ):
        for c in range(3):
            i = c * LZ + z
            image[c, z, 0:1, :] = image[c, z, 0:1, :] - xhalo[0, i : i + 1, :] * has_tb
            image[c, z, CX - 1 : CX, :] = (
                image[c, z, CX - 1 : CX, :] - tx[z, CX - 1 : CX, :] * (xhalo[1, i : i + 1, :] * has_tn)
            )
    along = jnp.zeros((8, 128), F32)
    power = jnp.zeros((8, 128), F32)
    err = jnp.zeros((8, 128), F32)
    for z in list(range(1, LZ - 1)) + [0] + ([LZ - 1] if LZ > 1 else []):
        if z == 0:
            for i in range(2):
                arrived(zhalo.at[i], zhs.at[i], zhr.at[i])
        for c in range(3):
            im = image[c, z]
            if z == 0:
                im = im - zhalo[0, c] * has_lb
            if z == LZ - 1:
                im = im - tz[z] * (zhalo[1, c] * has_ln)
            if z in (0, LZ - 1):
                image[c, z] = im
            b = rhs[c, z]
            r = b - guess * im
            along = along + fold(im * b)
            power = power + fold(im * im)
            err = err + fold(r * r)
    along, power, start = total(along), total(power), total(start)
    tilt = along - guess * power
    row = jnp.zeros((8, 128), F32)
    lane8 = lane_iota(8, 128)
    for i, x in enumerate((guess, power, start, total(err), tilt, along)):
        row = jnp.where(lane8 == i, x, row)
    s1[l] = jnp.where(row_iota(8, 128) == l, row, 0.0)
    to_layers(lambda p: s1.at[l], s1.at[l], s1s, s1r)
    from_layers(lambda p: s1.at[p], s1s, s1r)
    s2[t] = add_up(s1, L)
    ahead = list(started)
    started.clear()
    to_tiles(lambda p: s2.at[t], s2, s2s, s2r)
    for copy in ahead:
        copy.wait_send()
    from_tiles(s2, s2s, s2r)
    allrows = jnp.concatenate([s2[i] for i in range(T)], axis=0)
    sums = jnp.sum(allrows, axis=0, keepdims=True)
    omega = sums[:, 5:6] / sums[:, 1:2]
    shift = omega - allrows[:, 0:1]
    left = allrows[:, 3:4] - 2.0 * shift * allrows[:, 4:5] + shift * shift * allrows[:, 1:2]
    left = jnp.maximum(jnp.sum(left, axis=0, keepdims=True), 0.0)
    ratio = jnp.sqrt(left / sums[:, 2:3])
    omega_o[...] = omega
    ratio_o[...] = ratio
    for copy in started:
        copy.wait_send()


def shards(rhs, wts, bd, bi, tx, ty, tz, st, cell, front, prod, finv):
    T, L = lax.axis_size("tile"), lax.axis_size("layer")
    _, LZ, CX, NY = rhs.shape
    RPD, NF = finv.shape
    NYL = NY // L
    RO, RG = LZ * CX * NY // 128, L * CX * NYL // 128
    K = L * 256
    RS = NF // 128 // L
    N = LZ - 1
    field = (LZ, CX, NY)
    colf = (CX, NYL)
    V = lambda *s: pltpu.VMEM(s, F32)
    H = lambda *s: pltpu.VMEM(s, BF16)
    D = lambda *s: pltpu.SemaphoreType.DMA(s)
    scratch = [
        V(3, *field), V(3, *field), V(3, 3, *field), V(3, 3, *field),
        V(*field), V(*field), V(*field), V(*field),
        pltpu.VMEM((2, 128), I32), pltpu.VMEM((2, 128), I32), V(2, 128), V(RPD, NF),
        V(8, 128), V(L, 8, 128), V(*field), V(L, RS, 128), V(L, RS, 128), V(T, RS, 128), V(L, RS, 128),
        V(T, 1, 128), V(L, 8, 128),
        H(256, RO), H(RO, 256), H(RG, 2 * K), H(K, 8 * L), V(K, 128), V(2, K, 128), H(2 * K, 256),
        V(K, 128),
        V(N, CX, NY), V(N, CX, NY), V(N, CX, NY), V(N, CX, NY), V(3, CX, NY), V(2, CX, NY),
        V(L, 3, *colf), V(L, 2, *colf), V(L, *colf), V(L, *colf), V(L, *colf), V(L + 1, *colf),
        V(RG, 128),
        V(CX, NY), V(8, NY), V(8, NY), V(2, 2 * N, NY), V(2, 2 * N, NY), V(2, N, NY), V(2, N, NY),
        V(2, CX, NY), V(2, L, 2, NYL), V(2, 2, NY), V(*field), V(N, CX, NY),
        V(3, *field), V(*field), V(2, 16, NY), V(2, 16, NY), V(3, CX, NY), V(2, 3, CX, NY),
        V(L, 8, 128), V(T, 8, 128),
        D(12),
        D(L - 1), D(L - 1), D(T - 1), D(T - 1), D(L - 1), D(L - 1),
        D(T - 1), D(T - 1), D(L - 1), D(L - 1), D(L - 1), D(L - 1),
        D(2, L - 1), D(2, L - 1), D(2),
        D(1), D(1), D(1), D(1), D(2), D(2), D(2), D(2), D(L - 1), D(L - 1), D(1), D(2, L), D(2, L),
        D(2), D(2), D(2), D(2),
        D(L - 1), D(L - 1), D(T - 1), D(T - 1),
    ]
    anywhere = pl.BlockSpec(memory_space=pl.ANY)
    search, image, omega, ratio = pl.pallas_call(
        functools.partial(kernel, T, L, LZ, CX, NY, NF),
        out_shape=(
            pltpu.VMEM(rhs.shape, F32),
            pltpu.VMEM(rhs.shape, F32),
            jax.ShapeDtypeStruct((1, 1), F32),
            jax.ShapeDtypeStruct((1, 1), F32),
        ),
        in_specs=[anywhere] * 12,
        out_specs=(pl.BlockSpec(memory_space=pltpu.VMEM),) * 2 + (pl.BlockSpec(memory_space=pltpu.VMEM),) * 2,
        scratch_shapes=scratch,
        compiler_params=pltpu.CompilerParams(
            collective_id=0, has_side_effects=True, vmem_limit_bytes=int(56 * 1024 * 1024)
        ),
    )(
        rhs, wts, bd, bi, tx, ty, tz, st,
        cell.reshape(2, 128), front.reshape(2, 128), prod.reshape(2, 128), finv,
    )
    omega = omega[0, 0]
    return omega * search, rhs - omega * image, ratio[0, 0]


def solution(mesh):
    return jax.shard_map(
        shards,
        mesh=mesh,
        in_specs=(
            P(None, "layer", "tile", None),
            P(None, "layer", "tile", None),
            P(None, None, "layer", "tile", None),
            P(None, None, "layer", "tile", None),
            P("layer", "tile", None),
            P("layer", "tile", None),
            P("layer", "tile", None),
            P("layer", "tile", None),
            P(("tile", "layer")),
            P(("tile", "layer")),
            P(("tile", "layer")),
            P(("tile", "layer"), None),
        ),
        out_specs=(P(None, "layer", "tile", None), P(None, "layer", "tile", None), P()),
        check_vma=False,
    )
```

```python
import functools

import jax
import jax.numpy as jnp
from jax import lax
from jax.experimental import pallas as pl
from jax.experimental.pallas import tpu as pltpu
from jax.sharding import PartitionSpec as P

MESH = pl.DeviceIdType.MESH
F32 = jnp.float32
BF16 = jnp.bfloat16
I32 = jnp.int32


def bits(n):
    assert n & (n - 1) == 0
    return n.bit_length() - 1


def quot(a, n):
    return lax.shift_right_logical(a, jnp.full_like(a, bits(n)))


def rest(a, n):
    return a & (n - 1)


def split2(x):
    hi = x.astype(BF16)
    return jnp.concatenate([hi, (x - hi.astype(F32)).astype(BF16)], axis=1)


def pick_dot(onehot, pieces):
    out = lax.dot_general(onehot, pieces, (((1,), (0,)), ((), ())), preferred_element_type=F32)
    n = out.shape[1] // 2
    return out[:, :n] + out[:, n:]


def tiles(block):
    rows, cols = block.shape
    return [
        block[i : i + 8, j : j + 128] for i in range(0, rows, 8) for j in range(0, cols, 128)
    ]


def untile(mat, rows, cols):
    per = cols // 128
    out = []
    for i in range(rows // 8):
        out.append(
            jnp.concatenate(
                [mat[(i * per + j) * 8 : (i * per + j + 1) * 8, :] for j in range(per)], axis=1
            )
        )
    return jnp.concatenate(out, axis=0)


def fold(block):
    parts = tiles(block)
    while len(parts) > 1:
        parts = [a + b for a, b in zip(parts[::2], parts[1::2])]
    return parts[0]


def total(x):
    return jnp.sum(jnp.sum(x, axis=1, keepdims=True), axis=0, keepdims=True)


def onehot(mask):
    return jnp.where(mask, 1.0, 0.0).astype(BF16)


def kernel(
    T, L, LZ, CX, NY, NF,
    rhs_h, wts_h, bd_h, bi_h, tx_h, ty_h, tz_h, st_h, cell_h, front_h, prod_h, finv_h,
    search, image, omega_o, ratio_o,
    rhs, wts, bd, bi, tx, ty, tz, st, cell, front, prod, finv,
    perf_own, perf_buf, pres, fpart, f1, f2, f3, g1, g2,
    rown, rto, rtg, rgs, csol, ccell, q3, qs,
    alpha, beta, pivot, ratio_up, mred, rred, mcol, rcol, inv, mul, gam, ucol, corr,
    tzp, txs, txp, asend, ahalo, wsend, whalo, ends, hsend, phalo, adj, inner,
    slope, diag, xsend, xhalo, zsend, zhalo, s1, s2,
    ld, snd, rcv, loc,
):
    NYL, NFR = NY // L, NF // 128
    NBL, RS, RPD = NYL // 128, NFR // L, NF // (T * L)
    N = LZ - 1
    HALF = 128 // RPD
    RL = CX * NYL // 128
    RO = LZ * CX * NY // 128
    NB = NY // 128
    t, l = lax.axis_index("tile"), lax.axis_index("layer")

    loads = {}
    order = [
        ("cell", cell_h, cell), ("front", front_h, front), ("prod", prod_h, prod),
        ("rhs", rhs_h, rhs), ("wts", wts_h, wts), ("tz", tz_h, tz), ("st", st_h, st),
        ("finv", finv_h, finv), ("tx", tx_h, tx), ("ty", ty_h, ty), ("bi", bi_h, bi), ("bd", bd_h, bd),
    ]
    for i, (name, src, dst) in enumerate(order):
        loads[name] = pltpu.make_async_copy(src, dst, ld.at[i])
        if i < 5:
            loads[name].start()

    tn, tb = lax.rem(t + 1, T), lax.rem(t + T - 1, T)
    ln, lb = lax.rem(l + 1, L), lax.rem(l + L - 1, L)
    barrier = pltpu.get_barrier_semaphore()
    peers = [(t, lax.rem(l + i, L)) for i in range(1, L)]
    peers += [(lax.rem(t + i, T), l) for i in range(1, T)]
    peers += [(a, lax.rem(l + i, L)) for a in (tn, tb) for i in range(1, L)]
    for peer in peers:
        pl.semaphore_signal(barrier, inc=1, device_id=peer, device_id_type=MESH)

    sent = {}

    def link(name, to):
        return dict(
            send_sem=snd.at[NAMES.index(name)], recv_sem=rcv.at[NAMES.index(name)],
            device_id=to, device_id_type=MESH,
        )

    def send(src, dst, name, to):
        pltpu.make_async_remote_copy(src_ref=src, dst_ref=dst, **link(name, to)).start()

    def arrived(every, name):
        sent[name] = pltpu.make_async_remote_copy(
            src_ref=every, dst_ref=every, **link(name, (t, l))
        )
        sent[name].wait_recv()

    def gone():
        for name in list(sent):
            sent.pop(name).wait_send()

    def to_tiles(src, dst, name):
        for i in range(1, T):
            peer = lax.rem(t + i, T)
            send(src(peer), dst.at[t], name, (peer, l))

    def to_layers(src, dst, name):
        for i in range(1, L):
            peer = lax.rem(l + i, L)
            send(src(peer), dst, name, (t, peer))

    def from_tiles(buf, name):
        arrived(buf.at[pl.ds(0, T - 1)], name)

    def from_layers(buf, name):
        arrived(buf.at[pl.ds(0, L - 1)], name)

    def add_up(buf, n):
        parts = [buf[i] for i in range(n)]
        while len(parts) > 1:
            parts = [a + b for a, b in zip(parts[::2], parts[1::2])]
        return parts[0]

    def cols_block(ref, i):
        return ref.at[:, :, pl.ds(pl.multiple_of(i * NYL, NYL), NYL)]

    def lane_iota(rows, cols):
        return lax.broadcasted_iota(I32, (rows, cols), 1)

    def row_iota(rows, cols):
        return lax.broadcasted_iota(I32, (rows, cols), 0)

    def own_row(c):
        z, x, y = quot(c, CX * NY), rest(quot(c, NY), CX), rest(c, NY)
        return ((z * (CX // 8) + quot(x, 8)) * NB + quot(y, 128)) * 8 + rest(x, 8)

    def column_row(c):
        x, y = rest(quot(c, NY), CX), rest(c, NY)
        row = (quot(x, 8) * NBL + quot(rest(y, NYL), 128)) * 8 + rest(x, 8)
        return jnp.where(quot(y, NYL) == l, row, -(L + 1) * RL)

    def sol_row(f):
        d = quot(f, RPD)
        return rest(d, L) * 8 + quot(quot(d, L), HALF)

    def sol_lane(f):
        return rest(quot(quot(f, RPD), L), HALF) * RPD + rest(f, RPD)

    for name in ("cell", "front", "prod"):
        loads[name].wait()
    perf_own[...] = jnp.zeros((8, 128), F32)
    perf_own[0:2, :] = cell[...].astype(F32)
    perf_own[2:4, :] = front[...].astype(F32)
    perf_own[4:6, :] = prod[...]
    own = perf_own[...]
    own_t = jnp.transpose(jnp.concatenate([own, jnp.zeros((120, 128), F32)], axis=0))
    for h in range(2):
        c = own_t[:, h : h + 1].astype(I32)
        rown[h * 128 : (h + 1) * 128, :] = onehot(lane_iota(128, RO) == own_row(c))

    loads["rhs"].wait()
    loads["wts"].wait()
    for name, _, _ in order[5:]:
        loads[name].start()
    for z in range(LZ):
        pres[z] = wts[0, z] * rhs[0, z] + wts[1, z] * rhs[1, z] + wts[2, z] * rhs[2, z]
    pieces = split2(jnp.concatenate([p for z in range(LZ) for p in tiles(pres[z])], axis=0))
    at_perf = pick_dot(rown[...], pieces)
    lanes = lane_iota(128, 128)
    spread, where_to = [], []
    for h in range(2):
        c = own_t[:, h : h + 1].astype(I32)
        f = own_t[:, 2 + h : 3 + h].astype(I32)
        value = jnp.sum(
            jnp.where(lanes == rest(c, 128), at_perf[h * 128 : (h + 1) * 128, :], 0.0),
            axis=1, keepdims=True,
        ) * own_t[:, 4 + h : 5 + h]
        spread.append(split2(jnp.where(lanes == rest(f, 128), value, 0.0)))
        where_to.append(onehot(row_iota(NFR, 128) == quot(own[2 + h : 3 + h, :].astype(I32), 128)))
    part = pick_dot(jnp.concatenate(where_to, axis=1), jnp.concatenate(spread, axis=0))
    for i in range(L):
        fpart[i] = part[i * RS : (i + 1) * RS, :]
    f1[l] = fpart[l]

    pl.semaphore_wait(barrier, len(peers))
    to_layers(lambda p: fpart.at[p], f1.at[l], "f1")

    def spread_columns(i, src, dst):
        to_layers(lambda p: cols_block(src, p), dst.at[l], f"b{i}")
        pltpu.make_async_copy(cols_block(src, l), dst.at[l], loc.at[i]).start()

    def columns_here(i, src, dst):
        from_layers(dst, f"b{i}")
        pltpu.make_async_copy(cols_block(src, l), dst.at[l], loc.at[i]).wait()

    has_tb, has_tn = jnp.where(t > 0, 1.0, 0.0), jnp.where(t < T - 1, 1.0, 0.0)
    has_lb, has_ln = jnp.where(l > 0, 1.0, 0.0), jnp.where(l < L - 1, 1.0, 0.0)

    def solve_inner(right):
        d = []
        for i in range(N):
            r = right[i]
            if i and d[-1] is not None:
                link = tz[i] * d[-1]
                r = link if r is None else r + link
            d.append(None if r is None else r * pivot[i])
        for i in range(N - 2, -1, -1):
            back = ratio_up[i] * d[i + 1]
            d[i] = back if d[i] is None else d[i] + back
        return d

    loads["tz"].wait()
    loads["st"].wait()
    bottom = tz[LZ - 1] * has_ln
    for i in range(N):
        below = tz[i + 1] if i < N - 1 else bottom
        dia = tz[i] + below + st[i + 1]
        if i:
            dia = dia - tz[i] * ratio_up[i - 1]
        pivot[i] = 1.0 / dia
        if i < N - 1:
            ratio_up[i] = below * pivot[i]
    a = solve_inner([tz[0]] + [None] * (N - 1))
    b = solve_inner([None] * (N - 1) + [bottom])
    for i in range(N):
        alpha[i] = a[i]
        beta[i] = b[i]
    mred[0] = tz[0] + st[0] - tz[0] * a[0]
    mred[1] = tz[0] * b[0]
    mred[2] = bottom * (1.0 - b[N - 1])

    weight = []
    for first, rows in ((1.0, alpha), (0.0, beta)):
        parts = tiles(jnp.full((CX, NY), first, F32)) + [p for i in range(N) for p in tiles(rows[i])]
        at_perf = pick_dot(rown[...], split2(jnp.concatenate(parts, axis=0)))
        for h in range(2):
            c = own_t[:, h : h + 1].astype(I32)
            weight.append(
                jnp.sum(
                    jnp.where(lanes == rest(c, 128), at_perf[h * 128 : (h + 1) * 128, :], 0.0),
                    axis=1, keepdims=True,
                ) * own_t[:, 4 + h : 5 + h]
            )
    wide = jnp.zeros((128, 128), F32)
    for i in range(4):
        wide = jnp.where(lanes == i, weight[i], wide)
    perf_own[4:8, :] = jnp.transpose(wide)[0:4, :]
    perf_buf[l] = perf_own[...]
    to_layers(lambda p: perf_own, perf_buf.at[l], "pf")
    spread_columns(0, mred, mcol)

    from_layers(f1, "f1")
    f2[t] = add_up(f1, L)
    to_tiles(lambda p: f2.at[t], f2, "f2")
    w = solve_inner([pres[i + 1] for i in range(N)])
    rred[0] = pres[0] + tz[0] * w[0]
    rred[1] = bottom * w[N - 1]
    for h in range(2):
        c = own[h : h + 1, :].astype(I32)
        rto[:, h * 128 : (h + 1) * 128] = onehot(row_iota(RO, 128) == own_row(c))
    from_layers(perf_buf, "pf")
    group_t = jnp.transpose(
        jnp.concatenate([perf_buf[i] for i in range(L)] + [jnp.zeros((128 - 8 * L, 128), F32)], axis=0)
    )
    for e in range(L):
        for h in range(2):
            b = (e * 2 + h) * 128
            c = group_t[:, e * 8 + h : e * 8 + h + 1].astype(I32)
            f = group_t[:, e * 8 + 2 + h : e * 8 + 3 + h].astype(I32)
            rgs[b : b + 128, :] = onehot(lane_iota(128, 8 * L) == sol_row(f))
            csol[b : b + 128, :] = jnp.where(lanes == sol_lane(f), 1.0, 0.0)
            for i in range(2):
                ccell[i, b : b + 128, :] = jnp.where(
                    lanes == rest(c, 128), group_t[:, e * 8 + 4 + 2 * i + h : e * 8 + 5 + 2 * i + h], 0.0
                )
    from_tiles(f2, "f2")
    f3[l] = add_up(f2, T)
    to_layers(lambda p: f3.at[l], f3.at[l], "f3")
    spread_columns(1, rred, rcol)
    send(tz_h.at[LZ - 1], tzp, "tz", (t, ln))
    loads["tx"].wait()
    for z in range(LZ):
        txs[z : z + 1, :] = tx[z, CX - 1 : CX, :]
    for i in range(N):
        for d, x in enumerate((CX - 1, 0)):
            asend[d, i : i + 1, :] = alpha[i, x : x + 1, :]
            asend[d, N + i : N + i + 1, :] = beta[i, x : x + 1, :]
    send(txs, txp, "tx", (tn, l))
    send(asend.at[0], ahalo.at[0], "ah", (tn, l))
    send(asend.at[1], ahalo.at[1], "ah", (tb, l))
    for e in range(L):
        for h in range(2):
            row = column_row(perf_buf[e, h : h + 1, :].astype(I32)) + e * RL
            for i in range(2):
                k = (i * L * 2 + e * 2 + h) * 128
                rtg[:, k : k + 128] = onehot(row_iota(L * RL, 128) == row + i * RL)
    loads["finv"].wait()
    from_layers(f3, "f3")

    acc = jnp.zeros((RPD, 128), F32)
    for r in range(NFR):
        acc = acc + finv[:, r * 128 : (r + 1) * 128] * f3[r // RS, r % RS : r % RS + 1, :]
    rows = lax.dot_general(
        jnp.ones((8, 128), F32), acc, (((1,), (1,)), ((), ())),
        precision=lax.Precision.HIGHEST, preferred_element_type=F32,
    )
    rows = jnp.concatenate([rows] * HALF, axis=1)
    g1[t] = jnp.where(quot(lane_iota(1, 128), RPD) == lax.rem(t, HALF), rows[0:1, :], 0.0)
    to_tiles(lambda p: g1.at[t], g1, "g1")

    columns_here(0, mred, mcol)
    for k in range(L):
        dia = mcol[k, 0] + mcol[k - 1, 2] - mcol[k - 1, 1] * gam[k - 1] if k else mcol[k, 0]
        inv[k] = 1.0 / dia
        gam[k] = mcol[k, 1] * inv[k]
        if k:
            mul[k] = mcol[k - 1, 1] * inv[k]

    from_tiles(g1, "g1")
    pairs = [sum(g1[i + j] for j in range(1, HALF)) + g1[i] for i in range(0, T, HALF)]
    pairs += [jnp.zeros((1, 128), F32)] * (8 - len(pairs))
    g2[l] = jnp.concatenate(pairs, axis=0)
    to_layers(lambda p: g2.at[l], g2.at[l], "g2")
    columns_here(1, rred, rcol)
    from_layers(g2, "g2")

    sol = split2(jnp.concatenate([g2[i] for i in range(L)], axis=0))
    picked = pick_dot(rgs[...], sol)
    for b in range(0, L * 256, 128):
        q = jnp.sum(picked[b : b + 128, :] * csol[b : b + 128, :], axis=1, keepdims=True)
        qs[b : b + 128, 0:1] = q
        for i in range(2):
            q3[i * L * 256 + b : i * L * 256 + b + 128, :] = split2(ccell[i, b : b + 128, :] * q)
    corr[...] = pick_dot(rtg[...], q3[...])
    for k in range(L):
        r = rcol[k, 0] - untile(corr[k * RL : (k + 1) * RL, :], CX, NYL)
        d = (r + rcol[k - 1, 1]) * inv[k] + mul[k] * d if k else r * inv[k]
        ucol[k] = d
    ucol[L] = jnp.zeros((CX, NYL), F32)
    for k in range(L - 2, -1, -1):
        d = ucol[k] + gam[k] * d
        ucol[k] = d
    for e in range(L):
        for i in range(2):
            hsend[0, e, i : i + 1, :] = ucol[e + i, CX - 1 : CX, :]
            hsend[1, e, i : i + 1, :] = ucol[e + i, 0:1, :]
    to_layers(lambda p: ucol.at[pl.ds(p, 2)], cols_block(ends, l), "rt")
    pltpu.make_async_copy(ucol.at[pl.ds(l, 2)], cols_block(ends, l), loc.at[2]).start()
    here = pl.ds(pl.multiple_of(l * NYL, NYL), NYL)
    for i in range(L):
        e = lax.rem(l + i, L)
        send(hsend.at[0, e], phalo.at[0, :, here], "hl", (tn, e))
        send(hsend.at[1, e], phalo.at[1, :, here], "hl", (tb, e))

    mine = []
    for h in range(2):
        q = qs[pl.ds(pl.multiple_of(l * 256 + h * 128, 128), 128), 0:1] * own_t[:, 4 + h : 5 + h]
        c = own_t[:, h : h + 1].astype(I32)
        mine.append(split2(jnp.where(lanes == rest(c, 128), q, 0.0)))
    own_corr = pick_dot(rto[...], jnp.concatenate(mine, axis=0))
    for z in range(LZ):
        n = CX * NY // 128
        adj[z] = pres[z] - untile(own_corr[z * n : (z + 1) * n, :], CX, NY)
    w = solve_inner([adj[i + 1] for i in range(N)])
    for i in range(N):
        inner[i] = w[i]
        wsend[0, i : i + 1, :] = w[i][CX - 1 : CX, :]
        wsend[1, i : i + 1, :] = w[i][0:1, :]
    send(wsend.at[0], whalo.at[0], "wh", (tn, l))
    send(wsend.at[1], whalo.at[1], "wh", (tb, l))
    for name in ("ty", "bi", "bd"):
        loads[name].wait()
    arrived(tzp, "tz")
    arrived(txp, "tx")
    arrived(ahalo, "ah")
    start = jnp.zeros((8, 128), F32)
    for z in range(LZ):
        before = tz[z - 1] if z else tzp[...] * has_lb
        diag[z] = before + (tz[z] if z < LZ - 1 else tz[z] * has_ln) + st[z]
        for c in range(3):
            b = [bi[c, d, z] for d in range(3)]
            search[c, z] = b[0] * rhs[0, z] + b[1] * rhs[1, z] + b[2] * rhs[2, z]
            slope[c, z] = (1.0 if c == 0 else 0.0) - (
                b[0] * bd[0, 0, z] + b[1] * bd[1, 0, z] + b[2] * bd[2, 0, z]
            )
            start = start + fold(rhs[c, z] * rhs[c, z])
    arrived(whalo, "wh")
    from_layers(rcol, "rt")
    pltpu.make_async_copy(ucol.at[pl.ds(l, 2)], cols_block(ends, l), loc.at[2]).wait()
    arrived(hsend, "hl")

    sub, lane = row_iota(CX, NY), lane_iota(CX, NY)

    def from_xb(w, row):
        return jnp.where(sub == 0, row, pltpu.roll(w, 1, 0))

    def from_xn(v, row):
        return jnp.where(sub == CX - 1, row, pltpu.roll(v, CX - 1, 0))

    def from_yb(w):
        return jnp.where(lane == 0, 0.0, pltpu.roll(w, 1, 1))

    def from_yn(v):
        return jnp.where(lane == NY - 1, 0.0, pltpu.roll(v, NY - 1, 1))

    for z in [LZ - 1, 0] + list(range(1, LZ - 1)):
        p = inner[z - 1] + alpha[z - 1] * ends[0] + beta[z - 1] * ends[1] if z else ends[0]
        edge = [phalo[d, 0:1, :] for d in range(2)]
        if z:
            edge = [
                whalo[d, z - 1 : z, :]
                + ahalo[d, z - 1 : z, :] * phalo[d, 0:1, :]
                + ahalo[d, N + z - 1 : N + z, :] * phalo[d, 1:2, :]
                for d in range(2)
            ]
        near = diag[z] * p - adj[z]
        near = near + tx[z] * from_xn(p, edge[1] * has_tn)
        near = near + from_xb(tx[z] * p, txp[z : z + 1, :] * edge[0] * has_tb)
        near = near + ty[z] * from_yn(p) + from_yb(ty[z] * p)
        for c in range(3):
            v = search[c, z] + slope[c, z] * p + bi[c, 0, z] * near
            search[c, z] = v
            i = c * LZ + z
            xsend[0, i : i + 1, :] = tx[z, CX - 1 : CX, :] * v[CX - 1 : CX, :]
            xsend[1, i : i + 1, :] = v[0:1, :]
            if z == LZ - 1:
                zsend[c] = tz[z] * v
        if z == LZ - 1:
            send(zsend, zhalo.at[0], "zh", (t, ln))
        if z == 0:
            send(search.at[:, 0], zhalo.at[1], "zh", (t, lb))
    send(xsend.at[0], xhalo.at[0], "xh", (tn, l))
    send(xsend.at[1], xhalo.at[1], "xh", (tb, l))
    along = jnp.zeros((8, 128), F32)
    power = jnp.zeros((8, 128), F32)
    none = jnp.zeros((1, NY), F32)
    for z in range(LZ):
        for c in range(3):
            v = search[c, z]
            near = tx[z] * from_xn(v, none) + from_xb(tx[z] * v, none)
            near = near + ty[z] * from_yn(v) + from_yb(ty[z] * v)
            if z < LZ - 1:
                near = near + tz[z] * search[c, z + 1]
            if z:
                near = near + tz[z - 1] * search[c, z - 1]
            im = (
                bd[c, 0, z] * search[0, z] + bd[c, 1, z] * search[1, z] + bd[c, 2, z] * search[2, z]
            ) - near
            image[c, z] = im
            along = along + fold(im * rhs[c, z])
            power = power + fold(im * im)
    along, power = total(along), total(power)
    guess = jnp.where(power > 0.0, along / jnp.where(power > 0.0, power, 1.0), 0.0)

    arrived(xhalo, "xh")
    for z in range(LZ):
        for c in range(3):
            i = c * LZ + z
            image[c, z, 0:1, :] = image[c, z, 0:1, :] - xhalo[0, i : i + 1, :] * has_tb
            image[c, z, CX - 1 : CX, :] = (
                image[c, z, CX - 1 : CX, :] - tx[z, CX - 1 : CX, :] * (xhalo[1, i : i + 1, :] * has_tn)
            )
    along = jnp.zeros((8, 128), F32)
    power = jnp.zeros((8, 128), F32)
    err = jnp.zeros((8, 128), F32)
    for z in list(range(1, LZ - 1)) + [0] + ([LZ - 1] if LZ > 1 else []):
        if z == 0:
            arrived(zhalo, "zh")
        for c in range(3):
            im = image[c, z]
            if z == 0:
                im = im - zhalo[0, c] * has_lb
            if z == LZ - 1:
                im = im - tz[z] * (zhalo[1, c] * has_ln)
            if z in (0, LZ - 1):
                image[c, z] = im
            b = rhs[c, z]
            r = b - guess * im
            along = along + fold(im * b)
            power = power + fold(im * im)
            err = err + fold(r * r)
    along, power, start = total(along), total(power), total(start)
    tilt = along - guess * power
    row = jnp.zeros((8, 128), F32)
    lane8 = lane_iota(8, 128)
    for i, x in enumerate((guess, power, start, total(err), tilt, along)):
        row = jnp.where(lane8 == i, x, row)
    s1[l] = jnp.where(row_iota(8, 128) == l, row, 0.0)
    to_layers(lambda p: s1.at[l], s1.at[l], "s1")
    from_layers(s1, "s1")
    s2[t] = add_up(s1, L)
    to_tiles(lambda p: s2.at[t], s2, "s2")
    gone()
    from_tiles(s2, "s2")
    allrows = jnp.concatenate([s2[i] for i in range(T)], axis=0)
    sums = jnp.sum(allrows, axis=0, keepdims=True)
    omega = sums[:, 5:6] / sums[:, 1:2]
    shift = omega - allrows[:, 0:1]
    left = allrows[:, 3:4] - 2.0 * shift * allrows[:, 4:5] + shift * shift * allrows[:, 1:2]
    left = jnp.maximum(jnp.sum(left, axis=0, keepdims=True), 0.0)
    ratio = jnp.sqrt(left / sums[:, 2:3])
    omega_o[...] = omega
    ratio_o[...] = ratio
    gone()


NAMES = "f1 f2 f3 g1 g2 pf b0 b1 tz tx ah wh rt hl xh zh s1 s2".split()


def shards(rhs, wts, bd, bi, tx, ty, tz, st, cell, front, prod, finv):
    T, L = lax.axis_size("tile"), lax.axis_size("layer")
    _, LZ, CX, NY = rhs.shape
    RPD, NF = finv.shape
    NYL = NY // L
    RO, RG = LZ * CX * NY // 128, L * CX * NYL // 128
    K = L * 256
    RS = NF // 128 // L
    N = LZ - 1
    field = (LZ, CX, NY)
    colf = (CX, NYL)
    V = lambda *s: pltpu.VMEM(s, F32)
    H = lambda *s: pltpu.VMEM(s, BF16)
    D = lambda *s: pltpu.SemaphoreType.DMA(s)
    scratch = [
        V(3, *field), V(3, *field), V(3, 3, *field), V(3, 3, *field),
        V(*field), V(*field), V(*field), V(*field),
        pltpu.VMEM((2, 128), I32), pltpu.VMEM((2, 128), I32), V(2, 128), V(RPD, NF),
        V(8, 128), V(L, 8, 128), V(*field), V(L, RS, 128), V(L, RS, 128), V(T, RS, 128), V(L, RS, 128),
        V(T, 1, 128), V(L, 8, 128),
        H(256, RO), H(RO, 256), H(RG, 2 * K), H(K, 8 * L), V(K, 128), V(2, K, 128), H(2 * K, 256),
        V(K, 128),
        V(N, CX, NY), V(N, CX, NY), V(N, CX, NY), V(N, CX, NY), V(3, CX, NY), V(2, CX, NY),
        V(L, 3, *colf), V(L, 2, *colf), V(L, *colf), V(L, *colf), V(L, *colf), V(L + 1, *colf),
        V(RG, 128),
        V(CX, NY), V(8, NY), V(8, NY), V(2, 2 * N, NY), V(2, 2 * N, NY), V(2, N, NY), V(2, N, NY),
        V(2, CX, NY), V(2, L, 2, NYL), V(2, 2, NY), V(*field), V(N, CX, NY),
        V(3, *field), V(*field), V(2, 16, NY), V(2, 16, NY), V(3, CX, NY), V(2, 3, CX, NY),
        V(L, 8, 128), V(T, 8, 128),
        D(12), D(len(NAMES)), D(len(NAMES)), D(3),
    ]
    anywhere = pl.BlockSpec(memory_space=pl.ANY)
    search, image, omega, ratio = pl.pallas_call(
        functools.partial(kernel, T, L, LZ, CX, NY, NF),
        out_shape=(
            pltpu.VMEM(rhs.shape, F32),
            pltpu.VMEM(rhs.shape, F32),
            jax.ShapeDtypeStruct((1, 1), F32),
            jax.ShapeDtypeStruct((1, 1), F32),
        ),
        in_specs=[anywhere] * 12,
        out_specs=(pl.BlockSpec(memory_space=pltpu.VMEM),) * 2 + (pl.BlockSpec(memory_space=pltpu.VMEM),) * 2,
        scratch_shapes=scratch,
        compiler_params=pltpu.CompilerParams(
            collective_id=0, has_side_effects=True, vmem_limit_bytes=int(56 * 1024 * 1024)
        ),
    )(
        rhs, wts, bd, bi, tx, ty, tz, st,
        cell.reshape(2, 128), front.reshape(2, 128), prod.reshape(2, 128), finv,
    )
    omega = omega[0, 0]
    return omega * search, rhs - omega * image, ratio[0, 0]


def solution(mesh):
    return jax.shard_map(
        shards,
        mesh=mesh,
        in_specs=(
            P(None, "layer", "tile", None),
            P(None, "layer", "tile", None),
            P(None, None, "layer", "tile", None),
            P(None, None, "layer", "tile", None),
            P("layer", "tile", None),
            P("layer", "tile", None),
            P("layer", "tile", None),
            P("layer", "tile", None),
            P(("tile", "layer")),
            P(("tile", "layer")),
            P(("tile", "layer")),
            P(("tile", "layer"), None),
        ),
        out_specs=(P(None, "layer", "tile", None), P(None, "layer", "tile", None), P()),
        check_vma=False,
    )
```

```python
import functools

import jax
import jax.numpy as jnp
from jax import lax
from jax.experimental import pallas as pl
from jax.experimental.pallas import tpu as pltpu
from jax.sharding import PartitionSpec as P

MESH = pl.DeviceIdType.MESH
F32 = jnp.float32
BF16 = jnp.bfloat16
I32 = jnp.int32


def bits(n):
    assert n & (n - 1) == 0
    return n.bit_length() - 1


def quot(a, n):
    return lax.shift_right_logical(a, jnp.full_like(a, bits(n)))


def rest(a, n):
    return a & (n - 1)


def split2(x):
    hi = x.astype(BF16)
    return jnp.concatenate([hi, (x - hi.astype(F32)).astype(BF16)], axis=1)


def pick_dot(onehot, pieces):
    out = lax.dot_general(onehot, pieces, (((1,), (0,)), ((), ())), preferred_element_type=F32)
    n = out.shape[1] // 2
    return out[:, :n] + out[:, n:]


def tiles(block):
    rows, cols = block.shape
    return [
        block[i : i + 8, j : j + 128] for i in range(0, rows, 8) for j in range(0, cols, 128)
    ]


def untile(mat, rows, cols):
    per = cols // 128
    out = []
    for i in range(rows // 8):
        out.append(
            jnp.concatenate(
                [mat[(i * per + j) * 8 : (i * per + j + 1) * 8, :] for j in range(per)], axis=1
            )
        )
    return jnp.concatenate(out, axis=0)


def fold(block):
    parts = tiles(block)
    while len(parts) > 1:
        parts = [a + b for a, b in zip(parts[::2], parts[1::2])]
    return parts[0]


def total(x):
    return jnp.sum(jnp.sum(x, axis=1, keepdims=True), axis=0, keepdims=True)


def onehot(mask):
    return jnp.where(mask, 1.0, 0.0).astype(BF16)


def kernel(
    T, L, LZ, CX, NY, NF,
    rhs_h, wts_h, bd_h, bi_h, tx_h, ty_h, tz_h, st_h, cell_h, front_h, prod_h, finv_h,
    search, image, rhs, stat_o,
    wts, bd, bi, tx, ty, tz, st, cell, front, prod, finv,
    perf_own, perf_buf, pres, fpart, f1, f2, f3, g1, g2,
    rown, rto, rtg, rgs, csol, ccell, q3, qs,
    alpha, beta, pivot, ratio_up, mred, rred, mcol, rcol, inv, mul, gam, ucol, corr,
    tzp, txs, txp, asend, ahalo, wsend, whalo, ends, hsend, phalo, adj, inner,
    slope, diag, xsend, xhalo, zsend, zhalo, s1, s2,
    ld, snd, rcv, loc,
):
    NYL, NFR = NY // L, NF // 128
    NBL, RS, RPD = NYL // 128, NFR // L, NF // (T * L)
    N = LZ - 1
    HALF = 128 // RPD
    RL = CX * NYL // 128
    RO = LZ * CX * NY // 128
    NB = NY // 128
    t, l = lax.axis_index("tile"), lax.axis_index("layer")

    loads = {}
    order = [
        ("cell", cell_h, cell), ("front", front_h, front), ("prod", prod_h, prod),
        ("rhs", rhs_h, rhs), ("wts", wts_h, wts), ("tz", tz_h, tz), ("st", st_h, st),
        ("finv", finv_h, finv), ("tx", tx_h, tx), ("ty", ty_h, ty), ("bi", bi_h, bi), ("bd", bd_h, bd),
    ]
    for i, (name, src, dst) in enumerate(order):
        loads[name] = pltpu.make_async_copy(src, dst, ld.at[i])
        if i < 5:
            loads[name].start()

    tn, tb = lax.rem(t + 1, T), lax.rem(t + T - 1, T)
    ln, lb = lax.rem(l + 1, L), lax.rem(l + L - 1, L)
    barrier = pltpu.get_barrier_semaphore()
    peers = [(t, lax.rem(l + i, L)) for i in range(1, L)]
    peers += [(lax.rem(t + i, T), l) for i in range(1, T)]
    peers += [(a, lax.rem(l + i, L)) for a in (tn, tb) for i in range(1, L)]
    for peer in peers:
        pl.semaphore_signal(barrier, inc=1, device_id=peer, device_id_type=MESH)

    sent = {}

    def link(name, to):
        return dict(
            send_sem=snd.at[NAMES.index(name)], recv_sem=rcv.at[NAMES.index(name)],
            device_id=to, device_id_type=MESH,
        )

    def send(src, dst, name, to):
        pltpu.make_async_remote_copy(src_ref=src, dst_ref=dst, **link(name, to)).start()

    def arrived(every, name):
        sent[name] = pltpu.make_async_remote_copy(
            src_ref=every, dst_ref=every, **link(name, (t, l))
        )
        sent[name].wait_recv()

    def gone():
        for name in list(sent):
            sent.pop(name).wait_send()

    def to_tiles(src, dst, name):
        for i in range(1, T):
            peer = lax.rem(t + i, T)
            send(src(peer), dst.at[t], name, (peer, l))

    def to_layers(src, dst, name):
        for i in range(1, L):
            peer = lax.rem(l + i, L)
            send(src(peer), dst, name, (t, peer))

    def from_tiles(buf, name):
        arrived(buf.at[pl.ds(0, T - 1)], name)

    def from_layers(buf, name):
        arrived(buf.at[pl.ds(0, L - 1)], name)

    def add_up(buf, n):
        parts = [buf[i] for i in range(n)]
        while len(parts) > 1:
            parts = [a + b for a, b in zip(parts[::2], parts[1::2])]
        return parts[0]

    def cols_block(ref, i):
        return ref.at[:, :, pl.ds(pl.multiple_of(i * NYL, NYL), NYL)]

    def lane_iota(rows, cols):
        return lax.broadcasted_iota(I32, (rows, cols), 1)

    def row_iota(rows, cols):
        return lax.broadcasted_iota(I32, (rows, cols), 0)

    def own_row(c):
        z, x, y = quot(c, CX * NY), rest(quot(c, NY), CX), rest(c, NY)
        return ((z * (CX // 8) + quot(x, 8)) * NB + quot(y, 128)) * 8 + rest(x, 8)

    def column_row(c):
        x, y = rest(quot(c, NY), CX), rest(c, NY)
        row = (quot(x, 8) * NBL + quot(rest(y, NYL), 128)) * 8 + rest(x, 8)
        return jnp.where(quot(y, NYL) == l, row, -(L + 1) * RL)

    def sol_row(f):
        d = quot(f, RPD)
        return rest(d, L) * 8 + quot(quot(d, L), HALF)

    def sol_lane(f):
        return rest(quot(quot(f, RPD), L), HALF) * RPD + rest(f, RPD)

    for name in ("cell", "front", "prod"):
        loads[name].wait()
    perf_own[...] = jnp.zeros((8, 128), F32)
    perf_own[0:2, :] = cell[...].astype(F32)
    perf_own[2:4, :] = front[...].astype(F32)
    perf_own[4:6, :] = prod[...]
    own = perf_own[...]
    own_t = jnp.transpose(jnp.concatenate([own, jnp.zeros((120, 128), F32)], axis=0))
    for h in range(2):
        c = own_t[:, h : h + 1].astype(I32)
        rown[h * 128 : (h + 1) * 128, :] = onehot(lane_iota(128, RO) == own_row(c))

    loads["rhs"].wait()
    loads["wts"].wait()
    for name, _, _ in order[5:]:
        loads[name].start()
    for z in range(LZ):
        pres[z] = wts[0, z] * rhs[0, z] + wts[1, z] * rhs[1, z] + wts[2, z] * rhs[2, z]
    pieces = split2(jnp.concatenate([p for z in range(LZ) for p in tiles(pres[z])], axis=0))
    at_perf = pick_dot(rown[...], pieces)
    lanes = lane_iota(128, 128)
    spread, where_to = [], []
    for h in range(2):
        c = own_t[:, h : h + 1].astype(I32)
        f = own_t[:, 2 + h : 3 + h].astype(I32)
        value = jnp.sum(
            jnp.where(lanes == rest(c, 128), at_perf[h * 128 : (h + 1) * 128, :], 0.0),
            axis=1, keepdims=True,
        ) * own_t[:, 4 + h : 5 + h]
        spread.append(split2(jnp.where(lanes == rest(f, 128), value, 0.0)))
        where_to.append(onehot(row_iota(NFR, 128) == quot(own[2 + h : 3 + h, :].astype(I32), 128)))
    part = pick_dot(jnp.concatenate(where_to, axis=1), jnp.concatenate(spread, axis=0))
    for i in range(L):
        fpart[i] = part[i * RS : (i + 1) * RS, :]
    f1[l] = fpart[l]

    pl.semaphore_wait(barrier, len(peers))
    to_layers(lambda p: fpart.at[p], f1.at[l], "f1")

    def spread_columns(i, src, dst):
        to_layers(lambda p: cols_block(src, p), dst.at[l], f"b{i}")
        pltpu.make_async_copy(cols_block(src, l), dst.at[l], loc.at[i]).start()

    def columns_here(i, src, dst):
        from_layers(dst, f"b{i}")
        pltpu.make_async_copy(cols_block(src, l), dst.at[l], loc.at[i]).wait()

    has_tb, has_tn = jnp.where(t > 0, 1.0, 0.0), jnp.where(t < T - 1, 1.0, 0.0)
    has_lb, has_ln = jnp.where(l > 0, 1.0, 0.0), jnp.where(l < L - 1, 1.0, 0.0)

    def solve_inner(right):
        d = []
        for i in range(N):
            r = right[i]
            if i and d[-1] is not None:
                link = tz[i] * d[-1]
                r = link if r is None else r + link
            d.append(None if r is None else r * pivot[i])
        for i in range(N - 2, -1, -1):
            back = ratio_up[i] * d[i + 1]
            d[i] = back if d[i] is None else d[i] + back
        return d

    loads["tz"].wait()
    loads["st"].wait()
    bottom = tz[LZ - 1] * has_ln
    for i in range(N):
        below = tz[i + 1] if i < N - 1 else bottom
        dia = tz[i] + below + st[i + 1]
        if i:
            dia = dia - tz[i] * ratio_up[i - 1]
        pivot[i] = 1.0 / dia
        if i < N - 1:
            ratio_up[i] = below * pivot[i]
    a = solve_inner([tz[0]] + [None] * (N - 1))
    b = solve_inner([None] * (N - 1) + [bottom])
    for i in range(N):
        alpha[i] = a[i]
        beta[i] = b[i]
    mred[0] = tz[0] + st[0] - tz[0] * a[0]
    mred[1] = tz[0] * b[0]
    mred[2] = bottom * (1.0 - b[N - 1])

    weight = []
    for first, rows in ((1.0, alpha), (0.0, beta)):
        parts = tiles(jnp.full((CX, NY), first, F32)) + [p for i in range(N) for p in tiles(rows[i])]
        at_perf = pick_dot(rown[...], split2(jnp.concatenate(parts, axis=0)))
        for h in range(2):
            c = own_t[:, h : h + 1].astype(I32)
            weight.append(
                jnp.sum(
                    jnp.where(lanes == rest(c, 128), at_perf[h * 128 : (h + 1) * 128, :], 0.0),
                    axis=1, keepdims=True,
                ) * own_t[:, 4 + h : 5 + h]
            )
    wide = jnp.zeros((128, 128), F32)
    for i in range(4):
        wide = jnp.where(lanes == i, weight[i], wide)
    perf_own[4:8, :] = jnp.transpose(wide)[0:4, :]
    perf_buf[l] = perf_own[...]
    to_layers(lambda p: perf_own, perf_buf.at[l], "pf")
    spread_columns(0, mred, mcol)

    from_layers(f1, "f1")
    f2[t] = add_up(f1, L)
    to_tiles(lambda p: f2.at[t], f2, "f2")
    w = solve_inner([pres[i + 1] for i in range(N)])
    rred[0] = pres[0] + tz[0] * w[0]
    rred[1] = bottom * w[N - 1]
    for h in range(2):
        c = own[h : h + 1, :].astype(I32)
        rto[:, h * 128 : (h + 1) * 128] = onehot(row_iota(RO, 128) == own_row(c))
    from_layers(perf_buf, "pf")
    group_t = jnp.transpose(
        jnp.concatenate([perf_buf[i] for i in range(L)] + [jnp.zeros((128 - 8 * L, 128), F32)], axis=0)
    )
    for e in range(L):
        for h in range(2):
            b = (e * 2 + h) * 128
            c = group_t[:, e * 8 + h : e * 8 + h + 1].astype(I32)
            f = group_t[:, e * 8 + 2 + h : e * 8 + 3 + h].astype(I32)
            rgs[b : b + 128, :] = onehot(lane_iota(128, 8 * L) == sol_row(f))
            csol[b : b + 128, :] = jnp.where(lanes == sol_lane(f), 1.0, 0.0)
            for i in range(2):
                ccell[i, b : b + 128, :] = jnp.where(
                    lanes == rest(c, 128), group_t[:, e * 8 + 4 + 2 * i + h : e * 8 + 5 + 2 * i + h], 0.0
                )
    from_tiles(f2, "f2")
    f3[l] = add_up(f2, T)
    to_layers(lambda p: f3.at[l], f3.at[l], "f3")
    spread_columns(1, rred, rcol)
    send(tz_h.at[LZ - 1], tzp, "tz", (t, ln))
    loads["tx"].wait()
    for z in range(LZ):
        txs[z : z + 1, :] = tx[z, CX - 1 : CX, :]
    for i in range(N):
        for d, x in enumerate((CX - 1, 0)):
            asend[d, i : i + 1, :] = alpha[i, x : x + 1, :]
            asend[d, N + i : N + i + 1, :] = beta[i, x : x + 1, :]
    send(txs, txp, "tx", (tn, l))
    send(asend.at[0], ahalo.at[0], "ah", (tn, l))
    send(asend.at[1], ahalo.at[1], "ah", (tb, l))
    for e in range(L):
        for h in range(2):
            row = column_row(perf_buf[e, h : h + 1, :].astype(I32)) + e * RL
            for i in range(2):
                k = (i * L * 2 + e * 2 + h) * 128
                rtg[:, k : k + 128] = onehot(row_iota(L * RL, 128) == row + i * RL)
    loads["finv"].wait()
    from_layers(f3, "f3")

    acc = jnp.zeros((RPD, 128), F32)
    for r in range(NFR):
        acc = acc + finv[:, r * 128 : (r + 1) * 128] * f3[r // RS, r % RS : r % RS + 1, :]
    rows = lax.dot_general(
        jnp.ones((8, 128), F32), acc, (((1,), (1,)), ((), ())),
        precision=lax.Precision.HIGHEST, preferred_element_type=F32,
    )
    rows = jnp.concatenate([rows] * HALF, axis=1)
    g1[t] = jnp.where(quot(lane_iota(1, 128), RPD) == lax.rem(t, HALF), rows[0:1, :], 0.0)
    to_tiles(lambda p: g1.at[t], g1, "g1")

    columns_here(0, mred, mcol)
    for k in range(L):
        dia = mcol[k, 0] + mcol[k - 1, 2] - mcol[k - 1, 1] * gam[k - 1] if k else mcol[k, 0]
        inv[k] = 1.0 / dia
        gam[k] = mcol[k, 1] * inv[k]
        if k:
            mul[k] = mcol[k - 1, 1] * inv[k]

    from_tiles(g1, "g1")
    pairs = [sum(g1[i + j] for j in range(1, HALF)) + g1[i] for i in range(0, T, HALF)]
    pairs += [jnp.zeros((1, 128), F32)] * (8 - len(pairs))
    g2[l] = jnp.concatenate(pairs, axis=0)
    to_layers(lambda p: g2.at[l], g2.at[l], "g2")
    columns_here(1, rred, rcol)
    from_layers(g2, "g2")

    sol = split2(jnp.concatenate([g2[i] for i in range(L)], axis=0))
    picked = pick_dot(rgs[...], sol)
    for b in range(0, L * 256, 128):
        q = jnp.sum(picked[b : b + 128, :] * csol[b : b + 128, :], axis=1, keepdims=True)
        qs[b : b + 128, 0:1] = q
        for i in range(2):
            q3[i * L * 256 + b : i * L * 256 + b + 128, :] = split2(ccell[i, b : b + 128, :] * q)
    corr[...] = pick_dot(rtg[...], q3[...])
    for k in range(L):
        r = rcol[k, 0] - untile(corr[k * RL : (k + 1) * RL, :], CX, NYL)
        d = (r + rcol[k - 1, 1]) * inv[k] + mul[k] * d if k else r * inv[k]
        ucol[k] = d
    ucol[L] = jnp.zeros((CX, NYL), F32)
    for k in range(L - 2, -1, -1):
        d = ucol[k] + gam[k] * d
        ucol[k] = d
    for e in range(L):
        for i in range(2):
            hsend[0, e, i : i + 1, :] = ucol[e + i, CX - 1 : CX, :]
            hsend[1, e, i : i + 1, :] = ucol[e + i, 0:1, :]
    to_layers(lambda p: ucol.at[pl.ds(p, 2)], cols_block(ends, l), "rt")
    pltpu.make_async_copy(ucol.at[pl.ds(l, 2)], cols_block(ends, l), loc.at[2]).start()
    here = pl.ds(pl.multiple_of(l * NYL, NYL), NYL)
    for i in range(L):
        e = lax.rem(l + i, L)
        send(hsend.at[0, e], phalo.at[0, :, here], "hl", (tn, e))
        send(hsend.at[1, e], phalo.at[1, :, here], "hl", (tb, e))

    mine = []
    for h in range(2):
        q = qs[pl.ds(pl.multiple_of(l * 256 + h * 128, 128), 128), 0:1] * own_t[:, 4 + h : 5 + h]
        c = own_t[:, h : h + 1].astype(I32)
        mine.append(split2(jnp.where(lanes == rest(c, 128), q, 0.0)))
    own_corr = pick_dot(rto[...], jnp.concatenate(mine, axis=0))
    for z in range(LZ):
        n = CX * NY // 128
        adj[z] = pres[z] - untile(own_corr[z * n : (z + 1) * n, :], CX, NY)
    w = solve_inner([adj[i + 1] for i in range(N)])
    for i in range(N):
        inner[i] = w[i]
        wsend[0, i : i + 1, :] = w[i][CX - 1 : CX, :]
        wsend[1, i : i + 1, :] = w[i][0:1, :]
    send(wsend.at[0], whalo.at[0], "wh", (tn, l))
    send(wsend.at[1], whalo.at[1], "wh", (tb, l))
    for name in ("ty", "bi", "bd"):
        loads[name].wait()
    arrived(tzp, "tz")
    arrived(txp, "tx")
    arrived(ahalo, "ah")
    start = jnp.zeros((8, 128), F32)
    for z in range(LZ):
        before = tz[z - 1] if z else tzp[...] * has_lb
        diag[z] = before + (tz[z] if z < LZ - 1 else tz[z] * has_ln) + st[z]
        for c in range(3):
            b = [bi[c, d, z] for d in range(3)]
            search[c, z] = b[0] * rhs[0, z] + b[1] * rhs[1, z] + b[2] * rhs[2, z]
            slope[c, z] = (1.0 if c == 0 else 0.0) - (
                b[0] * bd[0, 0, z] + b[1] * bd[1, 0, z] + b[2] * bd[2, 0, z]
            )
            start = start + fold(rhs[c, z] * rhs[c, z])
    arrived(whalo, "wh")
    from_layers(rcol, "rt")
    pltpu.make_async_copy(ucol.at[pl.ds(l, 2)], cols_block(ends, l), loc.at[2]).wait()
    arrived(hsend, "hl")

    sub, lane = row_iota(CX, NY), lane_iota(CX, NY)

    def from_xb(w, row):
        return jnp.where(sub == 0, row, pltpu.roll(w, 1, 0))

    def from_xn(v, row):
        return jnp.where(sub == CX - 1, row, pltpu.roll(v, CX - 1, 0))

    def from_yb(w):
        return jnp.where(lane == 0, 0.0, pltpu.roll(w, 1, 1))

    def from_yn(v):
        return jnp.where(lane == NY - 1, 0.0, pltpu.roll(v, NY - 1, 1))

    for z in [LZ - 1, 0] + list(range(1, LZ - 1)):
        p = inner[z - 1] + alpha[z - 1] * ends[0] + beta[z - 1] * ends[1] if z else ends[0]
        edge = [phalo[d, 0:1, :] for d in range(2)]
        if z:
            edge = [
                whalo[d, z - 1 : z, :]
                + ahalo[d, z - 1 : z, :] * phalo[d, 0:1, :]
                + ahalo[d, N + z - 1 : N + z, :] * phalo[d, 1:2, :]
                for d in range(2)
            ]
        near = diag[z] * p - adj[z]
        near = near + tx[z] * from_xn(p, edge[1] * has_tn)
        near = near + from_xb(tx[z] * p, txp[z : z + 1, :] * edge[0] * has_tb)
        near = near + ty[z] * from_yn(p) + from_yb(ty[z] * p)
        for c in range(3):
            v = search[c, z] + slope[c, z] * p + bi[c, 0, z] * near
            search[c, z] = v
            i = c * LZ + z
            xsend[0, i : i + 1, :] = tx[z, CX - 1 : CX, :] * v[CX - 1 : CX, :]
            xsend[1, i : i + 1, :] = v[0:1, :]
            if z == LZ - 1:
                zsend[c] = tz[z] * v
        if z == LZ - 1:
            send(zsend, zhalo.at[0], "zh", (t, ln))
        if z == 0:
            send(search.at[:, 0], zhalo.at[1], "zh", (t, lb))
    send(xsend.at[0], xhalo.at[0], "xh", (tn, l))
    send(xsend.at[1], xhalo.at[1], "xh", (tb, l))
    along = jnp.zeros((8, 128), F32)
    power = jnp.zeros((8, 128), F32)
    none = jnp.zeros((1, NY), F32)
    for z in range(LZ):
        for c in range(3):
            v = search[c, z]
            near = tx[z] * from_xn(v, none) + from_xb(tx[z] * v, none)
            near = near + ty[z] * from_yn(v) + from_yb(ty[z] * v)
            if z < LZ - 1:
                near = near + tz[z] * search[c, z + 1]
            if z:
                near = near + tz[z - 1] * search[c, z - 1]
            im = (
                bd[c, 0, z] * search[0, z] + bd[c, 1, z] * search[1, z] + bd[c, 2, z] * search[2, z]
            ) - near
            image[c, z] = im
            along = along + fold(im * rhs[c, z])
            power = power + fold(im * im)
    along, power = total(along), total(power)
    guess = jnp.where(power > 0.0, along / jnp.where(power > 0.0, power, 1.0), 0.0)

    arrived(xhalo, "xh")
    for z in range(LZ):
        for c in range(3):
            i = c * LZ + z
            image[c, z, 0:1, :] = image[c, z, 0:1, :] - xhalo[0, i : i + 1, :] * has_tb
            image[c, z, CX - 1 : CX, :] = (
                image[c, z, CX - 1 : CX, :] - tx[z, CX - 1 : CX, :] * (xhalo[1, i : i + 1, :] * has_tn)
            )
    along = jnp.zeros((8, 128), F32)
    power = jnp.zeros((8, 128), F32)
    err = jnp.zeros((8, 128), F32)
    for z in list(range(1, LZ - 1)) + [0] + ([LZ - 1] if LZ > 1 else []):
        if z == 0:
            arrived(zhalo, "zh")
        for c in range(3):
            im = image[c, z]
            if z == 0:
                im = im - zhalo[0, c] * has_lb
            if z == LZ - 1:
                im = im - tz[z] * (zhalo[1, c] * has_ln)
            if z in (0, LZ - 1):
                image[c, z] = im
            b = rhs[c, z]
            r = b - guess * im
            along = along + fold(im * b)
            power = power + fold(im * im)
            err = err + fold(r * r)
    along, power, start = total(along), total(power), total(start)
    tilt = along - guess * power
    row = jnp.zeros((8, 128), F32)
    lane8 = lane_iota(8, 128)
    for i, x in enumerate((guess, power, start, total(err), tilt, along)):
        row = jnp.where(lane8 == i, x, row)
    s1[l] = jnp.where(row_iota(8, 128) == l, row, 0.0)
    to_layers(lambda p: s1.at[l], s1.at[l], "s1")
    from_layers(s1, "s1")
    s2[t] = add_up(s1, L)
    to_tiles(lambda p: s2.at[t], s2, "s2")
    gone()
    from_tiles(s2, "s2")
    allrows = jnp.concatenate([s2[i] for i in range(T)], axis=0)
    sums = jnp.sum(allrows, axis=0, keepdims=True)
    omega = sums[:, 5:6] / sums[:, 1:2]
    shift = omega - allrows[:, 0:1]
    left = allrows[:, 3:4] - 2.0 * shift * allrows[:, 4:5] + shift * shift * allrows[:, 1:2]
    left = jnp.maximum(jnp.sum(left, axis=0, keepdims=True), 0.0)
    ratio = jnp.sqrt(left / sums[:, 2:3])
    stat_o[...] = jnp.where(lane8 == 0, omega, ratio)
    gone()


NAMES = (
    "f1", "f2", "f3", "g1", "g2", "pf", "b0", "b1", "tz", "tx", "ah", "wh", "rt", "hl", "xh",
    "zh", "s1", "s2",
)


def scale(stat, search, image, rhs, update_o, lin_res_o, ratio_o, update, lin_res, sems):
    factor = stat[0:1, 0:1]
    ratio_o[...] = stat[0:1, 1:2]
    writes = []
    for c in range(3):
        for i, (out, src) in enumerate(((update_o, update), (lin_res_o, lin_res))):
            for z in range(rhs.shape[1]):
                if i:
                    src[c, z] = rhs[c, z] - factor * image[c, z]
                else:
                    src[c, z] = factor * search[c, z]
            writes.append(pltpu.make_async_copy(src.at[c], out.at[c], sems.at[i, c]))
            writes[-1].start()
    for write in writes:
        write.wait()


def shards(rhs, wts, bd, bi, tx, ty, tz, st, cell, front, prod, finv):
    T, L = lax.axis_size("tile"), lax.axis_size("layer")
    _, LZ, CX, NY = rhs.shape
    RPD, NF = finv.shape
    NYL = NY // L
    RO, RG = LZ * CX * NY // 128, L * CX * NYL // 128
    K = L * 256
    RS = NF // 128 // L
    N = LZ - 1
    field = (LZ, CX, NY)
    colf = (CX, NYL)
    V = lambda *s: pltpu.VMEM(s, F32)
    H = lambda *s: pltpu.VMEM(s, BF16)
    D = lambda *s: pltpu.SemaphoreType.DMA(s)
    scratch = [
        V(3, *field), V(3, 3, *field), V(3, 3, *field),
        V(*field), V(*field), V(*field), V(*field),
        pltpu.VMEM((2, 128), I32), pltpu.VMEM((2, 128), I32), V(2, 128), V(RPD, NF),
        V(8, 128), V(L, 8, 128), V(*field), V(L, RS, 128), V(L, RS, 128), V(T, RS, 128), V(L, RS, 128),
        V(T, 1, 128), V(L, 8, 128),
        H(256, RO), H(RO, 256), H(RG, 2 * K), H(K, 8 * L), V(K, 128), V(2, K, 128), H(2 * K, 256),
        V(K, 128),
        V(N, CX, NY), V(N, CX, NY), V(N, CX, NY), V(N, CX, NY), V(3, CX, NY), V(2, CX, NY),
        V(L, 3, *colf), V(L, 2, *colf), V(L, *colf), V(L, *colf), V(L, *colf), V(L + 1, *colf),
        V(RG, 128),
        V(CX, NY), V(8, NY), V(8, NY), V(2, 2 * N, NY), V(2, 2 * N, NY), V(2, N, NY), V(2, N, NY),
        V(2, CX, NY), V(2, L, 2, NYL), V(2, 2, NY), V(*field), V(N, CX, NY),
        V(3, *field), V(*field), V(2, 16, NY), V(2, 16, NY), V(3, CX, NY), V(2, 3, CX, NY),
        V(L, 8, 128), V(T, 8, 128),
        D(12), D(len(NAMES)), D(len(NAMES)), D(3),
    ]
    anywhere = pl.BlockSpec(memory_space=pl.ANY)
    search, image, kept, stat = pl.pallas_call(
        functools.partial(kernel, T, L, LZ, CX, NY, NF),
        out_shape=(
            pltpu.VMEM(rhs.shape, F32),
            pltpu.VMEM(rhs.shape, F32),
            pltpu.VMEM(rhs.shape, F32),
            pltpu.VMEM((8, 128), F32),
        ),
        in_specs=[anywhere] * 12,
        out_specs=(pl.BlockSpec(memory_space=pltpu.VMEM),) * 4,
        scratch_shapes=scratch,
        compiler_params=pltpu.CompilerParams(
            collective_id=0, has_side_effects=True, vmem_limit_bytes=int(56 * 1024 * 1024)
        ),
    )(
        rhs, wts, bd, bi, tx, ty, tz, st,
        cell.reshape(2, 128), front.reshape(2, 128), prod.reshape(2, 128), finv,
    )
    here = pl.BlockSpec(memory_space=pltpu.VMEM)
    update, lin_res, ratio = pl.pallas_call(
        scale,
        out_shape=(jax.ShapeDtypeStruct(rhs.shape, F32),) * 2 + (jax.ShapeDtypeStruct((1, 1), F32),),
        in_specs=[here] * 4,
        out_specs=(anywhere, anywhere, here),
        scratch_shapes=[V(3, *field), V(3, *field), D(2, 3)],
        compiler_params=pltpu.CompilerParams(vmem_limit_bytes=4 * 1024 * 1024),
    )(stat, search, image, kept)
    return update, lin_res, ratio[0, 0]


def solution(mesh):
    return jax.shard_map(
        shards,
        mesh=mesh,
        in_specs=(
            P(None, "layer", "tile", None),
            P(None, "layer", "tile", None),
            P(None, None, "layer", "tile", None),
            P(None, None, "layer", "tile", None),
            P("layer", "tile", None),
            P("layer", "tile", None),
            P("layer", "tile", None),
            P("layer", "tile", None),
            P(("tile", "layer")),
            P(("tile", "layer")),
            P(("tile", "layer")),
            P(("tile", "layer"), None),
        ),
        out_specs=(P(None, "layer", "tile", None), P(None, "layer", "tile", None), P()),
        check_vma=False,
    )
```

```python
import functools

import jax
import jax.numpy as jnp
from jax import lax
from jax.experimental import pallas as pl
from jax.experimental.pallas import tpu as pltpu
from jax.sharding import PartitionSpec as P

MESH = pl.DeviceIdType.MESH
F32 = jnp.float32
BF16 = jnp.bfloat16
I32 = jnp.int32


def bits(n):
    assert n & (n - 1) == 0
    return n.bit_length() - 1


def quot(a, n):
    return lax.shift_right_logical(a, jnp.full_like(a, bits(n)))


def rest(a, n):
    return a & (n - 1)


def split2(x):
    hi = x.astype(BF16)
    return jnp.concatenate([hi, (x - hi.astype(F32)).astype(BF16)], axis=1)


def pick_dot(onehot, pieces):
    out = lax.dot_general(onehot, pieces, (((1,), (0,)), ((), ())), preferred_element_type=F32)
    n = out.shape[1] // 2
    return out[:, :n] + out[:, n:]


def tiles(block):
    rows, cols = block.shape
    return [
        block[i : i + 8, j : j + 128] for i in range(0, rows, 8) for j in range(0, cols, 128)
    ]


def untile(mat, rows, cols):
    per = cols // 128
    out = []
    for i in range(rows // 8):
        out.append(
            jnp.concatenate(
                [mat[(i * per + j) * 8 : (i * per + j + 1) * 8, :] for j in range(per)], axis=1
            )
        )
    return jnp.concatenate(out, axis=0)


def fold(block):
    parts = tiles(block)
    while len(parts) > 1:
        parts = [a + b for a, b in zip(parts[::2], parts[1::2])]
    return parts[0]


def total(x):
    return jnp.sum(jnp.sum(x, axis=1, keepdims=True), axis=0, keepdims=True)


def onehot(mask):
    return jnp.where(mask, 1.0, 0.0).astype(BF16)


def kernel(
    T, L, LZ, CX, NY, NF,
    rhs_h, wts_h, bd_h, bi_h, tx_h, ty_h, tz_h, st_h, cell_h, front_h, prod_h, finv_h,
    search, image, rhs, stat_o,
    wts, bd, bi, tx, ty, tz, st, cell, front, prod, finv,
    perf_own, perf_buf, pres, fpart, f1, f2, f3, g1, g2,
    rown, rto, rtg, rgs, csol, ccell, q3, qs,
    alpha, beta, pivot, ratio_up, mred, rred, mcol, rcol, inv, mul, gam, ucol, corr,
    tzp, txs, txp, asend, ahalo, wsend, whalo, ends, hsend, phalo, adj, inner,
    slope, diag, xsend, xhalo, zsend, zhalo, s1, s2,
    ld, snd, rcv, loc,
):
    NYL, NFR = NY // L, NF // 128
    NBL, RS, RPD = NYL // 128, NFR // L, NF // (T * L)
    N = LZ - 1
    HALF = 128 // RPD
    RL = CX * NYL // 128
    RO = LZ * CX * NY // 128
    NB = NY // 128
    t, l = lax.axis_index("tile"), lax.axis_index("layer")

    loads = {}
    order = [
        ("cell", cell_h, cell), ("front", front_h, front), ("prod", prod_h, prod),
        ("rhs", rhs_h, rhs), ("wts", wts_h, wts), ("tz", tz_h, tz), ("st", st_h, st),
        ("finv", finv_h, finv), ("tx", tx_h, tx), ("ty", ty_h, ty), ("bi", bi_h, bi), ("bd", bd_h, bd),
    ]
    for i, (name, src, dst) in enumerate(order):
        loads[name] = pltpu.make_async_copy(src, dst, ld.at[i])
        if i < 5:
            loads[name].start()

    tn, tb = lax.rem(t + 1, T), lax.rem(t + T - 1, T)
    ln, lb = lax.rem(l + 1, L), lax.rem(l + L - 1, L)
    barrier = pltpu.get_barrier_semaphore()
    peers = [(lax.rem(t + i, T), l) for i in range(1, T)]
    peers += [(t, lax.rem(l + i, L)) for i in range(1, L)]
    peers += [(a, lax.rem(l + i, L)) for a in (tn, tb) for i in range(1, L)]
    for peer in peers:
        pl.semaphore_signal(barrier, inc=1, device_id=peer, device_id_type=MESH)

    sent = {}
    by_layer, by_tile = far_first(L, L), far_first(T, min(T, 4))

    def link(name, to):
        return dict(
            send_sem=snd.at[NAMES.index(name)], recv_sem=rcv.at[NAMES.index(name)],
            device_id=to, device_id_type=MESH,
        )

    def send(src, dst, name, to):
        pltpu.make_async_remote_copy(src_ref=src, dst_ref=dst, **link(name, to)).start()

    def arrived(every, name):
        sent[name] = pltpu.make_async_remote_copy(
            src_ref=every, dst_ref=every, **link(name, (t, l))
        )
        sent[name].wait_recv()

    def gone():
        for name in list(sent):
            sent.pop(name).wait_send()

    def to_tiles(src, dst, name):
        for i in by_tile[:-1]:
            peer = lax.rem(t + i, T)
            send(src(peer), dst.at[t], name, (peer, l))

    def to_layers(src, dst, name):
        for i in by_layer[:-1]:
            peer = lax.rem(l + i, L)
            send(src(peer), dst, name, (t, peer))

    def from_tiles(buf, name):
        arrived(buf.at[pl.ds(0, T - 1)], name)

    def from_layers(buf, name):
        arrived(buf.at[pl.ds(0, L - 1)], name)

    def add_up(buf, n):
        parts = [buf[i] for i in range(n)]
        while len(parts) > 1:
            parts = [a + b for a, b in zip(parts[::2], parts[1::2])]
        return parts[0]

    def cols_block(ref, i):
        return ref.at[:, :, pl.ds(pl.multiple_of(i * NYL, NYL), NYL)]

    def lane_iota(rows, cols):
        return lax.broadcasted_iota(I32, (rows, cols), 1)

    def row_iota(rows, cols):
        return lax.broadcasted_iota(I32, (rows, cols), 0)

    def own_row(c):
        z, x, y = quot(c, CX * NY), rest(quot(c, NY), CX), rest(c, NY)
        return ((z * (CX // 8) + quot(x, 8)) * NB + quot(y, 128)) * 8 + rest(x, 8)

    def column_row(c):
        x, y = rest(quot(c, NY), CX), rest(c, NY)
        row = (quot(x, 8) * NBL + quot(rest(y, NYL), 128)) * 8 + rest(x, 8)
        return jnp.where(quot(y, NYL) == l, row, -(L + 1) * RL)

    def sol_row(f):
        d = quot(f, RPD)
        return rest(d, L) * 8 + quot(quot(d, L), HALF)

    def sol_lane(f):
        return rest(quot(quot(f, RPD), L), HALF) * RPD + rest(f, RPD)

    for name in ("cell", "front", "prod"):
        loads[name].wait()
    perf_own[...] = jnp.zeros((8, 128), F32)
    perf_own[0:2, :] = cell[...].astype(F32)
    perf_own[2:4, :] = front[...].astype(F32)
    perf_own[4:6, :] = prod[...]
    own = perf_own[...]
    own_t = jnp.transpose(jnp.concatenate([own, jnp.zeros((120, 128), F32)], axis=0))
    for h in range(2):
        c = own_t[:, h : h + 1].astype(I32)
        rown[h * 128 : (h + 1) * 128, :] = onehot(lane_iota(128, RO) == own_row(c))

    loads["rhs"].wait()
    loads["wts"].wait()
    for name, _, _ in order[5:]:
        loads[name].start()
    for z in range(LZ):
        pres[z] = wts[0, z] * rhs[0, z] + wts[1, z] * rhs[1, z] + wts[2, z] * rhs[2, z]
    pieces = split2(jnp.concatenate([p for z in range(LZ) for p in tiles(pres[z])], axis=0))
    at_perf = pick_dot(rown[...], pieces)
    lanes = lane_iota(128, 128)
    spread, where_to = [], []
    for h in range(2):
        c = own_t[:, h : h + 1].astype(I32)
        f = own_t[:, 2 + h : 3 + h].astype(I32)
        value = jnp.sum(
            jnp.where(lanes == rest(c, 128), at_perf[h * 128 : (h + 1) * 128, :], 0.0),
            axis=1, keepdims=True,
        ) * own_t[:, 4 + h : 5 + h]
        spread.append(split2(jnp.where(lanes == rest(f, 128), value, 0.0)))
        where_to.append(onehot(row_iota(NFR, 128) == quot(own[2 + h : 3 + h, :].astype(I32), 128)))
    part = pick_dot(jnp.concatenate(where_to, axis=1), jnp.concatenate(spread, axis=0))
    for i in range(L):
        fpart[i] = part[i * RS : (i + 1) * RS, :]
    f1[l] = fpart[l]

    pl.semaphore_wait(barrier, len(peers))
    to_layers(lambda p: fpart.at[p], f1.at[l], "f1")

    def spread_columns(i, src, dst):
        to_layers(lambda p: cols_block(src, p), dst.at[l], f"b{i}")
        pltpu.make_async_copy(cols_block(src, l), dst.at[l], loc.at[i]).start()

    def columns_here(i, src, dst):
        from_layers(dst, f"b{i}")
        pltpu.make_async_copy(cols_block(src, l), dst.at[l], loc.at[i]).wait()

    has_tb, has_tn = jnp.where(t > 0, 1.0, 0.0), jnp.where(t < T - 1, 1.0, 0.0)
    has_lb, has_ln = jnp.where(l > 0, 1.0, 0.0), jnp.where(l < L - 1, 1.0, 0.0)

    def solve_inner(right):
        d = []
        for i in range(N):
            r = right[i]
            if i and d[-1] is not None:
                link = tz[i] * d[-1]
                r = link if r is None else r + link
            d.append(None if r is None else r * pivot[i])
        for i in range(N - 2, -1, -1):
            back = ratio_up[i] * d[i + 1]
            d[i] = back if d[i] is None else d[i] + back
        return d

    loads["tz"].wait()
    loads["st"].wait()
    bottom = tz[LZ - 1] * has_ln
    for i in range(N):
        below = tz[i + 1] if i < N - 1 else bottom
        dia = tz[i] + below + st[i + 1]
        if i:
            dia = dia - tz[i] * ratio_up[i - 1]
        pivot[i] = 1.0 / dia
        if i < N - 1:
            ratio_up[i] = below * pivot[i]
    a = solve_inner([tz[0]] + [None] * (N - 1))
    b = solve_inner([None] * (N - 1) + [bottom])
    for i in range(N):
        alpha[i] = a[i]
        beta[i] = b[i]
    mred[0] = tz[0] + st[0] - tz[0] * a[0]
    mred[1] = tz[0] * b[0]
    mred[2] = bottom * (1.0 - b[N - 1])

    weight = []
    for first, rows in ((1.0, alpha), (0.0, beta)):
        parts = tiles(jnp.full((CX, NY), first, F32)) + [p for i in range(N) for p in tiles(rows[i])]
        at_perf = pick_dot(rown[...], split2(jnp.concatenate(parts, axis=0)))
        for h in range(2):
            c = own_t[:, h : h + 1].astype(I32)
            weight.append(
                jnp.sum(
                    jnp.where(lanes == rest(c, 128), at_perf[h * 128 : (h + 1) * 128, :], 0.0),
                    axis=1, keepdims=True,
                ) * own_t[:, 4 + h : 5 + h]
            )
    wide = jnp.zeros((128, 128), F32)
    for i in range(4):
        wide = jnp.where(lanes == i, weight[i], wide)
    perf_own[4:8, :] = jnp.transpose(wide)[0:4, :]
    perf_buf[l] = perf_own[...]
    to_layers(lambda p: perf_own, perf_buf.at[l], "pf")
    spread_columns(0, mred, mcol)

    from_layers(f1, "f1")
    f2[t] = add_up(f1, L)
    to_tiles(lambda p: f2.at[t], f2, "f2")
    w = solve_inner([pres[i + 1] for i in range(N)])
    rred[0] = pres[0] + tz[0] * w[0]
    rred[1] = bottom * w[N - 1]
    for h in range(2):
        c = own[h : h + 1, :].astype(I32)
        rto[:, h * 128 : (h + 1) * 128] = onehot(row_iota(RO, 128) == own_row(c))
    from_layers(perf_buf, "pf")
    group_t = jnp.transpose(
        jnp.concatenate([perf_buf[i] for i in range(L)] + [jnp.zeros((128 - 8 * L, 128), F32)], axis=0)
    )
    for e in range(L):
        for h in range(2):
            b = (e * 2 + h) * 128
            c = group_t[:, e * 8 + h : e * 8 + h + 1].astype(I32)
            f = group_t[:, e * 8 + 2 + h : e * 8 + 3 + h].astype(I32)
            rgs[b : b + 128, :] = onehot(lane_iota(128, 8 * L) == sol_row(f))
            csol[b : b + 128, :] = jnp.where(lanes == sol_lane(f), 1.0, 0.0)
            for i in range(2):
                ccell[i, b : b + 128, :] = jnp.where(
                    lanes == rest(c, 128), group_t[:, e * 8 + 4 + 2 * i + h : e * 8 + 5 + 2 * i + h], 0.0
                )
    from_tiles(f2, "f2")
    f3[l] = add_up(f2, T)
    to_layers(lambda p: f3.at[l], f3.at[l], "f3")
    spread_columns(1, rred, rcol)
    send(tz_h.at[LZ - 1], tzp, "tz", (t, ln))
    loads["tx"].wait()
    for z in range(LZ):
        txs[z : z + 1, :] = tx[z, CX - 1 : CX, :]
    for i in range(N):
        for d, x in enumerate((CX - 1, 0)):
            asend[d, i : i + 1, :] = alpha[i, x : x + 1, :]
            asend[d, N + i : N + i + 1, :] = beta[i, x : x + 1, :]
    send(txs, txp, "tx", (tn, l))
    send(asend.at[0], ahalo.at[0], "ah", (tn, l))
    send(asend.at[1], ahalo.at[1], "ah", (tb, l))
    for e in range(L):
        for h in range(2):
            row = column_row(perf_buf[e, h : h + 1, :].astype(I32)) + e * RL
            for i in range(2):
                k = (i * L * 2 + e * 2 + h) * 128
                rtg[:, k : k + 128] = onehot(row_iota(L * RL, 128) == row + i * RL)
    loads["finv"].wait()
    from_layers(f3, "f3")

    acc = jnp.zeros((RPD, 128), F32)
    for r in range(NFR):
        acc = acc + finv[:, r * 128 : (r + 1) * 128] * f3[r // RS, r % RS : r % RS + 1, :]
    rows = lax.dot_general(
        jnp.ones((8, 128), F32), acc, (((1,), (1,)), ((), ())),
        precision=lax.Precision.HIGHEST, preferred_element_type=F32,
    )
    rows = jnp.concatenate([rows] * HALF, axis=1)
    g1[t] = jnp.where(quot(lane_iota(1, 128), RPD) == lax.rem(t, HALF), rows[0:1, :], 0.0)
    to_tiles(lambda p: g1.at[t], g1, "g1")

    columns_here(0, mred, mcol)
    for k in range(L):
        dia = mcol[k, 0] + mcol[k - 1, 2] - mcol[k - 1, 1] * gam[k - 1] if k else mcol[k, 0]
        inv[k] = 1.0 / dia
        gam[k] = mcol[k, 1] * inv[k]
        if k:
            mul[k] = mcol[k - 1, 1] * inv[k]

    from_tiles(g1, "g1")
    pairs = [sum(g1[i + j] for j in range(1, HALF)) + g1[i] for i in range(0, T, HALF)]
    pairs += [jnp.zeros((1, 128), F32)] * (8 - len(pairs))
    g2[l] = jnp.concatenate(pairs, axis=0)
    to_layers(lambda p: g2.at[l], g2.at[l], "g2")
    columns_here(1, rred, rcol)
    from_layers(g2, "g2")

    sol = split2(jnp.concatenate([g2[i] for i in range(L)], axis=0))
    picked = pick_dot(rgs[...], sol)
    for b in range(0, L * 256, 128):
        q = jnp.sum(picked[b : b + 128, :] * csol[b : b + 128, :], axis=1, keepdims=True)
        qs[b : b + 128, 0:1] = q
        for i in range(2):
            q3[i * L * 256 + b : i * L * 256 + b + 128, :] = split2(ccell[i, b : b + 128, :] * q)
    corr[...] = pick_dot(rtg[...], q3[...])
    for k in range(L):
        r = rcol[k, 0] - untile(corr[k * RL : (k + 1) * RL, :], CX, NYL)
        d = (r + rcol[k - 1, 1]) * inv[k] + mul[k] * d if k else r * inv[k]
        ucol[k] = d
    ucol[L] = jnp.zeros((CX, NYL), F32)
    for k in range(L - 2, -1, -1):
        d = ucol[k] + gam[k] * d
        ucol[k] = d
    for e in range(L):
        for i in range(2):
            hsend[0, e, i : i + 1, :] = ucol[e + i, CX - 1 : CX, :]
            hsend[1, e, i : i + 1, :] = ucol[e + i, 0:1, :]
    here = pl.ds(pl.multiple_of(l * NYL, NYL), NYL)
    for i in by_layer:
        e = lax.rem(l + i, L)
        send(hsend.at[0, e], phalo.at[0, :, here], "hl", (tn, e))
        send(hsend.at[1, e], phalo.at[1, :, here], "hl", (tb, e))
    to_layers(lambda p: ucol.at[pl.ds(p, 2)], cols_block(ends, l), "rt")
    pltpu.make_async_copy(ucol.at[pl.ds(l, 2)], cols_block(ends, l), loc.at[2]).start()

    mine = []
    for h in range(2):
        q = qs[pl.ds(pl.multiple_of(l * 256 + h * 128, 128), 128), 0:1] * own_t[:, 4 + h : 5 + h]
        c = own_t[:, h : h + 1].astype(I32)
        mine.append(split2(jnp.where(lanes == rest(c, 128), q, 0.0)))
    own_corr = pick_dot(rto[...], jnp.concatenate(mine, axis=0))
    for z in range(LZ):
        n = CX * NY // 128
        adj[z] = pres[z] - untile(own_corr[z * n : (z + 1) * n, :], CX, NY)
    w = solve_inner([adj[i + 1] for i in range(N)])
    for i in range(N):
        inner[i] = w[i]
        wsend[0, i : i + 1, :] = w[i][CX - 1 : CX, :]
        wsend[1, i : i + 1, :] = w[i][0:1, :]
    send(wsend.at[0], whalo.at[0], "wh", (tn, l))
    send(wsend.at[1], whalo.at[1], "wh", (tb, l))
    for name in ("ty", "bi", "bd"):
        loads[name].wait()
    arrived(tzp, "tz")
    arrived(txp, "tx")
    arrived(ahalo, "ah")
    start = jnp.zeros((8, 128), F32)
    for z in range(LZ):
        before = tz[z - 1] if z else tzp[...] * has_lb
        diag[z] = before + (tz[z] if z < LZ - 1 else tz[z] * has_ln) + st[z]
        for c in range(3):
            b = [bi[c, d, z] for d in range(3)]
            search[c, z] = b[0] * rhs[0, z] + b[1] * rhs[1, z] + b[2] * rhs[2, z]
            slope[c, z] = (1.0 if c == 0 else 0.0) - (
                b[0] * bd[0, 0, z] + b[1] * bd[1, 0, z] + b[2] * bd[2, 0, z]
            )
            start = start + fold(rhs[c, z] * rhs[c, z])
    arrived(whalo, "wh")
    from_layers(rcol, "rt")
    pltpu.make_async_copy(ucol.at[pl.ds(l, 2)], cols_block(ends, l), loc.at[2]).wait()
    arrived(hsend, "hl")

    sub, lane = row_iota(CX, NY), lane_iota(CX, NY)

    def from_xb(w, row):
        return jnp.where(sub == 0, row, pltpu.roll(w, 1, 0))

    def from_xn(v, row):
        return jnp.where(sub == CX - 1, row, pltpu.roll(v, CX - 1, 0))

    def from_yb(w):
        return jnp.where(lane == 0, 0.0, pltpu.roll(w, 1, 1))

    def from_yn(v):
        return jnp.where(lane == NY - 1, 0.0, pltpu.roll(v, NY - 1, 1))

    for z in [LZ - 1, 0] + list(range(1, LZ - 1)):
        p = inner[z - 1] + alpha[z - 1] * ends[0] + beta[z - 1] * ends[1] if z else ends[0]
        edge = [phalo[d, 0:1, :] for d in range(2)]
        if z:
            edge = [
                whalo[d, z - 1 : z, :]
                + ahalo[d, z - 1 : z, :] * phalo[d, 0:1, :]
                + ahalo[d, N + z - 1 : N + z, :] * phalo[d, 1:2, :]
                for d in range(2)
            ]
        near = diag[z] * p - adj[z]
        near = near + tx[z] * from_xn(p, edge[1] * has_tn)
        near = near + from_xb(tx[z] * p, txp[z : z + 1, :] * edge[0] * has_tb)
        near = near + ty[z] * from_yn(p) + from_yb(ty[z] * p)
        for c in range(3):
            v = search[c, z] + slope[c, z] * p + bi[c, 0, z] * near
            search[c, z] = v
            i = c * LZ + z
            xsend[0, i : i + 1, :] = tx[z, CX - 1 : CX, :] * v[CX - 1 : CX, :]
            xsend[1, i : i + 1, :] = v[0:1, :]
            if z == LZ - 1:
                zsend[c] = tz[z] * v
        if z == LZ - 1:
            send(zsend, zhalo.at[0], "zh", (t, ln))
        if z == 0:
            send(search.at[:, 0], zhalo.at[1], "zh", (t, lb))
    send(xsend.at[0], xhalo.at[0], "xh", (tn, l))
    send(xsend.at[1], xhalo.at[1], "xh", (tb, l))
    along = jnp.zeros((8, 128), F32)
    power = jnp.zeros((8, 128), F32)
    none = jnp.zeros((1, NY), F32)
    for z in range(LZ):
        for c in range(3):
            v = search[c, z]
            near = tx[z] * from_xn(v, none) + from_xb(tx[z] * v, none)
            near = near + ty[z] * from_yn(v) + from_yb(ty[z] * v)
            if z < LZ - 1:
                near = near + tz[z] * search[c, z + 1]
            if z:
                near = near + tz[z - 1] * search[c, z - 1]
            im = (
                bd[c, 0, z] * search[0, z] + bd[c, 1, z] * search[1, z] + bd[c, 2, z] * search[2, z]
            ) - near
            image[c, z] = im
            along = along + fold(im * rhs[c, z])
            power = power + fold(im * im)
    along, power = total(along), total(power)
    guess = jnp.where(power > 0.0, along / jnp.where(power > 0.0, power, 1.0), 0.0)

    arrived(xhalo, "xh")
    for z in range(LZ):
        for c in range(3):
            i = c * LZ + z
            image[c, z, 0:1, :] = image[c, z, 0:1, :] - xhalo[0, i : i + 1, :] * has_tb
            image[c, z, CX - 1 : CX, :] = (
                image[c, z, CX - 1 : CX, :] - tx[z, CX - 1 : CX, :] * (xhalo[1, i : i + 1, :] * has_tn)
            )
    along = jnp.zeros((8, 128), F32)
    power = jnp.zeros((8, 128), F32)
    err = jnp.zeros((8, 128), F32)
    for z in list(range(1, LZ - 1)) + [0] + ([LZ - 1] if LZ > 1 else []):
        if z == 0:
            arrived(zhalo, "zh")
        for c in range(3):
            im = image[c, z]
            if z == 0:
                im = im - zhalo[0, c] * has_lb
            if z == LZ - 1:
                im = im - tz[z] * (zhalo[1, c] * has_ln)
            if z in (0, LZ - 1):
                image[c, z] = im
            b = rhs[c, z]
            r = b - guess * im
            along = along + fold(im * b)
            power = power + fold(im * im)
            err = err + fold(r * r)
    along, power, start = total(along), total(power), total(start)
    tilt = along - guess * power
    row = jnp.zeros((8, 128), F32)
    lane8 = lane_iota(8, 128)
    for i, x in enumerate((guess, power, start, total(err), tilt, along)):
        row = jnp.where(lane8 == i, x, row)
    s1[l] = jnp.where(row_iota(8, 128) == l, row, 0.0)
    to_layers(lambda p: s1.at[l], s1.at[l], "s1")
    from_layers(s1, "s1")
    s2[t] = add_up(s1, L)
    to_tiles(lambda p: s2.at[t], s2, "s2")
    gone()
    from_tiles(s2, "s2")
    allrows = jnp.concatenate([s2[i] for i in range(T)], axis=0)
    sums = jnp.sum(allrows, axis=0, keepdims=True)
    omega = sums[:, 5:6] / sums[:, 1:2]
    shift = omega - allrows[:, 0:1]
    left = allrows[:, 3:4] - 2.0 * shift * allrows[:, 4:5] + shift * shift * allrows[:, 1:2]
    left = jnp.maximum(jnp.sum(left, axis=0, keepdims=True), 0.0)
    ratio = jnp.sqrt(left / sums[:, 2:3])
    stat_o[...] = jnp.where(lane8 == 0, omega, ratio)
    gone()


NAMES = (
    "f1", "f2", "f3", "g1", "g2", "pf", "b0", "b1", "tz", "tx", "ah", "wh", "rt", "hl", "xh",
    "zh", "s1", "s2",
)


def scale(stat, search, image, rhs, update_o, lin_res_o, ratio_o, update, lin_res, sems):
    factor = stat[0:1, 0:1]
    ratio_o[...] = stat[0:1, 1:2]
    writes = []
    for c in range(3):
        for i, (out, src) in enumerate(((update_o, update), (lin_res_o, lin_res))):
            for z in range(rhs.shape[1]):
                if i:
                    src[c, z] = rhs[c, z] - factor * image[c, z]
                else:
                    src[c, z] = factor * search[c, z]
            writes.append(pltpu.make_async_copy(src.at[c], out.at[c], sems.at[i, c]))
            writes[-1].start()
    for write in writes:
        write.wait()


def far_first(n, row):
    def hops(i):
        a, b = divmod(i, row)
        return min(a, n // row - a) + min(b, row - b)

    return sorted(range(n), key=hops, reverse=True)


def shards(rhs, wts, bd, bi, tx, ty, tz, st, cell, front, prod, finv):
    T, L = lax.axis_size("tile"), lax.axis_size("layer")
    _, LZ, CX, NY = rhs.shape
    RPD, NF = finv.shape
    NYL = NY // L
    RO, RG = LZ * CX * NY // 128, L * CX * NYL // 128
    K = L * 256
    RS = NF // 128 // L
    N = LZ - 1
    field = (LZ, CX, NY)
    colf = (CX, NYL)
    V = lambda *s: pltpu.VMEM(s, F32)
    H = lambda *s: pltpu.VMEM(s, BF16)
    D = lambda *s: pltpu.SemaphoreType.DMA(s)
    scratch = [
        V(3, *field), V(3, 3, *field), V(3, 3, *field),
        V(*field), V(*field), V(*field), V(*field),
        pltpu.VMEM((2, 128), I32), pltpu.VMEM((2, 128), I32), V(2, 128), V(RPD, NF),
        V(8, 128), V(L, 8, 128), V(*field), V(L, RS, 128), V(L, RS, 128), V(T, RS, 128), V(L, RS, 128),
        V(T, 1, 128), V(L, 8, 128),
        H(256, RO), H(RO, 256), H(RG, 2 * K), H(K, 8 * L), V(K, 128), V(2, K, 128), H(2 * K, 256),
        V(K, 128),
        V(N, CX, NY), V(N, CX, NY), V(N, CX, NY), V(N, CX, NY), V(3, CX, NY), V(2, CX, NY),
        V(L, 3, *colf), V(L, 2, *colf), V(L, *colf), V(L, *colf), V(L, *colf), V(L + 1, *colf),
        V(RG, 128),
        V(CX, NY), V(8, NY), V(8, NY), V(2, 2 * N, NY), V(2, 2 * N, NY), V(2, N, NY), V(2, N, NY),
        V(2, CX, NY), V(2, L, 2, NYL), V(2, 2, NY), V(*field), V(N, CX, NY),
        V(3, *field), V(*field), V(2, 16, NY), V(2, 16, NY), V(3, CX, NY), V(2, 3, CX, NY),
        V(L, 8, 128), V(T, 8, 128),
        D(12), D(len(NAMES)), D(len(NAMES)), D(3),
    ]
    anywhere = pl.BlockSpec(memory_space=pl.ANY)
    search, image, kept, stat = pl.pallas_call(
        functools.partial(kernel, T, L, LZ, CX, NY, NF),
        out_shape=(
            pltpu.VMEM(rhs.shape, F32),
            pltpu.VMEM(rhs.shape, F32),
            pltpu.VMEM(rhs.shape, F32),
            pltpu.VMEM((8, 128), F32),
        ),
        in_specs=[anywhere] * 12,
        out_specs=(pl.BlockSpec(memory_space=pltpu.VMEM),) * 4,
        scratch_shapes=scratch,
        compiler_params=pltpu.CompilerParams(
            collective_id=0, has_side_effects=True, vmem_limit_bytes=int(56 * 1024 * 1024)
        ),
    )(
        rhs, wts, bd, bi, tx, ty, tz, st,
        cell.reshape(2, 128), front.reshape(2, 128), prod.reshape(2, 128), finv,
    )
    here = pl.BlockSpec(memory_space=pltpu.VMEM)
    update, lin_res, ratio = pl.pallas_call(
        scale,
        out_shape=(jax.ShapeDtypeStruct(rhs.shape, F32),) * 2 + (jax.ShapeDtypeStruct((1, 1), F32),),
        in_specs=[here] * 4,
        out_specs=(anywhere, anywhere, here),
        scratch_shapes=[V(3, *field), V(3, *field), D(2, 3)],
        compiler_params=pltpu.CompilerParams(vmem_limit_bytes=4 * 1024 * 1024),
    )(stat, search, image, kept)
    return update, lin_res, ratio[0, 0]


def solution(mesh):
    return jax.shard_map(
        shards,
        mesh=mesh,
        in_specs=(
            P(None, "layer", "tile", None),
            P(None, "layer", "tile", None),
            P(None, None, "layer", "tile", None),
            P(None, None, "layer", "tile", None),
            P("layer", "tile", None),
            P("layer", "tile", None),
            P("layer", "tile", None),
            P("layer", "tile", None),
            P(("tile", "layer")),
            P(("tile", "layer")),
            P(("tile", "layer")),
            P(("tile", "layer"), None),
        ),
        out_specs=(P(None, "layer", "tile", None), P(None, "layer", "tile", None), P()),
        check_vma=False,
    )
```

```python
import functools

import jax
import jax.numpy as jnp
from jax import lax
from jax.experimental import pallas as pl
from jax.experimental.pallas import tpu as pltpu
from jax.sharding import PartitionSpec as P

MESH = pl.DeviceIdType.MESH
F32 = jnp.float32
BF16 = jnp.bfloat16
I32 = jnp.int32


def bits(n):
    assert n & (n - 1) == 0
    return n.bit_length() - 1


def quot(a, n):
    return lax.shift_right_logical(a, jnp.full_like(a, bits(n)))


def rest(a, n):
    return a & (n - 1)


def split2(x):
    hi = x.astype(BF16)
    return jnp.concatenate([hi, (x - hi.astype(F32)).astype(BF16)], axis=1)


def pick_dot(onehot, pieces):
    out = lax.dot_general(onehot, pieces, (((1,), (0,)), ((), ())), preferred_element_type=F32)
    n = out.shape[1] // 2
    return out[:, :n] + out[:, n:]


def tiles(block):
    rows, cols = block.shape
    return [
        block[i : i + 8, j : j + 128] for i in range(0, rows, 8) for j in range(0, cols, 128)
    ]


def untile(mat, rows, cols):
    per = cols // 128
    out = []
    for i in range(rows // 8):
        out.append(
            jnp.concatenate(
                [mat[(i * per + j) * 8 : (i * per + j + 1) * 8, :] for j in range(per)], axis=1
            )
        )
    return jnp.concatenate(out, axis=0)


def fold(block):
    parts = tiles(block)
    while len(parts) > 1:
        parts = [a + b for a, b in zip(parts[::2], parts[1::2])]
    return parts[0]


def total(x):
    return jnp.sum(jnp.sum(x, axis=1, keepdims=True), axis=0, keepdims=True)


def onehot(mask):
    return jnp.where(mask, 1.0, 0.0).astype(BF16)


def kernel(
    T, L, LZ, CX, NY, NF,
    rhs_h, wts_h, bd_h, bi_h, tx_h, ty_h, tz_h, st_h, cell_h, front_h, prod_h, finv_h,
    search, image, rhs, stat_o,
    wts, bd, bi, tx, ty, tz, st, cell, front, prod, finv,
    perf_own, perf_buf, pres, fpart, f1, f2, f3, g1, g2,
    rown, rto, rtg, rgs, csol, ccell, q3, qs,
    alpha, beta, pivot, ratio_up, mred, rred, mcol, rcol, inv, mul, gam, ucol, corr,
    tzp, txs, txp, asend, ahalo, wsend, whalo, ends, hsend, phalo, adj, inner,
    slope, diag, xsend, xhalo, zsend, zhalo, s1, s2,
    ld, snd, rcv, loc,
):
    NYL, NFR = NY // L, NF // 128
    NBL, RS, RPD = NYL // 128, NFR // L, NF // (T * L)
    N = LZ - 1
    HALF = 128 // RPD
    RL = CX * NYL // 128
    RO = LZ * CX * NY // 128
    NB = NY // 128
    t, l = lax.axis_index("tile"), lax.axis_index("layer")

    loads = {}
    order = [
        ("cell", cell_h, cell), ("front", front_h, front), ("prod", prod_h, prod),
        ("rhs", rhs_h, rhs), ("wts", wts_h, wts), ("tz", tz_h, tz), ("st", st_h, st),
        ("finv", finv_h, finv), ("tx", tx_h, tx), ("ty", ty_h, ty), ("bi", bi_h, bi), ("bd", bd_h, bd),
    ]
    for i, (name, src, dst) in enumerate(order):
        loads[name] = pltpu.make_async_copy(src, dst, ld.at[i])
        if i < 5:
            loads[name].start()

    tn, tb = lax.rem(t + 1, T), lax.rem(t + T - 1, T)
    ln, lb = lax.rem(l + 1, L), lax.rem(l + L - 1, L)
    barrier = pltpu.get_barrier_semaphore()
    peers = [(lax.rem(t + i, T), l) for i in range(1, T)]
    peers += [(t, lax.rem(l + i, L)) for i in range(1, L)]
    peers += [(a, lax.rem(l + i, L)) for a in (tn, tb) for i in range(1, L)]
    for peer in peers:
        pl.semaphore_signal(barrier, inc=1, device_id=peer, device_id_type=MESH)

    sent = {}
    by_layer, by_tile = far_first(L, L), far_first(T, min(T, 4))

    def link(name, to):
        return dict(
            send_sem=snd.at[NAMES.index(name)], recv_sem=rcv.at[NAMES.index(name)],
            device_id=to, device_id_type=MESH,
        )

    def send(src, dst, name, to):
        pltpu.make_async_remote_copy(src_ref=src, dst_ref=dst, **link(name, to)).start()

    def arrived(every, name):
        sent[name] = pltpu.make_async_remote_copy(
            src_ref=every, dst_ref=every, **link(name, (t, l))
        )
        sent[name].wait_recv()

    def gone():
        for name in list(sent):
            sent.pop(name).wait_send()

    def to_tiles(src, dst, name):
        for i in by_tile[:-1]:
            peer = lax.rem(t + i, T)
            send(src(peer), dst.at[t], name, (peer, l))

    def to_layers(src, dst, name):
        for i in by_layer[:-1]:
            peer = lax.rem(l + i, L)
            send(src(peer), dst, name, (t, peer))

    def from_tiles(buf, name):
        arrived(buf.at[pl.ds(0, T - 1)], name)

    def from_layers(buf, name):
        arrived(buf.at[pl.ds(0, L - 1)], name)

    def add_up(buf, n):
        parts = [buf[i] for i in range(n)]
        while len(parts) > 1:
            parts = [a + b for a, b in zip(parts[::2], parts[1::2])]
        return parts[0]

    def cols_block(ref, i):
        return ref.at[:, :, pl.ds(pl.multiple_of(i * NYL, NYL), NYL)]

    def lane_iota(rows, cols):
        return lax.broadcasted_iota(I32, (rows, cols), 1)

    def row_iota(rows, cols):
        return lax.broadcasted_iota(I32, (rows, cols), 0)

    def own_row(c):
        z, x, y = quot(c, CX * NY), rest(quot(c, NY), CX), rest(c, NY)
        return ((z * (CX // 8) + quot(x, 8)) * NB + quot(y, 128)) * 8 + rest(x, 8)

    def column_row(c):
        x, y = rest(quot(c, NY), CX), rest(c, NY)
        row = (quot(x, 8) * NBL + quot(rest(y, NYL), 128)) * 8 + rest(x, 8)
        return jnp.where(quot(y, NYL) == l, row, -(L + 1) * RL)

    def sol_row(f):
        d = quot(f, RPD)
        return rest(d, L) * 8 + quot(quot(d, L), HALF)

    def sol_lane(f):
        return rest(quot(quot(f, RPD), L), HALF) * RPD + rest(f, RPD)

    for name in ("cell", "front", "prod"):
        loads[name].wait()
    perf_own[...] = jnp.zeros((8, 128), F32)
    perf_own[0:2, :] = cell[...].astype(F32)
    perf_own[2:4, :] = front[...].astype(F32)
    perf_own[4:6, :] = prod[...]
    own = perf_own[...]
    own_t = jnp.transpose(jnp.concatenate([own, jnp.zeros((120, 128), F32)], axis=0))
    for h in range(2):
        c = own_t[:, h : h + 1].astype(I32)
        rown[h * 128 : (h + 1) * 128, :] = onehot(lane_iota(128, RO) == own_row(c))

    loads["rhs"].wait()
    loads["wts"].wait()
    for name, _, _ in order[5:]:
        loads[name].start()
    for z in range(LZ):
        pres[z] = wts[0, z] * rhs[0, z] + wts[1, z] * rhs[1, z] + wts[2, z] * rhs[2, z]
    pieces = split2(jnp.concatenate([p for z in range(LZ) for p in tiles(pres[z])], axis=0))
    at_perf = pick_dot(rown[...], pieces)
    lanes = lane_iota(128, 128)
    spread, where_to = [], []
    for h in range(2):
        c = own_t[:, h : h + 1].astype(I32)
        f = own_t[:, 2 + h : 3 + h].astype(I32)
        value = jnp.sum(
            jnp.where(lanes == rest(c, 128), at_perf[h * 128 : (h + 1) * 128, :], 0.0),
            axis=1, keepdims=True,
        ) * own_t[:, 4 + h : 5 + h]
        spread.append(split2(jnp.where(lanes == rest(f, 128), value, 0.0)))
        where_to.append(onehot(row_iota(NFR, 128) == quot(own[2 + h : 3 + h, :].astype(I32), 128)))
    part = pick_dot(jnp.concatenate(where_to, axis=1), jnp.concatenate(spread, axis=0))
    for i in range(L):
        fpart[i] = part[i * RS : (i + 1) * RS, :]
    f1[l] = fpart[l]

    pl.semaphore_wait(barrier, len(peers))
    to_layers(lambda p: fpart.at[p], f1.at[l], "f1")

    def spread_columns(i, src, dst):
        to_layers(lambda p: cols_block(src, p), dst.at[l], f"b{i}")
        pltpu.make_async_copy(cols_block(src, l), dst.at[l], loc.at[i]).start()

    def columns_here(i, src, dst):
        from_layers(dst, f"b{i}")
        pltpu.make_async_copy(cols_block(src, l), dst.at[l], loc.at[i]).wait()

    has_tb, has_tn = jnp.where(t > 0, 1.0, 0.0), jnp.where(t < T - 1, 1.0, 0.0)
    has_lb, has_ln = jnp.where(l > 0, 1.0, 0.0), jnp.where(l < L - 1, 1.0, 0.0)

    def solve_inner(right):
        d = []
        for i in range(N):
            r = right[i]
            if i and d[-1] is not None:
                link = tz[i] * d[-1]
                r = link if r is None else r + link
            d.append(None if r is None else r * pivot[i])
        for i in range(N - 2, -1, -1):
            back = ratio_up[i] * d[i + 1]
            d[i] = back if d[i] is None else d[i] + back
        return d

    loads["tz"].wait()
    loads["st"].wait()
    bottom = tz[LZ - 1] * has_ln
    for i in range(N):
        below = tz[i + 1] if i < N - 1 else bottom
        dia = tz[i] + below + st[i + 1]
        if i:
            dia = dia - tz[i] * ratio_up[i - 1]
        pivot[i] = 1.0 / dia
        if i < N - 1:
            ratio_up[i] = below * pivot[i]
    a = solve_inner([tz[0]] + [None] * (N - 1))
    b = solve_inner([None] * (N - 1) + [bottom])
    for i in range(N):
        alpha[i] = a[i]
        beta[i] = b[i]
    mred[0] = tz[0] + st[0] - tz[0] * a[0]
    mred[1] = tz[0] * b[0]
    mred[2] = bottom * (1.0 - b[N - 1])

    weight = []
    for first, rows in ((1.0, alpha), (0.0, beta)):
        parts = tiles(jnp.full((CX, NY), first, F32)) + [p for i in range(N) for p in tiles(rows[i])]
        at_perf = pick_dot(rown[...], split2(jnp.concatenate(parts, axis=0)))
        for h in range(2):
            c = own_t[:, h : h + 1].astype(I32)
            weight.append(
                jnp.sum(
                    jnp.where(lanes == rest(c, 128), at_perf[h * 128 : (h + 1) * 128, :], 0.0),
                    axis=1, keepdims=True,
                ) * own_t[:, 4 + h : 5 + h]
            )
    wide = jnp.zeros((128, 128), F32)
    for i in range(4):
        wide = jnp.where(lanes == i, weight[i], wide)
    perf_own[4:8, :] = jnp.transpose(wide)[0:4, :]
    perf_buf[l] = perf_own[...]
    to_layers(lambda p: perf_own, perf_buf.at[l], "pf")
    spread_columns(0, mred, mcol)

    from_layers(f1, "f1")
    f2[t] = add_up(f1, L)
    to_tiles(lambda p: f2.at[t], f2, "f2")
    w = solve_inner([pres[i + 1] for i in range(N)])
    rred[0] = pres[0] + tz[0] * w[0]
    rred[1] = bottom * w[N - 1]
    for h in range(2):
        c = own[h : h + 1, :].astype(I32)
        rto[:, h * 128 : (h + 1) * 128] = onehot(row_iota(RO, 128) == own_row(c))
    from_layers(perf_buf, "pf")
    group_t = jnp.transpose(
        jnp.concatenate([perf_buf[i] for i in range(L)] + [jnp.zeros((128 - 8 * L, 128), F32)], axis=0)
    )
    for e in range(L):
        for h in range(2):
            b = (e * 2 + h) * 128
            c = group_t[:, e * 8 + h : e * 8 + h + 1].astype(I32)
            f = group_t[:, e * 8 + 2 + h : e * 8 + 3 + h].astype(I32)
            rgs[b : b + 128, :] = onehot(lane_iota(128, 8 * L) == sol_row(f))
            csol[b : b + 128, :] = jnp.where(lanes == sol_lane(f), 1.0, 0.0)
            for i in range(2):
                ccell[i, b : b + 128, :] = jnp.where(
                    lanes == rest(c, 128), group_t[:, e * 8 + 4 + 2 * i + h : e * 8 + 5 + 2 * i + h], 0.0
                )
    from_tiles(f2, "f2")
    f3[l] = add_up(f2, T)
    to_layers(lambda p: f3.at[l], f3.at[l], "f3")
    spread_columns(1, rred, rcol)
    send(tz_h.at[LZ - 1], tzp, "tz", (t, ln))
    loads["tx"].wait()
    for z in range(LZ):
        txs[z : z + 1, :] = tx[z, CX - 1 : CX, :]
    for i in range(N):
        for d, x in enumerate((CX - 1, 0)):
            asend[d, i : i + 1, :] = alpha[i, x : x + 1, :]
            asend[d, N + i : N + i + 1, :] = beta[i, x : x + 1, :]
    send(txs, txp, "tx", (tn, l))
    send(asend.at[0], ahalo.at[0], "ah", (tn, l))
    send(asend.at[1], ahalo.at[1], "ah", (tb, l))
    for e in range(L):
        for h in range(2):
            row = column_row(perf_buf[e, h : h + 1, :].astype(I32)) + e * RL
            for i in range(2):
                k = (i * L * 2 + e * 2 + h) * 128
                rtg[:, k : k + 128] = onehot(row_iota(L * RL, 128) == row + i * RL)
    loads["finv"].wait()
    from_layers(f3, "f3")

    acc = jnp.zeros((RPD, 128), F32)
    for r in range(NFR):
        acc = acc + finv[:, r * 128 : (r + 1) * 128] * f3[r // RS, r % RS : r % RS + 1, :]
    rows = lax.dot_general(
        jnp.ones((8, 128), F32), acc, (((1,), (1,)), ((), ())),
        precision=lax.Precision.HIGHEST, preferred_element_type=F32,
    )
    rows = jnp.concatenate([rows] * HALF, axis=1)
    g1[t] = jnp.where(quot(lane_iota(1, 128), RPD) == lax.rem(t, HALF), rows[0:1, :], 0.0)
    to_tiles(lambda p: g1.at[t], g1, "g1")

    columns_here(0, mred, mcol)
    for k in range(L):
        dia = mcol[k, 0] + mcol[k - 1, 2] - mcol[k - 1, 1] * gam[k - 1] if k else mcol[k, 0]
        inv[k] = 1.0 / dia
        gam[k] = mcol[k, 1] * inv[k]
        if k:
            mul[k] = mcol[k - 1, 1] * inv[k]

    from_tiles(g1, "g1")
    pairs = [sum(g1[i + j] for j in range(1, HALF)) + g1[i] for i in range(0, T, HALF)]
    pairs += [jnp.zeros((1, 128), F32)] * (8 - len(pairs))
    g2[l] = jnp.concatenate(pairs, axis=0)
    to_layers(lambda p: g2.at[l], g2.at[l], "g2")
    columns_here(1, rred, rcol)
    from_layers(g2, "g2")

    sol = split2(jnp.concatenate([g2[i] for i in range(L)], axis=0))
    picked = pick_dot(rgs[...], sol)
    for b in range(0, L * 256, 128):
        q = jnp.sum(picked[b : b + 128, :] * csol[b : b + 128, :], axis=1, keepdims=True)
        qs[b : b + 128, 0:1] = q
        for i in range(2):
            q3[i * L * 256 + b : i * L * 256 + b + 128, :] = split2(ccell[i, b : b + 128, :] * q)
    corr[...] = pick_dot(rtg[...], q3[...])
    for k in range(L):
        r = rcol[k, 0] - untile(corr[k * RL : (k + 1) * RL, :], CX, NYL)
        d = (r + rcol[k - 1, 1]) * inv[k] + mul[k] * d if k else r * inv[k]
        ucol[k] = d
    ucol[L] = jnp.zeros((CX, NYL), F32)
    for k in range(L - 2, -1, -1):
        d = ucol[k] + gam[k] * d
        ucol[k] = d
    for e in range(L):
        for i in range(2):
            hsend[0, e, i : i + 1, :] = ucol[e + i, CX - 1 : CX, :]
            hsend[1, e, i : i + 1, :] = ucol[e + i, 0:1, :]
    here = pl.ds(pl.multiple_of(l * NYL, NYL), NYL)
    for i in by_layer:
        e = lax.rem(l + i, L)
        send(hsend.at[0, e], phalo.at[0, :, here], "hl", (tn, e))
        send(hsend.at[1, e], phalo.at[1, :, here], "hl", (tb, e))
    to_layers(lambda p: ucol.at[pl.ds(p, 2)], cols_block(ends, l), "rt")
    pltpu.make_async_copy(ucol.at[pl.ds(l, 2)], cols_block(ends, l), loc.at[2]).start()

    mine = []
    for h in range(2):
        q = qs[pl.ds(pl.multiple_of(l * 256 + h * 128, 128), 128), 0:1] * own_t[:, 4 + h : 5 + h]
        c = own_t[:, h : h + 1].astype(I32)
        mine.append(split2(jnp.where(lanes == rest(c, 128), q, 0.0)))
    own_corr = pick_dot(rto[...], jnp.concatenate(mine, axis=0))
    for z in range(LZ):
        n = CX * NY // 128
        adj[z] = pres[z] - untile(own_corr[z * n : (z + 1) * n, :], CX, NY)
    w = solve_inner([adj[i + 1] for i in range(N)])
    for i in range(N):
        inner[i] = w[i]
        wsend[0, i : i + 1, :] = w[i][CX - 1 : CX, :]
        wsend[1, i : i + 1, :] = w[i][0:1, :]
    send(wsend.at[0], whalo.at[0], "wh", (tn, l))
    send(wsend.at[1], whalo.at[1], "wh", (tb, l))
    for name in ("ty", "bi", "bd"):
        loads[name].wait()
    arrived(tzp, "tz")
    arrived(txp, "tx")
    arrived(ahalo, "ah")
    start = jnp.zeros((8, 128), F32)
    for z in range(LZ):
        before = tz[z - 1] if z else tzp[...] * has_lb
        diag[z] = before + (tz[z] if z < LZ - 1 else tz[z] * has_ln) + st[z]
        for c in range(3):
            b = [bi[c, d, z] for d in range(3)]
            search[c, z] = b[0] * rhs[0, z] + b[1] * rhs[1, z] + b[2] * rhs[2, z]
            slope[c, z] = (1.0 if c == 0 else 0.0) - (
                b[0] * bd[0, 0, z] + b[1] * bd[1, 0, z] + b[2] * bd[2, 0, z]
            )
            start = start + fold(rhs[c, z] * rhs[c, z])
    arrived(whalo, "wh")
    from_layers(rcol, "rt")
    pltpu.make_async_copy(ucol.at[pl.ds(l, 2)], cols_block(ends, l), loc.at[2]).wait()
    arrived(hsend, "hl")

    sub, lane = row_iota(CX, NY), lane_iota(CX, NY)

    def from_xb(w, row):
        return jnp.where(sub == 0, row, pltpu.roll(w, 1, 0))

    def from_xn(v, row):
        return jnp.where(sub == CX - 1, row, pltpu.roll(v, CX - 1, 0))

    def from_yb(w):
        return jnp.where(lane == 0, 0.0, pltpu.roll(w, 1, 1))

    def from_yn(v):
        return jnp.where(lane == NY - 1, 0.0, pltpu.roll(v, NY - 1, 1))

    def slab(z):
        p = inner[z - 1] + alpha[z - 1] * ends[0] + beta[z - 1] * ends[1] if z else ends[0]
        edge = [phalo[d, 0:1, :] for d in range(2)]
        if z:
            edge = [
                whalo[d, z - 1 : z, :]
                + ahalo[d, z - 1 : z, :] * phalo[d, 0:1, :]
                + ahalo[d, N + z - 1 : N + z, :] * phalo[d, 1:2, :]
                for d in range(2)
            ]
        near = diag[z] * p - adj[z]
        near = near + tx[z] * from_xn(p, edge[1] * has_tn)
        near = near + from_xb(tx[z] * p, txp[z : z + 1, :] * edge[0] * has_tb)
        near = near + ty[z] * from_yn(p) + from_yb(ty[z] * p)
        for c in range(3):
            v = search[c, z] + slope[c, z] * p + bi[c, 0, z] * near
            search[c, z] = v
            i = c * LZ + z
            xsend[0, i : i + 1, :] = tx[z, CX - 1 : CX, :] * v[CX - 1 : CX, :]
            xsend[1, i : i + 1, :] = v[0:1, :]
            if z == LZ - 1:
                zsend[c] = tz[z] * v
                send(zsend.at[c], zhalo.at[0, c], "zh", (t, ln))
            if z == 0:
                send(search.at[c, 0], zhalo.at[1, c], "zh", (t, lb))

    @pl.when(lax.rem(l, 2) == 1)
    def _():
        slab(LZ - 1)
        slab(0)

    @pl.when(lax.rem(l, 2) == 0)
    def _():
        slab(0)
        slab(LZ - 1)

    for z in range(1, LZ - 1):
        slab(z)
    send(xsend.at[0], xhalo.at[0], "xh", (tn, l))
    send(xsend.at[1], xhalo.at[1], "xh", (tb, l))
    along = jnp.zeros((8, 128), F32)
    power = jnp.zeros((8, 128), F32)
    none = jnp.zeros((1, NY), F32)
    for z in range(LZ):
        for c in range(3):
            v = search[c, z]
            near = tx[z] * from_xn(v, none) + from_xb(tx[z] * v, none)
            near = near + ty[z] * from_yn(v) + from_yb(ty[z] * v)
            if z < LZ - 1:
                near = near + tz[z] * search[c, z + 1]
            if z:
                near = near + tz[z - 1] * search[c, z - 1]
            im = (
                bd[c, 0, z] * search[0, z] + bd[c, 1, z] * search[1, z] + bd[c, 2, z] * search[2, z]
            ) - near
            image[c, z] = im
            along = along + fold(im * rhs[c, z])
            power = power + fold(im * im)
    along, power = total(along), total(power)
    guess = jnp.where(power > 0.0, along / jnp.where(power > 0.0, power, 1.0), 0.0)

    arrived(xhalo, "xh")
    for z in range(LZ):
        for c in range(3):
            i = c * LZ + z
            image[c, z, 0:1, :] = image[c, z, 0:1, :] - xhalo[0, i : i + 1, :] * has_tb
            image[c, z, CX - 1 : CX, :] = (
                image[c, z, CX - 1 : CX, :] - tx[z, CX - 1 : CX, :] * (xhalo[1, i : i + 1, :] * has_tn)
            )
    along = jnp.zeros((8, 128), F32)
    power = jnp.zeros((8, 128), F32)
    err = jnp.zeros((8, 128), F32)
    for z in list(range(1, LZ - 1)) + [0] + ([LZ - 1] if LZ > 1 else []):
        if z == 0:
            arrived(zhalo, "zh")
        for c in range(3):
            im = image[c, z]
            if z == 0:
                im = im - zhalo[0, c] * has_lb
            if z == LZ - 1:
                im = im - tz[z] * (zhalo[1, c] * has_ln)
            if z in (0, LZ - 1):
                image[c, z] = im
            b = rhs[c, z]
            r = b - guess * im
            along = along + fold(im * b)
            power = power + fold(im * im)
            err = err + fold(r * r)
    along, power, start = total(along), total(power), total(start)
    tilt = along - guess * power
    row = jnp.zeros((8, 128), F32)
    lane8 = lane_iota(8, 128)
    for i, x in enumerate((guess, power, start, total(err), tilt, along)):
        row = jnp.where(lane8 == i, x, row)
    s1[l] = jnp.where(row_iota(8, 128) == l, row, 0.0)
    to_layers(lambda p: s1.at[l], s1.at[l], "s1")
    from_layers(s1, "s1")
    s2[t] = add_up(s1, L)
    to_tiles(lambda p: s2.at[t], s2, "s2")
    gone()
    from_tiles(s2, "s2")
    allrows = jnp.concatenate([s2[i] for i in range(T)], axis=0)
    sums = jnp.sum(allrows, axis=0, keepdims=True)
    omega = sums[:, 5:6] / sums[:, 1:2]
    shift = omega - allrows[:, 0:1]
    left = allrows[:, 3:4] - 2.0 * shift * allrows[:, 4:5] + shift * shift * allrows[:, 1:2]
    left = jnp.maximum(jnp.sum(left, axis=0, keepdims=True), 0.0)
    ratio = jnp.sqrt(left / sums[:, 2:3])
    stat_o[...] = jnp.where(lane8 == 0, omega, ratio)
    gone()


NAMES = (
    "f1", "f2", "f3", "g1", "g2", "pf", "b0", "b1", "tz", "tx", "ah", "wh", "rt", "hl", "xh",
    "zh", "s1", "s2",
)


def scale(stat, search, image, rhs, update_o, lin_res_o, ratio_o, update, lin_res, sems):
    factor = stat[0:1, 0:1]
    ratio_o[...] = stat[0:1, 1:2]
    writes = []
    for c in range(3):
        for i, (out, src) in enumerate(((update_o, update), (lin_res_o, lin_res))):
            for z in range(rhs.shape[1]):
                if i:
                    src[c, z] = rhs[c, z] - factor * image[c, z]
                else:
                    src[c, z] = factor * search[c, z]
            writes.append(pltpu.make_async_copy(src.at[c], out.at[c], sems.at[i, c]))
            writes[-1].start()
    for write in writes:
        write.wait()


def far_first(n, row):
    def hops(i):
        a, b = divmod(i, row)
        return min(a, n // row - a) + min(b, row - b)

    return sorted(range(n), key=hops, reverse=True)


def shards(rhs, wts, bd, bi, tx, ty, tz, st, cell, front, prod, finv):
    T, L = lax.axis_size("tile"), lax.axis_size("layer")
    _, LZ, CX, NY = rhs.shape
    RPD, NF = finv.shape
    NYL = NY // L
    RO, RG = LZ * CX * NY // 128, L * CX * NYL // 128
    K = L * 256
    RS = NF // 128 // L
    N = LZ - 1
    field = (LZ, CX, NY)
    colf = (CX, NYL)
    V = lambda *s: pltpu.VMEM(s, F32)
    H = lambda *s: pltpu.VMEM(s, BF16)
    D = lambda *s: pltpu.SemaphoreType.DMA(s)
    scratch = [
        V(3, *field), V(3, 3, *field), V(3, 3, *field),
        V(*field), V(*field), V(*field), V(*field),
        pltpu.VMEM((2, 128), I32), pltpu.VMEM((2, 128), I32), V(2, 128), V(RPD, NF),
        V(8, 128), V(L, 8, 128), V(*field), V(L, RS, 128), V(L, RS, 128), V(T, RS, 128), V(L, RS, 128),
        V(T, 1, 128), V(L, 8, 128),
        H(256, RO), H(RO, 256), H(RG, 2 * K), H(K, 8 * L), V(K, 128), V(2, K, 128), H(2 * K, 256),
        V(K, 128),
        V(N, CX, NY), V(N, CX, NY), V(N, CX, NY), V(N, CX, NY), V(3, CX, NY), V(2, CX, NY),
        V(L, 3, *colf), V(L, 2, *colf), V(L, *colf), V(L, *colf), V(L, *colf), V(L + 1, *colf),
        V(RG, 128),
        V(CX, NY), V(8, NY), V(8, NY), V(2, 2 * N, NY), V(2, 2 * N, NY), V(2, N, NY), V(2, N, NY),
        V(2, CX, NY), V(2, L, 2, NYL), V(2, 2, NY), V(*field), V(N, CX, NY),
        V(3, *field), V(*field), V(2, 16, NY), V(2, 16, NY), V(3, CX, NY), V(2, 3, CX, NY),
        V(L, 8, 128), V(T, 8, 128),
        D(12), D(len(NAMES)), D(len(NAMES)), D(3),
    ]
    anywhere = pl.BlockSpec(memory_space=pl.ANY)
    search, image, kept, stat = pl.pallas_call(
        functools.partial(kernel, T, L, LZ, CX, NY, NF),
        out_shape=(
            pltpu.VMEM(rhs.shape, F32),
            pltpu.VMEM(rhs.shape, F32),
            pltpu.VMEM(rhs.shape, F32),
            pltpu.VMEM((8, 128), F32),
        ),
        in_specs=[anywhere] * 12,
        out_specs=(pl.BlockSpec(memory_space=pltpu.VMEM),) * 4,
        scratch_shapes=scratch,
        compiler_params=pltpu.CompilerParams(
            collective_id=0, has_side_effects=True, vmem_limit_bytes=int(56 * 1024 * 1024)
        ),
    )(
        rhs, wts, bd, bi, tx, ty, tz, st,
        cell.reshape(2, 128), front.reshape(2, 128), prod.reshape(2, 128), finv,
    )
    here = pl.BlockSpec(memory_space=pltpu.VMEM)
    update, lin_res, ratio = pl.pallas_call(
        scale,
        out_shape=(jax.ShapeDtypeStruct(rhs.shape, F32),) * 2 + (jax.ShapeDtypeStruct((1, 1), F32),),
        in_specs=[here] * 4,
        out_specs=(anywhere, anywhere, here),
        scratch_shapes=[V(3, *field), V(3, *field), D(2, 3)],
        compiler_params=pltpu.CompilerParams(vmem_limit_bytes=4 * 1024 * 1024),
    )(stat, search, image, kept)
    return update, lin_res, ratio[0, 0]


def solution(mesh):
    return jax.shard_map(
        shards,
        mesh=mesh,
        in_specs=(
            P(None, "layer", "tile", None),
            P(None, "layer", "tile", None),
            P(None, None, "layer", "tile", None),
            P(None, None, "layer", "tile", None),
            P("layer", "tile", None),
            P("layer", "tile", None),
            P("layer", "tile", None),
            P("layer", "tile", None),
            P(("tile", "layer")),
            P(("tile", "layer")),
            P(("tile", "layer")),
            P(("tile", "layer"), None),
        ),
        out_specs=(P(None, "layer", "tile", None), P(None, "layer", "tile", None), P()),
        check_vma=False,
    )
```
